32 devices in a mesh: dp: 4 (over y, x), fsdp: 8 (over z, core).
Axes of the slice: x: 2, y: 2, z: 4, core: 2. Of those that a mesh axis runs over, the one named last changes fastest.
Arguments:
- tokens: bfloat16 [4096, 768], P(('dp', 'fsdp')), may hold values from -6 to 6
- cotangent: bfloat16 [4096, 768], P(('dp', 'fsdp')), may hold values from -6 to 6
- segments: int32 [32, 128], P(('dp', 'fsdp')), may hold values from 0 to 7, never falling along the last dimension, each value on 1 to 64 neighbouring positions
- w_qkv: float32 [768, 2304], P(('dp', 'fsdp')), may hold values from -0.21875 to 0.21875
- w_out: float32 [768, 768], P(('dp', 'fsdp')), may hold values from -0.4375 to 0.4375
- w_up: float32 [768, 3072], P(('dp', 'fsdp')), may hold values from -0.21875 to 0.21875
- w_down: float32 [3072, 768], P(('dp', 'fsdp')), may hold values from -0.109375 to 0.109375
- vectors: float32 [9984], P(('dp', 'fsdp')), may hold values from -0.9 to 1.5
- first_qkv: float32 [768, 2304], P(('dp', 'fsdp')), may hold values from -1 to 1
- first_out: float32 [768, 768], P(('dp', 'fsdp')), may hold values from -1 to 1
- first_up: float32 [768, 3072], P(('dp', 'fsdp')), may hold values from -1 to 1
- first_down: float32 [3072, 768], P(('dp', 'fsdp')), may hold values from -1 to 1
- first_vec: float32 [9984], P(('dp', 'fsdp')), may hold values from -1 to 1
- second_qkv: float32 [768, 2304], P(('dp', 'fsdp')), may hold values from 0.02 to 0.2
- second_out: float32 [768, 768], P(('dp', 'fsdp')), may hold values from 0.02 to 0.2
- second_up: float32 [768, 3072], P(('dp', 'fsdp')), may hold values from 0.02 to 0.2
- second_down: float32 [3072, 768], P(('dp', 'fsdp')), may hold values from 0.02 to 0.2
- second_vec: float32 [9984], P(('dp', 'fsdp')), may hold values from 0.02 to 0.2
Outputs:
- output: bfloat16 [4096, 768], P(('dp', 'fsdp'))
- grad_tokens: bfloat16 [4096, 768], P(('dp', 'fsdp'))
- grad_w_qkv: float32 [768, 2304], P(('dp', 'fsdp'))
- grad_w_out: float32 [768, 768], P(('dp', 'fsdp'))
- grad_w_up: float32 [768, 3072], P(('dp', 'fsdp'))
- grad_w_down: float32 [3072, 768], P(('dp', 'fsdp'))
- grad_vectors: float32 [9984], P(('dp', 'fsdp'))
- new_w_qkv: float32 [768, 2304], P(('dp', 'fsdp'))
- new_w_out: float32 [768, 768], P(('dp', 'fsdp'))
- new_w_up: float32 [768, 3072], P(('dp', 'fsdp'))
- new_w_down: float32 [3072, 768], P(('dp', 'fsdp'))
- new_vectors: float32 [9984], P(('dp', 'fsdp'))
- new_first_qkv: float32 [768, 2304], P(('dp', 'fsdp'))
- new_first_out: float32 [768, 768], P(('dp', 'fsdp'))
- new_first_up: float32 [768, 3072], P(('dp', 'fsdp'))
- new_first_down: float32 [3072, 768], P(('dp', 'fsdp'))
- new_first_vec: float32 [9984], P(('dp', 'fsdp'))
- new_second_qkv: float32 [768, 2304], P(('dp', 'fsdp'))
- new_second_out: float32 [768, 768], P(('dp', 'fsdp'))
- new_second_up: float32 [768, 3072], P(('dp', 'fsdp'))
- new_second_down: float32 [3072, 768], P(('dp', 'fsdp'))
- new_second_vec: float32 [9984], P(('dp', 'fsdp'))
The draws below stay inside these ranges and needn't reach their ends.
Inputs may be any that keep to these rules, and one draw needn't show every extreme that they name: `segments`: in each row the numbers never fall; every number 0 to 7 names 1 to 64 consecutive tokens, and one names exactly 64.
All inputs are finite; a program needn't handle non-finite values.
Results may differ from the reference program's by a relative error of at most 0.012.
Values may be sent and summed in bfloat16 or wider, within the bound.
A program may use at most 128 MiB of HBM per device.

```python
import math
import jax
import jax.numpy as jnp
import numpy as np
from jax import lax

D = 768
HEADS = 12
HEAD_DIM = 64
ROT = 16
FF = 3072
ROWS = 128
SEGS = 8
STEP = 3
MOST = 64
TOKENS = 4096
DEVICES = 32


def draw_vectors(key, part):
    key_gain, key_shift = jax.random.split(key)
    row_index = jnp.arange(13 * D, dtype=jnp.int32) // D
    is_gain = (row_index == 0) | (row_index == 2)
    gain_draw = 1.0 + 0.5 * jnp.clip(jax.random.normal(key_gain, (13 * D,), jnp.float32), -1.0, 1.0)
    shift_draw = 0.3 * jnp.clip(jax.random.normal(key_shift, (13 * D,), jnp.float32), -3.0, 3.0)
    return jnp.where(is_gain, gain_draw, shift_draw)


def shard_levels(key, dims, shards, least, high):
    factor_of, own = 1.0, jax.random.fold_in(key, 6)
    for dim, parts in shards:
        steps = jnp.exp(jax.random.uniform(jax.random.fold_in(own, dim), (parts,), jnp.float32, least / len(shards), high / len(shards)))
        factor_of = factor_of * jnp.repeat(steps, dims[dim] // parts).reshape([-1 if axis == dim else 1 for axis in range(len(dims))])
    return factor_of


def profile(number_of, total, limit, skew):
    weights = [(1 << 20) // math.isqrt(standing ** skew) + 1 for standing in range(2, number_of + 1)]
    surplus, given = total - limit - (number_of - 1), [1] * (number_of - 1)
    while surplus > 0:
        free = [i for i in range(number_of - 1) if given[i] < limit]
        pool, budget = sum([weights[i] for i in free]), surplus
        for i in free:
            extra = min(limit - given[i], max(1, budget * weights[i] // pool), surplus)
            given[i] = given[i] + extra
            surplus = surplus - extra
    return np.array([limit] + given)


def ragged(own_key, number_of, total, limit, lean):
    if number_of == 2:
        one = jax.random.randint(own_key, (), max(1, total - limit), min(limit, total - 1) + 1)
        return jnp.stack([one, total - one])
    lengths = jnp.asarray(profile(number_of, total, limit, lean), jnp.int32)
    pairs = (number_of - 1) // 2
    donor, receiver = lengths[1:1 + 2 * pairs:2], lengths[2:2 + 2 * pairs:2]
    room = jnp.minimum(donor - 1, limit - receiver)
    moved = jax.random.randint(jax.random.fold_in(own_key, 1), (pairs,), 0, 1 << 20) % (room + 1)
    lengths = lengths.at[1:1 + 2 * pairs:2].set(donor - moved).at[2:2 + 2 * pairs:2].set(receiver + moved)
    return lengths[jax.random.permutation(jax.random.fold_in(own_key, 2), number_of)]


def normal_values(own_key, extent, width, limit, cuts=(), held_as=jnp.bfloat16):
    factor_of = shard_levels(own_key, extent, cuts, -0.22, 0.18) if cuts else 1.0
    array = jax.random.normal(own_key, extent, jnp.float32) * width * factor_of
    return jnp.minimum(jnp.maximum(array, -limit), limit).astype(held_as)


def setup_inputs(seed: int = 0) -> dict:
    seeds = jax.random.split(jax.random.key(seed), 19)
    return {
        "tokens": normal_values(seeds[0], (TOKENS, D), 1.0, 6.0, ((0, 32),)),
        "cotangent": normal_values(seeds[1], (TOKENS, D), 1.0, 6.0, ((0, 32),)),
        "segments": jax.vmap(lambda own: jnp.searchsorted(jnp.cumsum(ragged(own, SEGS, ROWS, MOST, 2)), jnp.arange(ROWS), side="right"))(jax.random.split(seeds[2], DEVICES)).reshape((DEVICES, ROWS)).astype(jnp.int32),
        "w_qkv": normal_values(seeds[3], (D, 3 * D), D ** -0.5, 0.21875, ((0, 32),), jnp.float32),
        "w_out": normal_values(seeds[4], (D, D), (D // 4) ** -0.5, 0.4375, ((0, 32),), jnp.float32),
        "w_up": normal_values(seeds[5], (D, FF), D ** -0.5, 0.21875, ((0, 32),), jnp.float32),
        "w_down": normal_values(seeds[6], (FF, D), FF ** -0.5, 0.109375, ((0, 32),), jnp.float32),
        "vectors": draw_vectors(jax.random.fold_in(seeds[18], 71), 0),
        "first_qkv": normal_values(seeds[8], (D, 3 * D), 0.2, 1.0, ((0, 32),), jnp.float32),
        "first_out": normal_values(seeds[9], (D, D), 0.2, 1.0, ((0, 32),), jnp.float32),
        "first_up": normal_values(seeds[10], (D, FF), 0.2, 1.0, ((0, 32),), jnp.float32),
        "first_down": normal_values(seeds[11], (FF, D), 0.2, 1.0, ((0, 32),), jnp.float32),
        "first_vec": normal_values(seeds[12], (13 * D,), 0.2, 1.0, ((0, 32),), jnp.float32),
        "second_qkv": jnp.clip(jnp.exp(math.log(0.2) - 2.3025851 * jax.random.uniform(seeds[13], (D, 3 * D), jnp.float32) ** shard_levels(seeds[13], (D, 3 * D), ((0, 32),), -0.2, 0.2)), 0.02, 0.2),
        "second_out": jnp.clip(jnp.exp(math.log(0.2) - 2.3025851 * jax.random.uniform(seeds[14], (D, D), jnp.float32) ** shard_levels(seeds[14], (D, D), ((0, 32),), -0.2, 0.2)), 0.02, 0.2),
        "second_up": jnp.clip(jnp.exp(math.log(0.2) - 2.3025851 * jax.random.uniform(seeds[15], (D, FF), jnp.float32) ** shard_levels(seeds[15], (D, FF), ((0, 32),), -0.2, 0.2)), 0.02, 0.2),
        "second_down": jnp.clip(jnp.exp(math.log(0.2) - 2.3025851 * jax.random.uniform(seeds[16], (FF, D), jnp.float32) ** shard_levels(seeds[16], (FF, D), ((0, 32),), -0.2, 0.2)), 0.02, 0.2),
        "second_vec": jnp.clip(jnp.exp(math.log(0.2) - 2.3025851 * jax.random.uniform(seeds[17], (13 * D,), jnp.float32) ** shard_levels(seeds[17], (13 * D,), ((0, 32),), -0.2, 0.2)), 0.02, 0.2),
    }


eps_norm = 1e-05
beta_first = 0.9
beta_second = 0.95
adam_epsilon = 1e-08
rate_matrix = 0.008
rate_vector = 0.1
decay_matrix = 0.01
rotary_base = 10000.0
mask_fill = -1e+30

def layer_norm(inputs, gain_row, offset):
    center = inputs - lax.optimization_barrier(jnp.mean(inputs, axis=-1, keepdims=True))
    inv_sigma = lax.rsqrt(lax.optimization_barrier(jnp.mean(center * center, axis=-1, keepdims=True)) + eps_norm)
    normed = center * inv_sigma
    return (normed, inv_sigma, normed * gain_row + offset)

def layer_norm_back(grad_norm, normed, inv_sigma, gain_row):
    scaled = grad_norm * gain_row
    return inv_sigma * (scaled - lax.optimization_barrier(jnp.mean(scaled, axis=-1, keepdims=True)) - normed * lax.optimization_barrier(jnp.mean(scaled * normed, axis=-1, keepdims=True)))

def gelu_value(inputs):
    return 0.5 * inputs * (1.0 + jax.scipy.special.erf(inputs * (1.0 / math.sqrt(2.0))))

def gelu_slope(inputs):
    cumulative = 0.5 * (1.0 + jax.scipy.special.erf(inputs * (1.0 / math.sqrt(2.0))))
    return cumulative + inputs * jnp.exp(-0.5 * inputs * inputs) * (1.0 / math.sqrt(2.0 * math.pi))

def rotary_tables(segment):
    rows_here = segment.shape[0]
    earlier = lax.optimization_barrier(jnp.sum((segment[None, :] < segment[:, None]).astype(jnp.int32), axis=1)).astype(jnp.int32)
    position = jnp.arange(rows_here, dtype=jnp.int32) - earlier
    half_rot = ROT // 2
    inverse = rotary_base ** (-2.0 * jnp.arange(half_rot, dtype=jnp.float32) / ROT)
    angles = position.astype(jnp.float32)[:, None] * inverse[None, :]
    return (jnp.cos(angles)[:, None, :], jnp.sin(angles)[:, None, :])

def rotate(tensor, cosine_part, sine_part):
    half_rot = ROT // 2
    front_part = tensor[..., :half_rot]
    middle = tensor[..., half_rot:ROT]
    remain = tensor[..., ROT:]
    return jnp.concatenate([front_part * cosine_part - middle * sine_part, middle * cosine_part + front_part * sine_part, remain], axis=-1)

def rotate_back(tensor, cosine_part, sine_part):
    half_rot = ROT // 2
    front_part = tensor[..., :half_rot]
    middle = tensor[..., half_rot:ROT]
    remain = tensor[..., ROT:]
    return jnp.concatenate([front_part * cosine_part + middle * sine_part, middle * cosine_part - front_part * sine_part, remain], axis=-1)

def doc_mask(segment):
    row_index = jnp.arange(segment.shape[0], dtype=jnp.int32)
    return (segment[:, None] == segment[None, :]) & (row_index[None, :] <= row_index[:, None])

def masked_scores(queries, key_rot, allowed):
    scores = jnp.einsum('qhd,khd->hqk', queries.astype(jnp.float32), key_rot.astype(jnp.float32)) * (1.0 / math.sqrt(HEAD_DIM))
    return jnp.where(allowed[None, :, :], scores, mask_fill)

def block_pass(tokens, cotangent, segment, low_qkv, low_out, low_up, low_down, low_vec):
    rows_here = tokens.shape[0]
    vec_table = low_vec.astype(jnp.float32).reshape(13, D)
    inputs = tokens.astype(jnp.float32)
    normed_one, sigma_one, hidden_one = layer_norm(inputs, vec_table[0], vec_table[1])
    normed_two, sigma_two, hidden_two = layer_norm(inputs, vec_table[2], vec_table[3])
    hidden_one = hidden_one.astype(jnp.bfloat16)
    hidden_two = hidden_two.astype(jnp.bfloat16)
    projected = jnp.dot(hidden_one, low_qkv, preferred_element_type=jnp.float32) + vec_table[4:7].reshape(-1)
    cosine_part, sine_part = rotary_tables(segment)
    queries = rotate(projected[:, :D].reshape(rows_here, HEADS, HEAD_DIM), cosine_part, sine_part).astype(jnp.bfloat16)
    key_rot = rotate(projected[:, D:2 * D].reshape(rows_here, HEADS, HEAD_DIM), cosine_part, sine_part).astype(jnp.bfloat16)
    values = projected[:, 2 * D:].reshape(rows_here, HEADS, HEAD_DIM).astype(jnp.bfloat16)
    allowed = doc_mask(segment)
    scores = masked_scores(queries, key_rot, allowed)
    top_score = lax.optimization_barrier(jnp.max(scores, axis=-1, keepdims=True))
    log_total = top_score + jnp.log(lax.optimization_barrier(jnp.sum(jnp.exp(scores - top_score), axis=-1, keepdims=True)))
    soft_weights = jnp.exp(scores - log_total).astype(jnp.bfloat16)
    context = jnp.einsum('hqk,khd->qhd', soft_weights.astype(jnp.float32), values.astype(jnp.float32)).reshape(rows_here, D).astype(jnp.bfloat16)
    attended = jnp.dot(context, low_out, preferred_element_type=jnp.float32) + vec_table[7]
    up_proj = jnp.dot(hidden_two, low_up, preferred_element_type=jnp.float32) + vec_table[8:12].reshape(-1)
    activated = gelu_value(up_proj).astype(jnp.bfloat16)
    feed_out = jnp.dot(activated, low_down, preferred_element_type=jnp.float32) + vec_table[12]
    output = (inputs + attended + feed_out).astype(jnp.bfloat16)
    grad_out = cotangent.astype(jnp.float32)
    grad_w_down = jnp.dot(activated.T, cotangent, preferred_element_type=jnp.float32)
    grad_act = jnp.dot(cotangent, low_down.T, preferred_element_type=jnp.float32)
    grad_up = grad_act * gelu_slope(up_proj)
    grad_up_low = grad_up.astype(jnp.bfloat16)
    grad_w_up = jnp.dot(hidden_two.T, grad_up_low, preferred_element_type=jnp.float32)
    grad_hidden_two = jnp.dot(grad_up_low, low_up.T, preferred_element_type=jnp.float32)
    grad_w_out = jnp.dot(context.T, cotangent, preferred_element_type=jnp.float32)
    grad_context = jnp.dot(cotangent, low_out.T, preferred_element_type=jnp.float32).astype(jnp.bfloat16).reshape(rows_here, HEADS, HEAD_DIM)
    again_scores = masked_scores(queries, key_rot, allowed)
    probs_full = jnp.exp(again_scores - log_total)
    grad_probs = jnp.einsum('qhd,khd->hqk', grad_context.astype(jnp.float32), values.astype(jnp.float32))
    row_inner = lax.optimization_barrier(jnp.sum(probs_full * grad_probs, axis=-1, keepdims=True))
    grad_scores = (probs_full * (grad_probs - row_inner) * (1.0 / math.sqrt(HEAD_DIM))).astype(jnp.bfloat16)
    grad_queries = jnp.einsum('hqk,khd->qhd', grad_scores.astype(jnp.float32), key_rot.astype(jnp.float32))
    grad_keys = jnp.einsum('hqk,qhd->khd', grad_scores.astype(jnp.float32), queries.astype(jnp.float32))
    grad_values = jnp.einsum('hqk,qhd->khd', soft_weights.astype(jnp.float32), grad_context.astype(jnp.float32))
    grad_projected = jnp.concatenate([rotate_back(grad_queries, cosine_part, sine_part).reshape(rows_here, D), rotate_back(grad_keys, cosine_part, sine_part).reshape(rows_here, D), grad_values.reshape(rows_here, D)], axis=1)
    grad_proj_low = grad_projected.astype(jnp.bfloat16)
    grad_w_qkv = jnp.dot(hidden_one.T, grad_proj_low, preferred_element_type=jnp.float32)
    grad_hidden_one = jnp.dot(grad_proj_low, low_qkv.T, preferred_element_type=jnp.float32)
    grad_table = jnp.concatenate([lax.optimization_barrier(jnp.sum(grad_hidden_one * normed_one, axis=0))[None], lax.optimization_barrier(jnp.sum(grad_hidden_one, axis=0))[None], lax.optimization_barrier(jnp.sum(grad_hidden_two * normed_two, axis=0))[None], lax.optimization_barrier(jnp.sum(grad_hidden_two, axis=0))[None], lax.optimization_barrier(jnp.sum(grad_projected, axis=0)).reshape(3, D), lax.optimization_barrier(jnp.sum(grad_out, axis=0))[None], lax.optimization_barrier(jnp.sum(grad_up, axis=0)).reshape(4, D), lax.optimization_barrier(jnp.sum(grad_out, axis=0))[None]], axis=0)
    grad_tokens = (grad_out + layer_norm_back(grad_hidden_one, normed_one, sigma_one, vec_table[0]) + layer_norm_back(grad_hidden_two, normed_two, sigma_two, vec_table[2])).astype(jnp.bfloat16)
    return (output, grad_tokens, (grad_w_qkv, grad_w_out, grad_w_up, grad_w_down, grad_table.reshape(-1)))

def adam_update(weight, gradient, moment_one, moment_two, rate_value, decay_value):
    new_one = beta_first * moment_one + (1.0 - beta_first) * gradient
    new_two = beta_second * moment_two + (1.0 - beta_second) * gradient * gradient
    corrected_one = new_one / (1.0 - beta_first ** STEP)
    corrected_two = new_two / (1.0 - beta_second ** STEP)
    new_weight = weight - rate_value * (corrected_one / (jnp.sqrt(corrected_two) + adam_epsilon) + decay_value * weight)
    return (new_weight, new_one, new_two)

def reference(tokens, cotangent, segments, w_qkv, w_out, w_up, w_down, vectors, first_qkv, first_out, first_up, first_down, first_vec, second_qkv, second_out, second_up, second_down, second_vec):
    device_count = segments.shape[0]
    group_size = max(1, min(device_count, 4096 // ROWS))
    low_qkv = w_qkv.astype(jnp.bfloat16)
    low_out = w_out.astype(jnp.bfloat16)
    low_up = w_up.astype(jnp.bfloat16)
    low_down = w_down.astype(jnp.bfloat16)
    low_vec = vectors.astype(jnp.bfloat16)
    token_blocks = tokens.reshape(device_count // group_size, group_size, ROWS, D)
    cot_blocks = cotangent.reshape(device_count // group_size, group_size, ROWS, D)
    seg_blocks = segments.reshape(device_count // group_size, group_size, ROWS)
    batched = jax.vmap(block_pass, in_axes=(0, 0, 0, None, None, None, None, None))

    def scan_step(running, block_data):
        outputs, grad_rows, grads = batched(block_data[0], block_data[1], block_data[2], low_qkv, low_out, low_up, low_down, low_vec)
        running = tuple((summed + member.sum(axis=0) for summed, member in zip(running, grads)))
        return (running, (outputs, grad_rows))
    initial = tuple((jnp.zeros(matrix.shape, jnp.float32) for matrix in (w_qkv, w_out, w_up, w_down, vectors)))
    totals, (outputs, grad_rows) = lax.scan(scan_step, initial, (token_blocks, cot_blocks, seg_blocks))
    factor = float(TOKENS) ** (-0.5)
    grad_w_qkv = totals[0] * factor
    grad_w_out = totals[1] * factor
    grad_w_up = totals[2] * factor
    grad_w_down = totals[3] * factor
    grad_vectors = totals[4] * factor
    new_w_qkv, new_first_qkv, new_second_qkv = adam_update(w_qkv, grad_w_qkv, first_qkv, second_qkv, rate_matrix, decay_matrix)
    new_w_out, new_first_out, new_second_out = adam_update(w_out, grad_w_out, first_out, second_out, rate_matrix, decay_matrix)
    new_w_up, new_first_up, new_second_up = adam_update(w_up, grad_w_up, first_up, second_up, rate_matrix, decay_matrix)
    new_w_down, new_first_down, new_second_down = adam_update(w_down, grad_w_down, first_down, second_down, rate_matrix, decay_matrix)
    new_vectors, new_first_vec, new_second_vec = adam_update(vectors, grad_vectors, first_vec, second_vec, rate_vector, 0.0)
    output = outputs.reshape(TOKENS, D)
    grad_tokens = grad_rows.reshape(TOKENS, D)
    return (output, grad_tokens, grad_w_qkv, grad_w_out, grad_w_up, grad_w_down, grad_vectors, new_w_qkv, new_w_out, new_w_up, new_w_down, new_vectors, new_first_qkv, new_first_out, new_first_up, new_first_down, new_first_vec, new_second_qkv, new_second_out, new_second_up, new_second_down, new_second_vec)
```

```python
import functools
import math

import jax
import jax.numpy as jnp
import ml_dtypes
import numpy as np
from jax import lax
from jax.experimental import pallas as pl
from jax.experimental.pallas import tpu as pltpu
from jax.sharding import PartitionSpec as P

D = 768
HEADS = 12
HEAD_DIM = 64
ROT = 16
STEP = 3


eps_norm = 1e-05
beta_first = 0.9
beta_second = 0.95
adam_epsilon = 1e-08
rate_matrix = 0.008
rate_vector = 0.1
decay_matrix = 0.01
rotary_base = 10000.0
mask_fill = -1e30


def layer_norm(inputs, gain_row, offset):
    center = inputs - jnp.mean(inputs, axis=-1, keepdims=True)
    inv_sigma = lax.rsqrt(jnp.mean(center * center, axis=-1, keepdims=True) + eps_norm)
    normed = center * inv_sigma
    return (normed, inv_sigma, normed * gain_row + offset)


def layer_norm_back(grad_norm, normed, inv_sigma, gain_row):
    scaled = grad_norm * gain_row
    return inv_sigma * (
        scaled
        - jnp.mean(scaled, axis=-1, keepdims=True)
        - normed * jnp.mean(scaled * normed, axis=-1, keepdims=True)
    )


def gelu_value(inputs):
    return 0.5 * inputs * (1.0 + jax.scipy.special.erf(inputs * (1.0 / math.sqrt(2.0))))


def gelu_slope(inputs):
    cumulative = 0.5 * (1.0 + jax.scipy.special.erf(inputs * (1.0 / math.sqrt(2.0))))
    return cumulative + inputs * jnp.exp(-0.5 * inputs * inputs) * (1.0 / math.sqrt(2.0 * math.pi))


def rotary_tables(segment):
    rows_here = segment.shape[0]
    earlier = jnp.sum((segment[None, :] < segment[:, None]).astype(jnp.int32), axis=1)
    position = jnp.arange(rows_here, dtype=jnp.int32) - earlier
    half_rot = ROT // 2
    inverse = rotary_base ** (-2.0 * jnp.arange(half_rot, dtype=jnp.float32) / ROT)
    angles = position.astype(jnp.float32)[:, None] * inverse[None, :]
    return (jnp.cos(angles)[:, None, :], jnp.sin(angles)[:, None, :])


def rotate(tensor, cosine_part, sine_part):
    half_rot = ROT // 2
    front_part = tensor[..., :half_rot]
    middle = tensor[..., half_rot:ROT]
    remain = tensor[..., ROT:]
    return jnp.concatenate(
        [
            front_part * cosine_part - middle * sine_part,
            middle * cosine_part + front_part * sine_part,
            remain,
        ],
        axis=-1,
    )


def rotate_back(tensor, cosine_part, sine_part):
    half_rot = ROT // 2
    front_part = tensor[..., :half_rot]
    middle = tensor[..., half_rot:ROT]
    remain = tensor[..., ROT:]
    return jnp.concatenate(
        [
            front_part * cosine_part + middle * sine_part,
            middle * cosine_part - front_part * sine_part,
            remain,
        ],
        axis=-1,
    )


def doc_mask(segment):
    row_index = jnp.arange(segment.shape[0], dtype=jnp.int32)
    return (segment[:, None] == segment[None, :]) & (row_index[None, :] <= row_index[:, None])


def masked_scores(queries, key_rot, allowed):
    scores = jnp.einsum("qhd,khd->hqk", queries, key_rot, preferred_element_type=jnp.float32) * (
        1.0 / math.sqrt(HEAD_DIM)
    )
    return jnp.where(allowed[None, :, :], scores, mask_fill)


def forward_pass(
    tokens, allowed, cosine_part, sine_part, full_qkv, full_out, full_up, full_down, full_vec
):
    rows_here = tokens.shape[0]
    vec_table = full_vec.astype(jnp.float32).reshape(13, D)
    inputs = tokens.astype(jnp.float32)
    normed_one, sigma_one, hidden_one = layer_norm(inputs, vec_table[0], vec_table[1])
    normed_two, sigma_two, hidden_two = layer_norm(inputs, vec_table[2], vec_table[3])
    hidden_one = hidden_one.astype(jnp.bfloat16)
    hidden_two = hidden_two.astype(jnp.bfloat16)
    projected = jnp.dot(hidden_one, full_qkv, preferred_element_type=jnp.float32) + vec_table[
        4:7
    ].reshape(-1)
    queries = rotate(
        projected[:, :D].reshape(rows_here, HEADS, HEAD_DIM), cosine_part, sine_part
    ).astype(jnp.bfloat16)
    key_rot = rotate(
        projected[:, D : 2 * D].reshape(rows_here, HEADS, HEAD_DIM), cosine_part, sine_part
    ).astype(jnp.bfloat16)
    values = projected[:, 2 * D :].reshape(rows_here, HEADS, HEAD_DIM).astype(jnp.bfloat16)
    scores = masked_scores(queries, key_rot, allowed)
    top_score = jnp.max(scores, axis=-1, keepdims=True)
    log_total = top_score + jnp.log(jnp.sum(jnp.exp(scores - top_score), axis=-1, keepdims=True))
    soft_weights = jnp.exp(scores - log_total).astype(jnp.bfloat16)
    context = (
        jnp.einsum("hqk,khd->qhd", soft_weights, values, preferred_element_type=jnp.float32)
        .reshape(rows_here, D)
        .astype(jnp.bfloat16)
    )
    attended = jnp.dot(context, full_out, preferred_element_type=jnp.float32) + vec_table[7]
    up_proj = jnp.dot(hidden_two, full_up, preferred_element_type=jnp.float32) + vec_table[
        8:12
    ].reshape(-1)
    activated = gelu_value(up_proj).astype(jnp.bfloat16)
    feed_out = jnp.dot(activated, full_down, preferred_element_type=jnp.float32) + vec_table[12]
    output = (inputs + attended + feed_out).astype(jnp.bfloat16)
    saved = (
        normed_one,
        sigma_one,
        hidden_one,
        normed_two,
        sigma_two,
        hidden_two,
        queries,
        key_rot,
        values,
        log_total,
        context,
        up_proj,
        activated,
    )
    return (output, saved)


def backward_pass(
    saved,
    cotangent,
    allowed,
    cosine_part,
    sine_part,
    back_qkv,
    back_out,
    back_up,
    back_down,
    back_vec,
):
    (
        normed_one,
        sigma_one,
        hidden_one,
        normed_two,
        sigma_two,
        hidden_two,
        queries,
        key_rot,
        values,
        log_total,
        context,
        up_proj,
        activated,
    ) = saved
    rows_here = cotangent.shape[0]
    vec_table = back_vec.astype(jnp.float32).reshape(13, D)
    grad_out = cotangent.astype(jnp.float32)
    grad_w_down = jnp.dot(activated.T, cotangent, preferred_element_type=jnp.float32)
    grad_act = jnp.dot(cotangent, back_down.T, preferred_element_type=jnp.float32)
    grad_up = grad_act * gelu_slope(up_proj)
    grad_up_low = grad_up.astype(jnp.bfloat16)
    grad_w_up = jnp.dot(hidden_two.T, grad_up_low, preferred_element_type=jnp.float32)
    grad_hidden_two = jnp.dot(grad_up_low, back_up.T, preferred_element_type=jnp.float32)
    grad_w_out = jnp.dot(context.T, cotangent, preferred_element_type=jnp.float32)
    grad_context = (
        jnp.dot(cotangent, back_out.T, preferred_element_type=jnp.float32)
        .astype(jnp.bfloat16)
        .reshape(rows_here, HEADS, HEAD_DIM)
    )
    again_scores = masked_scores(queries, key_rot, allowed)
    probs_full = jnp.exp(again_scores - log_total)
    probs_low = probs_full.astype(jnp.bfloat16)
    grad_probs = jnp.einsum(
        "qhd,khd->hqk", grad_context, values, preferred_element_type=jnp.float32
    )
    row_inner = jnp.sum(probs_full * grad_probs, axis=-1, keepdims=True)
    grad_scores = (probs_full * (grad_probs - row_inner) * (1.0 / math.sqrt(HEAD_DIM))).astype(
        jnp.bfloat16
    )
    grad_queries = jnp.einsum(
        "hqk,khd->qhd", grad_scores, key_rot, preferred_element_type=jnp.float32
    )
    grad_keys = jnp.einsum("hqk,qhd->khd", grad_scores, queries, preferred_element_type=jnp.float32)
    grad_values = jnp.einsum(
        "hqk,qhd->khd", probs_low, grad_context, preferred_element_type=jnp.float32
    )
    grad_projected = jnp.concatenate(
        [
            rotate_back(grad_queries, cosine_part, sine_part).reshape(rows_here, D),
            rotate_back(grad_keys, cosine_part, sine_part).reshape(rows_here, D),
            grad_values.reshape(rows_here, D),
        ],
        axis=1,
    )
    grad_proj_low = grad_projected.astype(jnp.bfloat16)
    grad_w_qkv = jnp.dot(hidden_one.T, grad_proj_low, preferred_element_type=jnp.float32)
    grad_hidden_one = jnp.dot(grad_proj_low, back_qkv.T, preferred_element_type=jnp.float32)
    grad_table = jnp.concatenate(
        [
            jnp.sum(grad_hidden_one * normed_one, axis=0)[None],
            jnp.sum(grad_hidden_one, axis=0)[None],
            jnp.sum(grad_hidden_two * normed_two, axis=0)[None],
            jnp.sum(grad_hidden_two, axis=0)[None],
            jnp.sum(grad_projected, axis=0).reshape(3, D),
            jnp.sum(grad_out, axis=0)[None],
            jnp.sum(grad_up, axis=0).reshape(4, D),
            jnp.sum(grad_out, axis=0)[None],
        ],
        axis=0,
    )
    grad_tokens = (
        grad_out
        + layer_norm_back(grad_hidden_one, normed_one, sigma_one, vec_table[0])
        + layer_norm_back(grad_hidden_two, normed_two, sigma_two, vec_table[2])
    ).astype(jnp.bfloat16)
    grad_table = lax.optimization_barrier(grad_table)
    return (grad_tokens, grad_w_qkv, grad_w_out, grad_w_up, grad_w_down, grad_table.reshape(-1))


def adam_update(weight, gradient, moment_one, moment_two, rate_value, decay_value):
    new_one = beta_first * moment_one + (1.0 - beta_first) * gradient
    new_two = beta_second * moment_two + (1.0 - beta_second) * gradient * gradient
    corrected_one = new_one / (1.0 - beta_first**STEP)
    corrected_two = new_two / (1.0 - beta_second**STEP)
    new_weight = weight - rate_value * (
        corrected_one / (jnp.sqrt(corrected_two) + adam_epsilon) + decay_value * weight
    )
    return (new_weight, new_one, new_two)


MESH = pl.DeviceIdType.MESH
LANES = 128


def mm(left, right):
    return lax.dot_general(left, right, (((1,), (0,)), ((), ())), preferred_element_type=jnp.float32)


def mm_nt(left, right):
    return lax.dot_general(left, right, (((1,), (1,)), ((), ())), preferred_element_type=jnp.float32)


def mm_tn(left, right):
    return lax.dot_general(left, right, (((0,), (0,)), ((), ())), preferred_element_type=jnp.float32)


def rotary_constants(rows):
    half_rot = ROT // 2
    lane = np.arange(LANES) % HEAD_DIM
    inverse = np.float32(rotary_base) ** (-2.0 * np.arange(half_rot, dtype=np.float32) / ROT)
    angles = np.arange(rows, dtype=np.float32)[:, None] * inverse.astype(np.float32)[lane % half_rot]
    cosine = np.where(lane < ROT, np.cos(angles), 1.0).astype(np.float32)
    sine = np.where(lane < ROT, np.sin(angles), 0.0).astype(np.float32)
    both = np.concatenate([cosine, sine], axis=1)
    high = both.astype(ml_dtypes.bfloat16)
    low = (both - high.astype(np.float32)).astype(ml_dtypes.bfloat16)
    swap = np.zeros((LANES, LANES), np.float32)
    for j in range(LANES):
        if lane[j] < half_rot:
            swap[j + half_rot, j] = -1.0
        elif lane[j] < ROT:
            swap[j - half_rot, j] = 1.0
    return np.concatenate([high, low], axis=1), swap.astype(ml_dtypes.bfloat16)


def swapped(value, swap):
    high = value.astype(jnp.bfloat16)
    low = (value - high.astype(jnp.float32)).astype(jnp.bfloat16)
    return mm(high, swap) + mm(low, swap)


def normalize(value):
    center = value - jnp.mean(value, axis=-1, keepdims=True)
    inv_sigma = lax.rsqrt(jnp.mean(center * center, axis=-1, keepdims=True) + eps_norm)
    return center * inv_sigma, inv_sigma


SENDS, ARRIVALS = 160, 160


def layer_kernel(nd, nf, scale, *refs):
    (tok, cot, seg, wq, wo, wu, wd, vtab, trig, swap) = refs[:10]
    (out, gtok, gq, go, gu, gd, gv) = refs[10:17]
    (xs, ys, sg, vd, vz, vp, upS, qS, g_up, g_q, g_down, g_out, w_up, w_q, w_o) = refs[17:32]
    (norm, h1, h2, act, du, outp, ep, proj, ctx, dctx, dp_low, table) = refs[32:44]
    m_up, m_q, m_down, m_out = refs[44:48]
    p_up, p_q, p_down, p_out = refs[48:52]
    r_up, r_q, r_down, r_out = refs[52:56]
    l_up, l_q, l_down, l_out = refs[56:60]
    a_up, a_q, a_down, a_out = refs[60:64]
    (b_up, b_q, f_up, f_q, o_send, e_send, o_recv, e_recv, tz, tp) = refs[64:74]
    sent, came = refs[74:]
    nz = nf // 2
    rows, width = tok.shape
    low = jnp.bfloat16
    wide = jnp.float32
    d, f = lax.axis_index("dp"), lax.axis_index("fsdp")
    z, c = lax.div(f, 2), lax.rem(f, 2)
    part = wq.shape[1] // nd
    third = part // 3
    hid = wu.shape[1] // nd
    block = wq.shape[0]

    state = {"sent": 0, "came": 0}
    pend = []

    def grab(count):
        at = state["came"]
        state["came"] += count
        assert state["came"] <= ARRIVALS
        return at

    def send(source, target, arrival, peer, cond=None):
        slot = state["sent"]
        state["sent"] += 1
        assert slot < SENDS

        copy = pltpu.make_async_remote_copy(
            src_ref=source(),
            dst_ref=target(),
            send_sem=sent.at[slot],
            recv_sem=came.at[arrival],
            device_id=peer,
            device_id_type=MESH,
        )
        pend.append((cond, copy))
        if cond is None:
            copy.start()
        else:
            pl.when(cond)(lambda: copy.start())

    def landed(ref, arrival):
        pltpu.make_async_copy(ref, ref, came.at[arrival]).wait()

    def mate(k):
        return (lax.rem(d + k, nd), f)

    def origin(k):
        return lax.rem(d + nd - k, nd)

    pair = (d, z * 2 + 1 - c)
    right, left = (d, (z + 1) * 2 + c), (d, (z - 1) * 2 + c)
    level = lambda k: (d, lax.rem(z + k, nz) * 2 + c)

    def span(index, size):
        return pl.ds(pl.multiple_of(index * size, size), size)

    barrier = pltpu.get_barrier_semaphore()
    peers = [mate(k) for k in range(1, nd)] + [level(k) for k in range(1, nz)] + [pair]
    for peer in peers:
        pl.semaphore_signal(barrier, inc=1, device_id=peer, device_id_type=MESH)
    g_down[f] = wd[...].astype(low)
    g_out[f] = wo[...].astype(low)
    pl.semaphore_wait(barrier, len(peers))

    gathered = [g_down, g_out, g_up, g_q]
    wire = [grab(nz) for _ in gathered]
    cross = [grab(nz) for _ in gathered]

    def own(p):
        buf = gathered[p]
        here = lambda: buf.at[f]
        send(here, here, wire[p] + z, right, z < nz - 1)
        send(here, here, wire[p] + z, left, z > 0)
        send(here, here, cross[p] + z, pair)

    own(0)
    own(1)
    for j in range(nd):
        upS[j] = wu[:, j * hid : (j + 1) * hid].astype(low)
        qS[j] = jnp.concatenate(
            [
                wq[:, t * width + j * third : t * width + (j + 1) * third]
                for t in range(3)
            ],
            axis=1,
        ).astype(low)
    mates = range(1, nd)
    up_in, q_in = grab(nd), grab(nd)
    x_in, y_in, s_in, v_in = grab(nd), grab(nd), grab(nd), grab(nd)
    for k in mates:
        to = lax.rem(d + k, nd)
        send(lambda: upS.at[to], lambda: g_up.at[f, d], up_in + k, mate(k))
        send(lambda: qS.at[to], lambda: g_q.at[f, d], q_in + k, mate(k))
        send(lambda: vtab, lambda: vd.at[d], v_in + k, mate(k))
        send(lambda: seg, lambda: sg.at[d], s_in + k, mate(k))
    for k in mates:
        send(lambda: tok, lambda: xs.at[span(d, rows)], x_in + k, mate(k))
        send(lambda: cot, lambda: ys.at[span(d, rows)], y_in + k, mate(k))
    g_up[f, d] = upS[d]
    g_q[f, d] = qS[d]
    xs[span(d, rows), :] = tok[...]
    ys[span(d, rows), :] = cot[...]
    sg[d] = seg[...]
    vd[d] = vtab[...]
    for k in mates:
        landed(g_up.at[f, origin(k)], up_in + k)
    own(2)
    for k in mates:
        landed(g_q.at[f, origin(k)], q_in + k)
    own(3)

    vz_in, vp_in = grab(nz), grab(1)
    for k in mates:
        landed(vd.at[origin(k)], v_in + k)
    vz[z] = sum(vd[j].astype(wide) for j in range(nd)).astype(low)
    for k in range(1, nz):
        send(lambda: vz.at[z], lambda: vz.at[z], vz_in + k, level(k))

    def relay(p, hop):
        buf = gathered[p]
        for origin_z, cond, onward, more in (
            (z - hop, z >= hop, right, z < nz - 1),
            (z + hop, z + hop < nz, left, z > 0),
        ):
            piece = functools.partial(lambda o: buf.at[o * 2 + c], origin_z)
            pl.when(cond)(functools.partial(lambda pc, o: landed(pc(), wire[p] + o), piece, origin_z))
            send(piece, piece, wire[p] + origin_z, onward, jnp.logical_and(cond, more))
            send(piece, piece, cross[p] + origin_z, pair, cond)

    for hop in range(1, nz):
        for p in range(4):
            relay(p, hop)
        if hop == 1:
            for k in range(1, nz):
                landed(vz.at[lax.rem(z + nz - k, nz)], vz_in + k)
            vp[c] = sum(vz[j].astype(wide) for j in range(nz)).astype(low)
            send(lambda: vp.at[c], lambda: vp.at[c], vp_in, pair)
            landed(vp.at[1 - c], vp_in)
    vec = vp[0].astype(wide) + vp[1].astype(wide)

    for k in mates:
        landed(xs.at[span(origin(k), rows)], x_in + k)
        landed(ys.at[span(origin(k), rows)], y_in + k)
        landed(sg.at[origin(k)], s_in + k)
    for b in range(nd):
        at = slice(b * rows, (b + 1) * rows)
        value, _ = normalize(xs[at, :].astype(wide))
        norm[at, :] = value
        h1[at, :] = (value * vec[0:1] + vec[1:2]).astype(low)
        h2[at, :] = (value * vec[2:3] + vec[3:4]).astype(low)

    def mine_of(pieces):
        return sum(jnp.where(d == j, pieces[j], 0.0) for j in range(nd))

    for p in (0, 2):
        for o in range(nz):
            landed(gathered[p].at[2 * o + 1 - c], cross[p] + o)
    def unblock(source, target):
        for j in range(nd):
            for o in range(nz):
                value = jnp.concatenate(
                    [source[2 * o, j].astype(wide), source[2 * o + 1, j].astype(wide)], axis=0
                )
                start = (j * nf + 2 * o) * block
                target[start : start + 2 * block, :] = value.astype(low)

    unblock(g_up, w_up)
    w_down = g_down[...].reshape(hid, width)
    cu = mine_of([vec[8 + j : 9 + j] for j in range(nd)])
    cut = 256
    du_sums = []
    for n in range(hid // cut):
        cols = slice(n * cut, (n + 1) * cut)
        u = mm(h2[...], w_up[:, cols]) + cu[:, cols]
        da = mm_nt(ys[...], w_down[cols, :])
        phi = 0.5 * (1.0 + lax.erf(u * (1.0 / math.sqrt(2.0))))
        act[:, cols] = (u * phi).astype(low)
        value = da * (phi + u * jnp.exp(-0.5 * u * u) * (1.0 / math.sqrt(2.0 * math.pi)))
        du_sums.append(jnp.sum(value, axis=0, keepdims=True))
        du[:, cols] = value.astype(low)
    du_sum = jnp.concatenate(du_sums, axis=1)
    value = mm_tn(act[...], ys[...])
    size = wd.shape[0]
    for i in range(nf):
        m_down[i % 2, i // 2] = value[i * size : (i + 1) * size].astype(low)
    value = mm_tn(h2[...], du[...])
    for j in range(nd):
        for i in range(nf):
            start = (j * nf + i) * block
            m_up[i % 2, i // 2, j] = value[start : start + block].astype(low)

    sums = [m_down, m_up, m_q, m_out]
    paired = [p_down, p_up, p_q, p_out]
    rights = [r_down, r_up, r_q, r_out]
    lefts = [l_down, l_up, l_q, l_out]
    totals = [a_down, a_up, a_q, a_out]
    pair_in = [grab(1) for _ in sums]
    right_in = [grab(nz) for _ in sums]
    left_in = [grab(nz) for _ in sums]

    def share(p):
        send(lambda: sums[p].at[1 - c], lambda: paired[p].at[...], pair_in[p], pair)

    def first(p):
        landed(paired[p], pair_in[p])
        for k in range(nz - 1, 0, -1):
            for target, bound, inbox, sem, peer in (
                (z + k, z == 0, rights[p], right_in[p], right),
                (z - k, z == nz - 1, lefts[p], left_in[p], left),
            ):

                def add(target=target):
                    sums[p][c, target] = (
                        sums[p][c, target].astype(wide) + paired[p][target].astype(wide)
                    ).astype(low)

                pl.when(bound)(add)
                send(
                    functools.partial(lambda t: sums[p].at[c, t], target),
                    functools.partial(lambda box, t: box.at[t], inbox, target),
                    sem + target,
                    peer,
                    bound,
                )

    def middle(p, k):
        for target, bound, inbox, sem, peer in (
            (z + k, jnp.logical_and(z > 0, z + k < nz), rights[p], right_in[p], right),
            (z - k, jnp.logical_and(z < nz - 1, z >= k), lefts[p], left_in[p], left),
        ):

            def add(target=target, inbox=inbox, sem=sem):
                landed(inbox.at[target], sem + target)
                sums[p][c, target] = (
                    sums[p][c, target].astype(wide)
                    + paired[p][target].astype(wide)
                    + inbox[target].astype(wide)
                ).astype(low)

            pl.when(bound)(add)
            send(
                functools.partial(lambda t: sums[p].at[c, t], target),
                functools.partial(lambda box, t: box.at[t], inbox, target),
                sem + target,
                peer,
                bound,
            )

    def last(p):
        totals[p][...] = sums[p][c, z].astype(wide) + paired[p][z].astype(wide)
        for bound, inbox, sem in ((z > 0, rights[p], right_in[p]), (z < nz - 1, lefts[p], left_in[p])):

            def add(inbox=inbox, sem=sem):
                landed(inbox.at[z], sem + z)
                totals[p][...] = totals[p][...] + inbox[z].astype(wide)

            pl.when(bound)(add)

    share(0)
    share(1)
    outp[...] = mm(act[...], w_down)
    dh = mm_nt(du[...], w_up[...])
    ep[...] = dh * vec[2:3]
    table[...] = jnp.zeros_like(table)
    table[2:3, :] = jnp.sum(dh * norm[...], axis=0, keepdims=True)
    table[3:4, :] = jnp.sum(dh, axis=0, keepdims=True)
    dy_sum = jnp.sum(cot[...].astype(wide), axis=0, keepdims=True)
    table[7:8, :] = dy_sum
    table[12:13, :] = dy_sum
    for j in range(nd):
        table[8 + j : 9 + j, :] = jnp.where(d == j, du_sum, 0.0)
    first(0)
    first(1)

    for p in (1, 3):
        for o in range(nz):
            landed(gathered[p].at[2 * o + 1 - c], cross[p] + o)
    unblock(g_q, w_q)
    for o in range(nz):
        value = jnp.concatenate([g_out[2 * o].astype(wide), g_out[2 * o + 1].astype(wide)], axis=0)
        w_o[2 * o * block : 2 * (o + 1) * block, :] = value.astype(low)
    cq = jnp.concatenate(
        [
            mine_of([vec[4 + t : 5 + t, j * third : (j + 1) * third] for j in range(nd)])
            for t in range(3)
        ],
        axis=1,
    )
    proj[...] = mm(h1[...], w_q[...]) + cq
    dctx[...] = mm_nt(ys[...], w_o[...]).astype(low)
    row_at = lax.broadcasted_iota(jnp.int32, (rows, rows), 0)
    col_at = lax.broadcasted_iota(jnp.int32, (rows, rows), 1)
    causal = col_at <= row_at
    sharp = 1.0 / math.sqrt(HEAD_DIM)

    def attend(b, dp_sum):
        at = span(b, rows)
        name = jnp.broadcast_to(sg[b][0:1, :].astype(wide), (rows, rows))
        allowed = jnp.logical_and(name == name.T, causal)
        pos = jnp.sum(jnp.where(allowed, 1.0, 0.0), axis=1, keepdims=True) - 1.0
        hot = jnp.where(col_at.astype(wide) == pos, 1.0, 0.0).astype(low)
        tables = mm(hot, trig[...])
        tables = tables[:, : 2 * LANES] + tables[:, 2 * LANES :]
        cosine, sine = tables[:, :LANES], tables[:, LANES:]
        base = proj[at, :]
        turned = []
        for t in range(2 * third // LANES):
            x = base[:, t * LANES : (t + 1) * LANES]
            turned.append((x * cosine + swapped(x, swap[...]) * sine).astype(low))
        turned = jnp.concatenate(turned, axis=1)
        values = base[:, 2 * third :].astype(low)
        grad_c = dctx[at, :]
        dqs, dks, dvs, contexts = [], [], [], []
        for h in range(third // HEAD_DIM):
            hs = slice(h * HEAD_DIM, (h + 1) * HEAD_DIM)
            q, k = turned[:, hs], turned[:, third + h * HEAD_DIM : third + (h + 1) * HEAD_DIM]
            v, dc = values[:, hs], grad_c[:, hs]
            s = jnp.where(allowed, mm_nt(q, k) * sharp, mask_fill)
            e = jnp.exp(s - jnp.max(s, axis=-1, keepdims=True))
            a = e / jnp.sum(e, axis=-1, keepdims=True)
            a_low = a.astype(low)
            contexts.append(mm(a_low, v))
            da = mm_nt(dc, v)
            inner = jnp.sum(a * da, axis=-1, keepdims=True)
            ds = (a * (da - inner) * sharp).astype(low)
            dqs.append(mm(ds, k))
            dks.append(mm_tn(ds, q))
            dvs.append(mm_tn(a_low, dc))
        ctx[at, :] = jnp.concatenate(contexts, axis=1).astype(low)
        turned = jnp.concatenate(dqs + dks, axis=1)
        grads = []
        for t in range(2 * third // LANES):
            x = turned[:, t * LANES : (t + 1) * LANES]
            grads.append(x * cosine - swapped(x, swap[...]) * sine)
        grads = jnp.concatenate(grads + dvs, axis=1)
        dp_low[at, :] = grads.astype(low)
        return dp_sum + jnp.sum(grads, axis=0, keepdims=True)

    dp_sum = lax.fori_loop(0, nd, attend, jnp.zeros((1, part), wide))
    for t in range(3):
        piece = dp_sum[:, t * third : (t + 1) * third]
        table[4 + t : 5 + t, :] = jnp.concatenate(
            [jnp.where(d == j, piece, 0.0) for j in range(nd)], axis=1
        )
    value = mm_tn(h1[...], dp_low[...])
    for j in range(nd):
        for i in range(nf):
            start = (j * nf + i) * block
            m_q[i % 2, i // 2, j] = value[start : start + block].astype(low)
    value = mm_tn(ctx[...], ys[...])
    for i in range(nf):
        m_out[i % 2, i // 2] = value[i * block : (i + 1) * block].astype(low)
    share(2)
    share(3)
    outp[...] += mm(ctx[...], w_o[...])
    dh = mm_nt(dp_low[...], w_q[...])
    ep[...] += dh * vec[0:1]
    table[0:1, :] = jnp.sum(dh * norm[...], axis=0, keepdims=True)
    table[1:2, :] = jnp.sum(dh, axis=0, keepdims=True)
    o_in, e_in, t_in = grab(nd), grab(nd), grab(nd)
    o_send[...] = outp[...].astype(low)
    e_send[...] = ep[...].astype(low)
    vd_in = vd
    tz_in, tp_in = grab(nz), grab(1)
    first(2)
    first(3)
    tz[0] = table[...].astype(low)
    for k in mates:
        to = lax.rem(d + k, nd)
        send(lambda: tz.at[0], lambda: tz.at[k], t_in + k, mate(k))
    for k in mates:
        to = lax.rem(d + k, nd)
        send(lambda: o_send.at[span(to, rows)], lambda: o_recv.at[k], o_in + k, mate(k))
        send(lambda: e_send.at[span(to, rows)], lambda: e_recv.at[k], e_in + k, mate(k))
    for p in range(4):
        for k in range(nz - 2, 0, -1):
            middle(p, k)
    for k in mates:
        landed(tz.at[k], t_in + k)
    tz[nd] = (table[...] + sum(tz[k].astype(wide) for k in mates)).astype(low)
    for k in range(1, nz):
        send(lambda: tz.at[nd], lambda: tz.at[nd + k], tz_in + k, level(k))
    fu_in, fq_in = grab(nd), grab(nd)
    for p, whole, box, arrivals in ((1, b_up, f_up, fu_in), (2, b_q, f_q, fq_in)):
        last(p)
        whole[...] = totals[p][...].astype(low)
        for k in mates:
            to = lax.rem(d + k, nd)
            send(
                functools.partial(lambda w, t: w.at[t], whole, to),
                functools.partial(lambda x: x.at[d], box),
                arrivals + k,
                mate(k),
            )
        box[d] = whole[d]
    for k in range(1, nz):
        landed(tz.at[nd + k], tz_in + k)
    tp[0] = sum(tz[nd + k].astype(wide) for k in range(nz)).astype(low)
    send(lambda: tp.at[0], lambda: tp.at[1], tp_in, pair)
    last(0)
    last(3)
    gd[...] = a_down[...] * scale
    go[...] = a_out[...] * scale
    for k in mates:
        landed(o_recv.at[k], o_in + k)
        landed(e_recv.at[k], e_in + k)
    total = tok[...].astype(wide) + vec[7:8] + vec[12:13] + outp[span(d, rows), :]
    out[...] = (total + sum(o_recv[k].astype(wide) for k in mates)).astype(low)
    value, inv_sigma = normalize(tok[...].astype(wide))
    e = ep[span(d, rows), :] + sum(e_recv[k].astype(wide) for k in mates)
    gtok[...] = (
        cot[...].astype(wide)
        + inv_sigma
        * (
            e
            - jnp.mean(e, axis=-1, keepdims=True)
            - value * jnp.mean(e * value, axis=-1, keepdims=True)
        )
    ).astype(low)
    landed(tp.at[1], tp_in)
    gv[...] = (tp[0].astype(wide) + tp[1].astype(wide)) * scale
    for k in mates:
        landed(f_up.at[origin(k)], fu_in + k)
        landed(f_q.at[origin(k)], fq_in + k)
    for j in range(nd):
        gu[:, j * hid : (j + 1) * hid] = f_up[j].astype(wide) * scale
    gq[...] = scale * jnp.concatenate(
        [f_q[j].astype(wide)[:, t * third : (t + 1) * third] for t in range(3) for j in range(nd)],
        axis=1,
    )
    for cond, copy in pend:
        if cond is None:
            copy.wait_send()
        else:
            pl.when(cond)(functools.partial(lambda x: x.wait_send(), copy))


def layer_step(tokens, cotangent, segments, w_qkv, w_out, w_up, w_down, vectors, nd, nf):
    rows, width = tokens.shape
    low, wide = jnp.bfloat16, jnp.float32
    nz, block, size = nf // 2, w_qkv.shape[0], w_down.shape[0]
    part, hid = w_qkv.shape[1] // nd, w_up.shape[1] // nd
    third = part // 3
    group = nd * rows
    rank = lax.axis_index("dp") * nf + lax.axis_index("fsdp")
    count = vectors.shape[0]
    flat = lax.dynamic_update_slice(
        jnp.zeros((16 * width,), low), vectors.astype(low), (rank * count,)
    )
    trig, swap = rotary_constants(rows)
    inputs = (
        tokens,
        cotangent,
        jnp.broadcast_to(segments, (8, rows)),
        w_qkv,
        w_out,
        w_up,
        w_down,
        flat.reshape(16, width),
        jnp.asarray(trig),
        jnp.asarray(swap),
    )
    outs = [
        jax.ShapeDtypeStruct((rows, width), low),
        jax.ShapeDtypeStruct((rows, width), low),
        *[jax.ShapeDtypeStruct(x.shape, wide) for x in (w_qkv, w_out, w_up, w_down)],
        jax.ShapeDtypeStruct((16, width), wide),
    ]
    vm = pltpu.VMEM
    four = [(nd, block, hid), (nd, block, part), (size, width), (block, width)]
    scratch = [
        vm((group, width), low),
        vm((group, width), low),
        vm((nd, 8, rows), jnp.int32),
        vm((nd, 16, width), low),
        vm((nz, 16, width), low),
        vm((2, 16, width), low),
        vm((nd, block, hid), low),
        vm((nd, block, part), low),
        *[vm((nf, *x), low) for x in four],
        vm((width, hid), low),
        vm((width, part), low),
        vm((third, width), low),
        vm((group, width), wide),
        vm((group, width), low),
        vm((group, width), low),
        vm((group, hid), low),
        vm((group, hid), low),
        vm((group, width), wide),
        vm((group, width), wide),
        vm((group, part), wide),
        vm((group, third), low),
        vm((group, third), low),
        vm((group, part), low),
        vm((16, width), wide),
        *[vm((2, nz, *x), low) for x in four],
        *[vm((nz, *x), low) for x in four],
        *[vm((nz, *x), low) for x in four],
        *[vm((nz, *x), low) for x in four],
        *[vm(x, wide) for x in four],
        vm((nd, block, hid), low),
        vm((nd, block, part), low),
        vm((nd, block, hid), low),
        vm((nd, block, part), low),
        vm((group, width), low),
        vm((group, width), low),
        vm((nd, rows, width), low),
        vm((nd, rows, width), low),
        vm((nd + nz, 16, width), low),
        vm((2, 16, width), low),
        pltpu.SemaphoreType.DMA((SENDS,)),
        pltpu.SemaphoreType.DMA((ARRIVALS,)),
    ]
    scale = 1.0 / math.sqrt(rows * nd * nf)
    spec = pl.BlockSpec(memory_space=pltpu.VMEM)
    return pl.pallas_call(
        functools.partial(layer_kernel, nd, nf, scale),
        out_shape=outs,
        in_specs=[spec] * len(inputs),
        out_specs=[spec] * len(outs),
        scratch_shapes=scratch,
        compiler_params=pltpu.CompilerParams(
            collective_id=0, has_side_effects=True, vmem_limit_bytes=60 << 20
        ),
    )(*inputs)


def per_device(
    tokens,
    cotangent,
    segments,
    w_qkv,
    w_out,
    w_up,
    w_down,
    vectors,
    first_qkv,
    first_out,
    first_up,
    first_down,
    first_vec,
    second_qkv,
    second_out,
    second_up,
    second_down,
    second_vec,
):
    device_count = lax.axis_size(("dp", "fsdp"))
    axes = ("dp", "fsdp")
    nd, nf = lax.axis_size("dp"), lax.axis_size("fsdp")
    direct = (
        nd > 1
        and nf % 2 == 0
        and nf > 2
        and HEADS % nd == 0
        and tokens.shape[0] == LANES
        and w_up.shape[1] == nd * D
        and (2 * D // nd) % LANES == 0
        and w_qkv.shape[0] % 8 == 0
        and w_down.shape[0] % 16 == 0
    )
    if direct:
        output, grad_tokens, grad_w_qkv, grad_w_out, grad_w_up, grad_w_down, whole = layer_step(
            tokens, cotangent, segments, w_qkv, w_out, w_up, w_down, vectors, nd, nf
        )
        rank = lax.axis_index("dp") * nf + lax.axis_index("fsdp")
        count = vectors.shape[0]
        grad_vectors = lax.dynamic_slice(whole.reshape(-1), (rank * count,), (count,))
    else:
        segment = segments[0]
        allowed = doc_mask(segment)
        cosine_part, sine_part = rotary_tables(segment)
        whole = [
            lax.all_gather(x.astype(jnp.bfloat16), axes, axis=0, tiled=True)
            for x in (w_qkv, w_out, w_up, w_down, vectors)
        ]
        output, saved = forward_pass(tokens, allowed, cosine_part, sine_part, *whole)
        grad_tokens, *local = backward_pass(
            saved, cotangent, allowed, cosine_part, sine_part, *whole
        )
        factor = 1.0 / math.sqrt(device_count * tokens.shape[0])
        grad_w_qkv, grad_w_out, grad_w_up, grad_w_down, grad_vectors = (
            factor * lax.psum_scatter(x, axes, scatter_dimension=0, tiled=True) for x in local
        )
    new_w_qkv, new_first_qkv, new_second_qkv = adam_update(
        w_qkv, grad_w_qkv, first_qkv, second_qkv, rate_matrix, decay_matrix
    )
    new_w_out, new_first_out, new_second_out = adam_update(
        w_out, grad_w_out, first_out, second_out, rate_matrix, decay_matrix
    )
    new_w_up, new_first_up, new_second_up = adam_update(
        w_up, grad_w_up, first_up, second_up, rate_matrix, decay_matrix
    )
    new_w_down, new_first_down, new_second_down = adam_update(
        w_down, grad_w_down, first_down, second_down, rate_matrix, decay_matrix
    )
    new_vectors, new_first_vec, new_second_vec = adam_update(
        vectors, grad_vectors, first_vec, second_vec, rate_vector, 0.0
    )
    return (
        output,
        grad_tokens,
        grad_w_qkv,
        grad_w_out,
        grad_w_up,
        grad_w_down,
        grad_vectors,
        new_w_qkv,
        new_w_out,
        new_w_up,
        new_w_down,
        new_vectors,
        new_first_qkv,
        new_first_out,
        new_first_up,
        new_first_down,
        new_first_vec,
        new_second_qkv,
        new_second_out,
        new_second_up,
        new_second_down,
        new_second_vec,
    )


def solution(mesh):
    placed = (
        P(("dp", "fsdp"), None),
        P(("dp", "fsdp"), None),
        P(("dp", "fsdp"), None),
        P(("dp", "fsdp"), None),
        P(("dp", "fsdp"), None),
        P(("dp", "fsdp"), None),
        P(("dp", "fsdp"), None),
        P(("dp", "fsdp")),
        P(("dp", "fsdp"), None),
        P(("dp", "fsdp"), None),
        P(("dp", "fsdp"), None),
        P(("dp", "fsdp"), None),
        P(("dp", "fsdp")),
        P(("dp", "fsdp"), None),
        P(("dp", "fsdp"), None),
        P(("dp", "fsdp"), None),
        P(("dp", "fsdp"), None),
        P(("dp", "fsdp")),
    )
    return jax.shard_map(
        per_device,
        mesh=mesh,
        in_specs=placed,
        out_specs=(
            P(("dp", "fsdp"), None),
            P(("dp", "fsdp"), None),
            P(("dp", "fsdp"), None),
            P(("dp", "fsdp"), None),
            P(("dp", "fsdp"), None),
            P(("dp", "fsdp"), None),
            P(("dp", "fsdp")),
            P(("dp", "fsdp"), None),
            P(("dp", "fsdp"), None),
            P(("dp", "fsdp"), None),
            P(("dp", "fsdp"), None),
            P(("dp", "fsdp")),
            P(("dp", "fsdp"), None),
            P(("dp", "fsdp"), None),
            P(("dp", "fsdp"), None),
            P(("dp", "fsdp"), None),
            P(("dp", "fsdp")),
            P(("dp", "fsdp"), None),
            P(("dp", "fsdp"), None),
            P(("dp", "fsdp"), None),
            P(("dp", "fsdp"), None),
            P(("dp", "fsdp")),
        ),
        check_vma=False,
    )
```

```python
import functools
import math

import jax
import jax.numpy as jnp
import ml_dtypes
import numpy as np
from jax import lax
from jax.experimental import pallas as pl
from jax.experimental.pallas import tpu as pltpu
from jax.sharding import PartitionSpec as P

D = 768
HEADS = 12
HEAD_DIM = 64
ROT = 16
STEP = 3


eps_norm = 1e-05
beta_first = 0.9
beta_second = 0.95
adam_epsilon = 1e-08
rate_matrix = 0.008
rate_vector = 0.1
decay_matrix = 0.01
rotary_base = 10000.0
mask_fill = -1e30


def layer_norm(inputs, gain_row, offset):
    center = inputs - jnp.mean(inputs, axis=-1, keepdims=True)
    inv_sigma = lax.rsqrt(jnp.mean(center * center, axis=-1, keepdims=True) + eps_norm)
    normed = center * inv_sigma
    return (normed, inv_sigma, normed * gain_row + offset)


def layer_norm_back(grad_norm, normed, inv_sigma, gain_row):
    scaled = grad_norm * gain_row
    return inv_sigma * (
        scaled
        - jnp.mean(scaled, axis=-1, keepdims=True)
        - normed * jnp.mean(scaled * normed, axis=-1, keepdims=True)
    )


def gelu_value(inputs):
    return 0.5 * inputs * (1.0 + jax.scipy.special.erf(inputs * (1.0 / math.sqrt(2.0))))


def gelu_slope(inputs):
    cumulative = 0.5 * (1.0 + jax.scipy.special.erf(inputs * (1.0 / math.sqrt(2.0))))
    return cumulative + inputs * jnp.exp(-0.5 * inputs * inputs) * (1.0 / math.sqrt(2.0 * math.pi))


def rotary_tables(segment):
    rows_here = segment.shape[0]
    earlier = jnp.sum((segment[None, :] < segment[:, None]).astype(jnp.int32), axis=1)
    position = jnp.arange(rows_here, dtype=jnp.int32) - earlier
    half_rot = ROT // 2
    inverse = rotary_base ** (-2.0 * jnp.arange(half_rot, dtype=jnp.float32) / ROT)
    angles = position.astype(jnp.float32)[:, None] * inverse[None, :]
    return (jnp.cos(angles)[:, None, :], jnp.sin(angles)[:, None, :])


def rotate(tensor, cosine_part, sine_part):
    half_rot = ROT // 2
    front_part = tensor[..., :half_rot]
    middle = tensor[..., half_rot:ROT]
    remain = tensor[..., ROT:]
    return jnp.concatenate(
        [
            front_part * cosine_part - middle * sine_part,
            middle * cosine_part + front_part * sine_part,
            remain,
        ],
        axis=-1,
    )


def rotate_back(tensor, cosine_part, sine_part):
    half_rot = ROT // 2
    front_part = tensor[..., :half_rot]
    middle = tensor[..., half_rot:ROT]
    remain = tensor[..., ROT:]
    return jnp.concatenate(
        [
            front_part * cosine_part + middle * sine_part,
            middle * cosine_part - front_part * sine_part,
            remain,
        ],
        axis=-1,
    )


def doc_mask(segment):
    row_index = jnp.arange(segment.shape[0], dtype=jnp.int32)
    return (segment[:, None] == segment[None, :]) & (row_index[None, :] <= row_index[:, None])


def masked_scores(queries, key_rot, allowed):
    scores = jnp.einsum("qhd,khd->hqk", queries, key_rot, preferred_element_type=jnp.float32) * (
        1.0 / math.sqrt(HEAD_DIM)
    )
    return jnp.where(allowed[None, :, :], scores, mask_fill)


def forward_pass(
    tokens, allowed, cosine_part, sine_part, full_qkv, full_out, full_up, full_down, full_vec
):
    rows_here = tokens.shape[0]
    vec_table = full_vec.astype(jnp.float32).reshape(13, D)
    inputs = tokens.astype(jnp.float32)
    normed_one, sigma_one, hidden_one = layer_norm(inputs, vec_table[0], vec_table[1])
    normed_two, sigma_two, hidden_two = layer_norm(inputs, vec_table[2], vec_table[3])
    hidden_one = hidden_one.astype(jnp.bfloat16)
    hidden_two = hidden_two.astype(jnp.bfloat16)
    projected = jnp.dot(hidden_one, full_qkv, preferred_element_type=jnp.float32) + vec_table[
        4:7
    ].reshape(-1)
    queries = rotate(
        projected[:, :D].reshape(rows_here, HEADS, HEAD_DIM), cosine_part, sine_part
    ).astype(jnp.bfloat16)
    key_rot = rotate(
        projected[:, D : 2 * D].reshape(rows_here, HEADS, HEAD_DIM), cosine_part, sine_part
    ).astype(jnp.bfloat16)
    values = projected[:, 2 * D :].reshape(rows_here, HEADS, HEAD_DIM).astype(jnp.bfloat16)
    scores = masked_scores(queries, key_rot, allowed)
    top_score = jnp.max(scores, axis=-1, keepdims=True)
    log_total = top_score + jnp.log(jnp.sum(jnp.exp(scores - top_score), axis=-1, keepdims=True))
    soft_weights = jnp.exp(scores - log_total).astype(jnp.bfloat16)
    context = (
        jnp.einsum("hqk,khd->qhd", soft_weights, values, preferred_element_type=jnp.float32)
        .reshape(rows_here, D)
        .astype(jnp.bfloat16)
    )
    attended = jnp.dot(context, full_out, preferred_element_type=jnp.float32) + vec_table[7]
    up_proj = jnp.dot(hidden_two, full_up, preferred_element_type=jnp.float32) + vec_table[
        8:12
    ].reshape(-1)
    activated = gelu_value(up_proj).astype(jnp.bfloat16)
    feed_out = jnp.dot(activated, full_down, preferred_element_type=jnp.float32) + vec_table[12]
    output = (inputs + attended + feed_out).astype(jnp.bfloat16)
    saved = (
        normed_one,
        sigma_one,
        hidden_one,
        normed_two,
        sigma_two,
        hidden_two,
        queries,
        key_rot,
        values,
        log_total,
        context,
        up_proj,
        activated,
    )
    return (output, saved)


def backward_pass(
    saved,
    cotangent,
    allowed,
    cosine_part,
    sine_part,
    back_qkv,
    back_out,
    back_up,
    back_down,
    back_vec,
):
    (
        normed_one,
        sigma_one,
        hidden_one,
        normed_two,
        sigma_two,
        hidden_two,
        queries,
        key_rot,
        values,
        log_total,
        context,
        up_proj,
        activated,
    ) = saved
    rows_here = cotangent.shape[0]
    vec_table = back_vec.astype(jnp.float32).reshape(13, D)
    grad_out = cotangent.astype(jnp.float32)
    grad_w_down = jnp.dot(activated.T, cotangent, preferred_element_type=jnp.float32)
    grad_act = jnp.dot(cotangent, back_down.T, preferred_element_type=jnp.float32)
    grad_up = grad_act * gelu_slope(up_proj)
    grad_up_low = grad_up.astype(jnp.bfloat16)
    grad_w_up = jnp.dot(hidden_two.T, grad_up_low, preferred_element_type=jnp.float32)
    grad_hidden_two = jnp.dot(grad_up_low, back_up.T, preferred_element_type=jnp.float32)
    grad_w_out = jnp.dot(context.T, cotangent, preferred_element_type=jnp.float32)
    grad_context = (
        jnp.dot(cotangent, back_out.T, preferred_element_type=jnp.float32)
        .astype(jnp.bfloat16)
        .reshape(rows_here, HEADS, HEAD_DIM)
    )
    again_scores = masked_scores(queries, key_rot, allowed)
    probs_full = jnp.exp(again_scores - log_total)
    probs_low = probs_full.astype(jnp.bfloat16)
    grad_probs = jnp.einsum(
        "qhd,khd->hqk", grad_context, values, preferred_element_type=jnp.float32
    )
    row_inner = jnp.sum(probs_full * grad_probs, axis=-1, keepdims=True)
    grad_scores = (probs_full * (grad_probs - row_inner) * (1.0 / math.sqrt(HEAD_DIM))).astype(
        jnp.bfloat16
    )
    grad_queries = jnp.einsum(
        "hqk,khd->qhd", grad_scores, key_rot, preferred_element_type=jnp.float32
    )
    grad_keys = jnp.einsum("hqk,qhd->khd", grad_scores, queries, preferred_element_type=jnp.float32)
    grad_values = jnp.einsum(
        "hqk,qhd->khd", probs_low, grad_context, preferred_element_type=jnp.float32
    )
    grad_projected = jnp.concatenate(
        [
            rotate_back(grad_queries, cosine_part, sine_part).reshape(rows_here, D),
            rotate_back(grad_keys, cosine_part, sine_part).reshape(rows_here, D),
            grad_values.reshape(rows_here, D),
        ],
        axis=1,
    )
    grad_proj_low = grad_projected.astype(jnp.bfloat16)
    grad_w_qkv = jnp.dot(hidden_one.T, grad_proj_low, preferred_element_type=jnp.float32)
    grad_hidden_one = jnp.dot(grad_proj_low, back_qkv.T, preferred_element_type=jnp.float32)
    grad_table = jnp.concatenate(
        [
            jnp.sum(grad_hidden_one * normed_one, axis=0)[None],
            jnp.sum(grad_hidden_one, axis=0)[None],
            jnp.sum(grad_hidden_two * normed_two, axis=0)[None],
            jnp.sum(grad_hidden_two, axis=0)[None],
            jnp.sum(grad_projected, axis=0).reshape(3, D),
            jnp.sum(grad_out, axis=0)[None],
            jnp.sum(grad_up, axis=0).reshape(4, D),
            jnp.sum(grad_out, axis=0)[None],
        ],
        axis=0,
    )
    grad_tokens = (
        grad_out
        + layer_norm_back(grad_hidden_one, normed_one, sigma_one, vec_table[0])
        + layer_norm_back(grad_hidden_two, normed_two, sigma_two, vec_table[2])
    ).astype(jnp.bfloat16)
    grad_table = lax.optimization_barrier(grad_table)
    return (grad_tokens, grad_w_qkv, grad_w_out, grad_w_up, grad_w_down, grad_table.reshape(-1))


def adam_update(weight, gradient, moment_one, moment_two, rate_value, decay_value):
    new_one = beta_first * moment_one + (1.0 - beta_first) * gradient
    new_two = beta_second * moment_two + (1.0 - beta_second) * gradient * gradient
    corrected_one = new_one * (1.0 / (1.0 - beta_first**STEP))
    corrected_two = new_two * (1.0 / (1.0 - beta_second**STEP))
    new_weight = weight - rate_value * (
        corrected_one / (jnp.sqrt(corrected_two) + adam_epsilon) + decay_value * weight
    )
    return (new_weight, new_one, new_two)


MESH = pl.DeviceIdType.MESH
LANES = 128


def mm(left, right):
    return lax.dot_general(left, right, (((1,), (0,)), ((), ())), preferred_element_type=jnp.float32)


def mm_nt(left, right):
    return lax.dot_general(left, right, (((1,), (1,)), ((), ())), preferred_element_type=jnp.float32)


def mm_tn(left, right):
    return lax.dot_general(left, right, (((0,), (0,)), ((), ())), preferred_element_type=jnp.float32)


def rotary_constants(rows):
    half_rot = ROT // 2
    lane = np.arange(LANES) % HEAD_DIM
    inverse = np.float32(rotary_base) ** (-2.0 * np.arange(half_rot, dtype=np.float32) / ROT)
    angles = np.arange(rows, dtype=np.float32)[:, None] * inverse.astype(np.float32)[lane % half_rot]
    cosine = np.where(lane < ROT, np.cos(angles), 1.0).astype(np.float32)
    sine = np.where(lane < ROT, np.sin(angles), 0.0).astype(np.float32)
    both = np.concatenate([cosine, sine], axis=1)
    high = both.astype(ml_dtypes.bfloat16)
    low = (both - high.astype(np.float32)).astype(ml_dtypes.bfloat16)
    swap = np.zeros((LANES, LANES), np.float32)
    for j in range(LANES):
        if lane[j] < half_rot:
            swap[j + half_rot, j] = -1.0
        elif lane[j] < ROT:
            swap[j - half_rot, j] = 1.0
    return np.concatenate([high, low], axis=1), swap.astype(ml_dtypes.bfloat16)


def swapped(value, swap):
    high = value.astype(jnp.bfloat16)
    low = (value - high.astype(jnp.float32)).astype(jnp.bfloat16)
    return mm(high, swap) + mm(low, swap)


def normalize(value):
    center = value - jnp.mean(value, axis=-1, keepdims=True)
    inv_sigma = lax.rsqrt(jnp.mean(center * center, axis=-1, keepdims=True) + eps_norm)
    return center * inv_sigma, inv_sigma


SENDS, ARRIVALS = 160, 160


def layer_kernel(nd, nf, scale, *refs):
    (tok, cot, seg, wq_far, wo_far, wu_far, wd_far, vecs, trig, swap) = refs[:10]
    (out, gtok, gq, go, gu, gd, gv) = refs[10:17]
    (xs, ys, sg, vd, vz, vp, upS, qS, g_up, g_q, g_down, g_out, w_up, w_q, w_o) = refs[17:32]
    (norm, h1, h2, act, du, outp, ep, proj, ctx, dctx, dp_low, table) = refs[32:44]
    m_up, m_q, m_down, m_out = refs[44:48]
    p_up, p_q, p_down, p_out = refs[48:52]
    r_up, r_q, r_down, r_out = refs[52:56]
    l_up, l_q, l_down, l_out = refs[56:60]
    a_up, a_q, a_down, a_out = refs[60:64]
    (b_up, b_q, f_up, f_q, o_send, e_send, o_recv, e_recv, tz, tp) = refs[64:74]
    wq, wo, wu, wd, vtab = refs[74:79]
    sent, came, near = refs[79:]
    nz = nf // 2
    rows, width = tok.shape
    low = jnp.bfloat16
    wide = jnp.float32
    d, f = lax.axis_index("dp"), lax.axis_index("fsdp")
    z, c = lax.div(f, 2), lax.rem(f, 2)
    loads = [
        pltpu.make_async_copy(far, close, near.at[i])
        for i, (far, close) in enumerate(
            ((wd_far, wd), (wo_far, wo), (wu_far, wu), (wq_far, wq))
        )
    ]
    for load in loads:
        load.start()
    part = wq.shape[1] // nd
    third = part // 3
    hid = wu.shape[1] // nd
    block = wq.shape[0]

    state = {"sent": 0, "came": 0}
    pend = []

    def grab(count):
        at = state["came"]
        state["came"] += count
        assert state["came"] <= ARRIVALS
        return at

    def send(source, target, arrival, peer, cond=None):
        slot = state["sent"]
        state["sent"] += 1
        assert slot < SENDS

        copy = pltpu.make_async_remote_copy(
            src_ref=source(),
            dst_ref=target(),
            send_sem=sent.at[slot],
            recv_sem=came.at[arrival],
            device_id=peer,
            device_id_type=MESH,
        )
        pend.append((cond, copy))
        if cond is None:
            copy.start()
        else:
            pl.when(cond)(lambda: copy.start())

    def landed(ref, arrival):
        pltpu.make_async_copy(ref, ref, came.at[arrival]).wait()

    def mate(k):
        return (lax.rem(d + k, nd), f)

    def origin(k):
        return lax.rem(d + nd - k, nd)

    pair = (d, z * 2 + 1 - c)
    right, left = (d, (z + 1) * 2 + c), (d, (z - 1) * 2 + c)
    level = lambda k: (d, lax.rem(z + k, nz) * 2 + c)

    def span(index, size):
        return pl.ds(pl.multiple_of(index * size, size), size)

    barrier = pltpu.get_barrier_semaphore()
    peers = [mate(k) for k in range(1, nd)] + [level(k) for k in range(1, nz)] + [pair]
    for peer in peers:
        pl.semaphore_signal(barrier, inc=1, device_id=peer, device_id_type=MESH)
    count = vecs.shape[0]
    first_at = (d * nf + f) * count
    row = lax.div(first_at, width)
    shift = first_at - row * width
    row_of = lax.broadcasted_iota(jnp.int32, (16, width), 0)
    lane_of = lax.broadcasted_iota(jnp.int32, (16, width), 1)
    wraps = lane_of < shift
    own_row = row_of == row + jnp.where(wraps, 1, 0)
    inside = lane_of - shift + jnp.where(wraps, width, 0) < count
    line = jnp.concatenate([vecs[...].reshape(1, count), jnp.zeros((1, width - count), wide)], axis=1)
    line = pltpu.roll(jnp.broadcast_to(line, (16, width)), shift, 1)
    vtab[...] = jnp.where(jnp.logical_and(own_row, inside), line, 0.0).astype(low)
    vd[d] = vtab[...]
    sg[d] = jnp.broadcast_to(seg[...], (8, rows))
    for load in loads[:2]:
        load.wait()
    g_down[f] = wd[...].astype(low)
    g_out[f] = wo[...].astype(low)
    pl.semaphore_wait(barrier, len(peers))

    gathered = [g_down, g_out, g_up, g_q]
    wire = [grab(nz) for _ in gathered]
    cross = [grab(nz) for _ in gathered]

    def own(p):
        buf = gathered[p]
        here = lambda: buf.at[f]
        send(here, here, wire[p] + z, right, z < nz - 1)
        send(here, here, wire[p] + z, left, z > 0)
        send(here, here, cross[p] + z, pair)

    own(0)
    own(1)
    for load in loads[2:]:
        load.wait()
    for j in range(nd):
        upS[j] = wu[:, j * hid : (j + 1) * hid].astype(low)
        qS[j] = jnp.concatenate(
            [
                wq[:, t * width + j * third : t * width + (j + 1) * third]
                for t in range(3)
            ],
            axis=1,
        ).astype(low)
    mates = range(1, nd)
    up_in, q_in = grab(nd), grab(nd)
    x_in, y_in, s_in, v_in = grab(nd), grab(nd), grab(nd), grab(nd)
    for k in mates:
        to = lax.rem(d + k, nd)
        send(lambda: upS.at[to], lambda: g_up.at[f, d], up_in + k, mate(k))
        send(lambda: qS.at[to], lambda: g_q.at[f, d], q_in + k, mate(k))
        send(lambda: vtab, lambda: vd.at[d], v_in + k, mate(k))
        send(lambda: sg.at[d], lambda: sg.at[d], s_in + k, mate(k))
    for k in mates:
        send(lambda: tok, lambda: xs.at[span(d, rows)], x_in + k, mate(k))
        send(lambda: cot, lambda: ys.at[span(d, rows)], y_in + k, mate(k))
    g_up[f, d] = upS[d]
    g_q[f, d] = qS[d]
    keep = [
        pltpu.make_async_copy(tok, xs.at[span(d, rows)], near.at[4]),
        pltpu.make_async_copy(cot, ys.at[span(d, rows)], near.at[5]),
    ]
    for copy in keep:
        copy.start()
    for k in mates:
        landed(g_up.at[f, origin(k)], up_in + k)
    own(2)
    for k in mates:
        landed(g_q.at[f, origin(k)], q_in + k)
    own(3)

    vz_in, vp_in = grab(nz), grab(1)
    for k in mates:
        landed(vd.at[origin(k)], v_in + k)
    vz[z] = sum(vd[j].astype(wide) for j in range(nd)).astype(low)
    for k in range(1, nz):
        send(lambda: vz.at[z], lambda: vz.at[z], vz_in + k, level(k))

    def relay(p, hop):
        buf = gathered[p]
        for origin_z, cond, onward, more in (
            (z - hop, z >= hop, right, z < nz - 1),
            (z + hop, z + hop < nz, left, z > 0),
        ):
            piece = functools.partial(lambda o: buf.at[o * 2 + c], origin_z)
            pl.when(cond)(functools.partial(lambda pc, o: landed(pc(), wire[p] + o), piece, origin_z))
            send(piece, piece, wire[p] + origin_z, onward, jnp.logical_and(cond, more))
            send(piece, piece, cross[p] + origin_z, pair, cond)

    for hop in range(1, nz):
        for p in range(4):
            relay(p, hop)
        if hop == 1:
            for k in range(1, nz):
                landed(vz.at[lax.rem(z + nz - k, nz)], vz_in + k)
            vp[c] = sum(vz[j].astype(wide) for j in range(nz)).astype(low)
            send(lambda: vp.at[c], lambda: vp.at[c], vp_in, pair)
            landed(vp.at[1 - c], vp_in)
    vec = vp[0].astype(wide) + vp[1].astype(wide)

    for copy in keep:
        copy.wait()
    for k in mates:
        landed(xs.at[span(origin(k), rows)], x_in + k)
        landed(ys.at[span(origin(k), rows)], y_in + k)
        landed(sg.at[origin(k)], s_in + k)
    for b in range(nd):
        at = slice(b * rows, (b + 1) * rows)
        value, _ = normalize(xs[at, :].astype(wide))
        norm[at, :] = value
        h1[at, :] = (value * vec[0:1] + vec[1:2]).astype(low)
        h2[at, :] = (value * vec[2:3] + vec[3:4]).astype(low)

    def mine_of(pieces):
        return sum(jnp.where(d == j, pieces[j], 0.0) for j in range(nd))

    for p in (0, 2):
        for o in range(nz):
            landed(gathered[p].at[2 * o + 1 - c], cross[p] + o)
    def unblock(source, target):
        for j in range(nd):
            for o in range(nz):
                value = jnp.concatenate(
                    [source[2 * o, j].astype(wide), source[2 * o + 1, j].astype(wide)], axis=0
                )
                start = (j * nf + 2 * o) * block
                target[start : start + 2 * block, :] = value.astype(low)

    unblock(g_up, w_up)
    w_down = g_down[...].reshape(hid, width)
    cu = mine_of([vec[8 + j : 9 + j] for j in range(nd)])
    cut = 256
    du_sums = []
    for n in range(hid // cut):
        cols = slice(n * cut, (n + 1) * cut)
        u = mm(h2[...], w_up[:, cols]) + cu[:, cols]
        da = mm_nt(ys[...], w_down[cols, :])
        phi = 0.5 * (1.0 + lax.erf(u * (1.0 / math.sqrt(2.0))))
        act[:, cols] = (u * phi).astype(low)
        value = da * (phi + u * jnp.exp(-0.5 * u * u) * (1.0 / math.sqrt(2.0 * math.pi)))
        du_sums.append(jnp.sum(value, axis=0, keepdims=True))
        du[:, cols] = value.astype(low)
    du_sum = jnp.concatenate(du_sums, axis=1)
    value = mm_tn(act[...], ys[...])
    size = wd.shape[0]
    for i in range(nf):
        m_down[i % 2, i // 2] = value[i * size : (i + 1) * size].astype(low)
    value = mm_tn(h2[...], du[...])
    for j in range(nd):
        for i in range(nf):
            start = (j * nf + i) * block
            m_up[i % 2, i // 2, j] = value[start : start + block].astype(low)

    sums = [m_down, m_up, m_q, m_out]
    paired = [p_down, p_up, p_q, p_out]
    rights = [r_down, r_up, r_q, r_out]
    lefts = [l_down, l_up, l_q, l_out]
    totals = [a_down, a_up, a_q, a_out]
    pair_in = [grab(1) for _ in sums]
    right_in = [grab(nz) for _ in sums]
    left_in = [grab(nz) for _ in sums]

    def share(p):
        send(lambda: sums[p].at[1 - c], lambda: paired[p].at[...], pair_in[p], pair)

    def first(p):
        landed(paired[p], pair_in[p])
        for k in range(nz - 1, 0, -1):
            for target, bound, inbox, sem, peer in (
                (z + k, z == 0, rights[p], right_in[p], right),
                (z - k, z == nz - 1, lefts[p], left_in[p], left),
            ):

                def add(target=target):
                    sums[p][c, target] = (
                        sums[p][c, target].astype(wide) + paired[p][target].astype(wide)
                    ).astype(low)

                pl.when(bound)(add)
                send(
                    functools.partial(lambda t: sums[p].at[c, t], target),
                    functools.partial(lambda box, t: box.at[t], inbox, target),
                    sem + target,
                    peer,
                    bound,
                )

    def middle(p, k):
        for target, bound, inbox, sem, peer in (
            (z + k, jnp.logical_and(z > 0, z + k < nz), rights[p], right_in[p], right),
            (z - k, jnp.logical_and(z < nz - 1, z >= k), lefts[p], left_in[p], left),
        ):

            def add(target=target, inbox=inbox, sem=sem):
                landed(inbox.at[target], sem + target)
                sums[p][c, target] = (
                    sums[p][c, target].astype(wide)
                    + paired[p][target].astype(wide)
                    + inbox[target].astype(wide)
                ).astype(low)

            pl.when(bound)(add)
            send(
                functools.partial(lambda t: sums[p].at[c, t], target),
                functools.partial(lambda box, t: box.at[t], inbox, target),
                sem + target,
                peer,
                bound,
            )

    def last(p):
        totals[p][...] = sums[p][c, z].astype(wide) + paired[p][z].astype(wide)
        for bound, inbox, sem in ((z > 0, rights[p], right_in[p]), (z < nz - 1, lefts[p], left_in[p])):

            def add(inbox=inbox, sem=sem):
                landed(inbox.at[z], sem + z)
                totals[p][...] = totals[p][...] + inbox[z].astype(wide)

            pl.when(bound)(add)

    share(0)
    share(1)
    outp[...] = mm(act[...], w_down)
    dh = mm_nt(du[...], w_up[...])
    ep[...] = dh * vec[2:3]
    table[...] = jnp.zeros_like(table)
    table[2:3, :] = jnp.sum(dh * norm[...], axis=0, keepdims=True)
    table[3:4, :] = jnp.sum(dh, axis=0, keepdims=True)
    dy_sum = jnp.sum(ys[span(d, rows), :].astype(wide), axis=0, keepdims=True)
    table[7:8, :] = dy_sum
    table[12:13, :] = dy_sum
    for j in range(nd):
        table[8 + j : 9 + j, :] = jnp.where(d == j, du_sum, 0.0)
    first(0)
    first(1)

    for p in (1, 3):
        for o in range(nz):
            landed(gathered[p].at[2 * o + 1 - c], cross[p] + o)
    unblock(g_q, w_q)
    for o in range(nz):
        value = jnp.concatenate([g_out[2 * o].astype(wide), g_out[2 * o + 1].astype(wide)], axis=0)
        w_o[2 * o * block : 2 * (o + 1) * block, :] = value.astype(low)
    cq = jnp.concatenate(
        [
            mine_of([vec[4 + t : 5 + t, j * third : (j + 1) * third] for j in range(nd)])
            for t in range(3)
        ],
        axis=1,
    )
    proj[...] = mm(h1[...], w_q[...]) + cq
    dctx[...] = mm_nt(ys[...], w_o[...]).astype(low)
    row_at = lax.broadcasted_iota(jnp.int32, (rows, rows), 0)
    col_at = lax.broadcasted_iota(jnp.int32, (rows, rows), 1)
    causal = col_at <= row_at
    sharp = 1.0 / math.sqrt(HEAD_DIM)

    def attend(b, dp_sum):
        at = span(b, rows)
        name = jnp.broadcast_to(sg[b][0:1, :].astype(wide), (rows, rows))
        allowed = jnp.logical_and(name == name.T, causal)
        pos = jnp.sum(jnp.where(allowed, 1.0, 0.0), axis=1, keepdims=True) - 1.0
        hot = jnp.where(col_at.astype(wide) == pos, 1.0, 0.0).astype(low)
        tables = mm(hot, trig[...])
        tables = tables[:, : 2 * LANES] + tables[:, 2 * LANES :]
        cosine, sine = tables[:, :LANES], tables[:, LANES:]
        base = proj[at, :]
        turned = []
        for t in range(2 * third // LANES):
            x = base[:, t * LANES : (t + 1) * LANES]
            turned.append((x * cosine + swapped(x, swap[...]) * sine).astype(low))
        turned = jnp.concatenate(turned, axis=1)
        values = base[:, 2 * third :].astype(low)
        grad_c = dctx[at, :]
        dqs, dks, dvs, contexts = [], [], [], []
        for h in range(third // HEAD_DIM):
            hs = slice(h * HEAD_DIM, (h + 1) * HEAD_DIM)
            q, k = turned[:, hs], turned[:, third + h * HEAD_DIM : third + (h + 1) * HEAD_DIM]
            v, dc = values[:, hs], grad_c[:, hs]
            s = jnp.where(allowed, mm_nt(q, k) * sharp, mask_fill)
            e = jnp.exp(s - jnp.max(s, axis=-1, keepdims=True))
            a = e / jnp.sum(e, axis=-1, keepdims=True)
            a_low = a.astype(low)
            contexts.append(mm(a_low, v))
            da = mm_nt(dc, v)
            inner = jnp.sum(a * da, axis=-1, keepdims=True)
            ds = (a * (da - inner) * sharp).astype(low)
            dqs.append(mm(ds, k))
            dks.append(mm_tn(ds, q))
            dvs.append(mm_tn(a_low, dc))
        ctx[at, :] = jnp.concatenate(contexts, axis=1).astype(low)
        turned = jnp.concatenate(dqs + dks, axis=1)
        grads = []
        for t in range(2 * third // LANES):
            x = turned[:, t * LANES : (t + 1) * LANES]
            grads.append(x * cosine - swapped(x, swap[...]) * sine)
        grads = jnp.concatenate(grads + dvs, axis=1)
        dp_low[at, :] = grads.astype(low)
        return dp_sum + jnp.sum(grads, axis=0, keepdims=True)

    dp_sum = lax.fori_loop(0, nd, attend, jnp.zeros((1, part), wide))
    for t in range(3):
        piece = dp_sum[:, t * third : (t + 1) * third]
        table[4 + t : 5 + t, :] = jnp.concatenate(
            [jnp.where(d == j, piece, 0.0) for j in range(nd)], axis=1
        )
    value = mm_tn(h1[...], dp_low[...])
    for j in range(nd):
        for i in range(nf):
            start = (j * nf + i) * block
            m_q[i % 2, i // 2, j] = value[start : start + block].astype(low)
    value = mm_tn(ctx[...], ys[...])
    for i in range(nf):
        m_out[i % 2, i // 2] = value[i * block : (i + 1) * block].astype(low)
    share(2)
    share(3)
    outp[...] += mm(ctx[...], w_o[...])
    dh = mm_nt(dp_low[...], w_q[...])
    ep[...] += dh * vec[0:1]
    table[0:1, :] = jnp.sum(dh * norm[...], axis=0, keepdims=True)
    table[1:2, :] = jnp.sum(dh, axis=0, keepdims=True)
    o_in, e_in, t_in = grab(nd), grab(nd), grab(nd)
    o_send[...] = outp[...].astype(low)
    e_send[...] = ep[...].astype(low)
    vd_in = vd
    tz_in, tp_in = grab(nz), grab(1)
    first(2)
    first(3)
    tz[0] = table[...].astype(low)
    for k in mates:
        to = lax.rem(d + k, nd)
        send(lambda: tz.at[0], lambda: tz.at[k], t_in + k, mate(k))
    for k in mates:
        to = lax.rem(d + k, nd)
        send(lambda: o_send.at[span(to, rows)], lambda: o_recv.at[k], o_in + k, mate(k))
        send(lambda: e_send.at[span(to, rows)], lambda: e_recv.at[k], e_in + k, mate(k))
    for p in range(4):
        for k in range(nz - 2, 0, -1):
            middle(p, k)
    for k in mates:
        landed(tz.at[k], t_in + k)
    tz[nd] = (table[...] + sum(tz[k].astype(wide) for k in mates)).astype(low)
    for k in range(1, nz):
        send(lambda: tz.at[nd], lambda: tz.at[nd + k], tz_in + k, level(k))
    fu_in, fq_in = grab(nd), grab(nd)
    for p, whole, box, arrivals in ((1, b_up, f_up, fu_in), (2, b_q, f_q, fq_in)):
        last(p)
        whole[...] = totals[p][...].astype(low)
        for k in mates:
            to = lax.rem(d + k, nd)
            send(
                functools.partial(lambda w, t: w.at[t], whole, to),
                functools.partial(lambda x: x.at[d], box),
                arrivals + k,
                mate(k),
            )
        box[d] = whole[d]
    for k in range(1, nz):
        landed(tz.at[nd + k], tz_in + k)
    tp[0] = sum(tz[nd + k].astype(wide) for k in range(nz)).astype(low)
    send(lambda: tp.at[0], lambda: tp.at[1], tp_in, pair)
    last(0)
    last(3)
    gd[...] = a_down[...] * scale
    go[...] = a_out[...] * scale
    for k in mates:
        landed(o_recv.at[k], o_in + k)
        landed(e_recv.at[k], e_in + k)
    total = xs[span(d, rows), :].astype(wide) + vec[7:8] + vec[12:13] + outp[span(d, rows), :]
    out[...] = (total + sum(o_recv[k].astype(wide) for k in mates)).astype(low)
    value, inv_sigma = normalize(xs[span(d, rows), :].astype(wide))
    e = ep[span(d, rows), :] + sum(e_recv[k].astype(wide) for k in mates)
    gtok[...] = (
        ys[span(d, rows), :].astype(wide)
        + inv_sigma
        * (
            e
            - jnp.mean(e, axis=-1, keepdims=True)
            - value * jnp.mean(e * value, axis=-1, keepdims=True)
        )
    ).astype(low)
    landed(tp.at[1], tp_in)
    whole = (tp[0].astype(wide) + tp[1].astype(wide)) * scale
    line = jnp.sum(jnp.where(own_row, whole, 0.0), axis=0, keepdims=True)
    line = pltpu.roll(jnp.broadcast_to(line, (8, width)), lax.rem(width - shift, width), 1)
    gv[...] = line[0:1, :count].reshape(count)
    for k in mates:
        landed(f_up.at[origin(k)], fu_in + k)
        landed(f_q.at[origin(k)], fq_in + k)
    for j in range(nd):
        gu[:, j * hid : (j + 1) * hid] = f_up[j].astype(wide) * scale
    gq[...] = scale * jnp.concatenate(
        [f_q[j].astype(wide)[:, t * third : (t + 1) * third] for t in range(3) for j in range(nd)],
        axis=1,
    )
    for cond, copy in pend:
        if cond is None:
            copy.wait_send()
        else:
            pl.when(cond)(functools.partial(lambda x: x.wait_send(), copy))


def layer_step(tokens, cotangent, segments, w_qkv, w_out, w_up, w_down, vectors, nd, nf):
    rows, width = tokens.shape
    low, wide = jnp.bfloat16, jnp.float32
    nz, block, size = nf // 2, w_qkv.shape[0], w_down.shape[0]
    part, hid = w_qkv.shape[1] // nd, w_up.shape[1] // nd
    third = part // 3
    group = nd * rows
    count = vectors.shape[0]
    trig, swap = rotary_constants(rows)
    inputs = (
        tokens,
        cotangent,
        segments,
        w_qkv,
        w_out,
        w_up,
        w_down,
        vectors,
        jnp.asarray(trig),
        jnp.asarray(swap),
    )
    outs = [
        jax.ShapeDtypeStruct((rows, width), low),
        jax.ShapeDtypeStruct((rows, width), low),
        *[jax.ShapeDtypeStruct(x.shape, wide) for x in (w_qkv, w_out, w_up, w_down)],
        jax.ShapeDtypeStruct((count,), wide),
    ]
    vm = pltpu.VMEM
    four = [(nd, block, hid), (nd, block, part), (size, width), (block, width)]
    scratch = [
        vm((group, width), low),
        vm((group, width), low),
        vm((nd, 8, rows), jnp.int32),
        vm((nd, 16, width), low),
        vm((nz, 16, width), low),
        vm((2, 16, width), low),
        vm((nd, block, hid), low),
        vm((nd, block, part), low),
        *[vm((nf, *x), low) for x in four],
        vm((width, hid), low),
        vm((width, part), low),
        vm((third, width), low),
        vm((group, width), wide),
        vm((group, width), low),
        vm((group, width), low),
        vm((group, hid), low),
        vm((group, hid), low),
        vm((group, width), wide),
        vm((group, width), wide),
        vm((group, part), wide),
        vm((group, third), low),
        vm((group, third), low),
        vm((group, part), low),
        vm((16, width), wide),
        *[vm((2, nz, *x), low) for x in four],
        *[vm((nz, *x), low) for x in four],
        *[vm((nz, *x), low) for x in four],
        *[vm((nz, *x), low) for x in four],
        *[vm(x, wide) for x in four],
        vm((nd, block, hid), low),
        vm((nd, block, part), low),
        vm((nd, block, hid), low),
        vm((nd, block, part), low),
        vm((group, width), low),
        vm((group, width), low),
        vm((nd, rows, width), low),
        vm((nd, rows, width), low),
        vm((nd + nz, 16, width), low),
        vm((2, 16, width), low),
        *[vm(x.shape, wide) for x in (w_qkv, w_out, w_up, w_down)],
        vm((16, width), low),
        pltpu.SemaphoreType.DMA((SENDS,)),
        pltpu.SemaphoreType.DMA((ARRIVALS,)),
        pltpu.SemaphoreType.DMA((6,)),
    ]
    scale = 1.0 / math.sqrt(rows * nd * nf)
    spec = pl.BlockSpec(memory_space=pltpu.VMEM)
    far = pl.BlockSpec(memory_space=pl.ANY)
    return pl.pallas_call(
        functools.partial(layer_kernel, nd, nf, scale),
        out_shape=outs,
        in_specs=[far, far, spec, far, far, far, far, spec, spec, spec],
        out_specs=[spec] * len(outs),
        scratch_shapes=scratch,
        compiler_params=pltpu.CompilerParams(
            collective_id=0, has_side_effects=True, vmem_limit_bytes=60 << 20
        ),
    )(*inputs)


def adam_kernel(count, *refs):
    far = [refs[i * count : (i + 1) * count] for i in range(4)]
    passed, refs = refs[4 * count : 4 * count + 2], refs[4 * count + 2 :]
    pass_outs, refs = refs[:2], refs[2:]
    outs = [refs[i * count : (i + 1) * count] for i in range(4)]
    refs = refs[4 * count :]
    near = [refs[i * count : (i + 1) * count] for i in range(4)]
    held = [refs[(4 + i) * count : (5 + i) * count] for i in range(3)]
    passing = refs[7 * count : 7 * count + 2]
    load_sems, sems = refs[7 * count + 2 :]
    loads = [
        [
            pltpu.make_async_copy(far[j][i], near[j][i], load_sems.at[i * 4 + j])
            for j in range(4)
        ]
        for i in range(count)
    ]
    carried = [
        pltpu.make_async_copy(source, close, load_sems.at[4 * count + i])
        for i, (source, close) in enumerate(zip(passed, passing))
    ]
    for group in [carried] + loads:
        for copy in group:
            copy.start()
    copies = []

    def write(source, target):
        copies.append(pltpu.make_async_copy(source, target, sems.at[len(copies)]))
        copies[-1].start()

    for copy, close, target in zip(carried, passing, pass_outs):
        copy.wait()
        write(close, target)
    for i in range(count):
        for copy in loads[i]:
            copy.wait()
        write(near[0][i], outs[0][i])
        vector = i == count - 1
        results = adam_update(
            near[1][i][...],
            near[0][i][...],
            near[2][i][...],
            near[3][i][...],
            rate_vector if vector else rate_matrix,
            0.0 if vector else decay_matrix,
        )
        for j in range(3):
            held[j][i][...] = results[j]
            write(held[j][i], outs[j + 1][i])
    for copy in copies:
        copy.wait()


def adam_all(grads, weights, firsts, seconds, passed):
    count = len(grads)
    shapes = [jax.ShapeDtypeStruct(x.shape, x.dtype) for x in weights]
    given = [jax.ShapeDtypeStruct(x.shape, x.dtype) for x in passed]
    total = 4 * count + len(passed)
    return pl.pallas_call(
        functools.partial(adam_kernel, count),
        out_shape=given + shapes * 4,
        in_specs=[pl.BlockSpec(memory_space=pl.ANY)] * total,
        out_specs=[pl.BlockSpec(memory_space=pl.ANY)] * total,
        scratch_shapes=[pltpu.VMEM(x.shape, x.dtype) for x in shapes * 7 + given]
        + [pltpu.SemaphoreType.DMA((total,)), pltpu.SemaphoreType.DMA((total,))],
        compiler_params=pltpu.CompilerParams(vmem_limit_bytes=60 << 20),
    )(*grads, *weights, *firsts, *seconds, *passed)


def per_device(
    tokens,
    cotangent,
    segments,
    w_qkv,
    w_out,
    w_up,
    w_down,
    vectors,
    first_qkv,
    first_out,
    first_up,
    first_down,
    first_vec,
    second_qkv,
    second_out,
    second_up,
    second_down,
    second_vec,
):
    device_count = lax.axis_size(("dp", "fsdp"))
    axes = ("dp", "fsdp")
    nd, nf = lax.axis_size("dp"), lax.axis_size("fsdp")
    direct = (
        nd > 1
        and nf % 2 == 0
        and nf > 2
        and HEADS % nd == 0
        and tokens.shape[0] == LANES
        and w_up.shape[1] == nd * D
        and (2 * D // nd) % LANES == 0
        and w_qkv.shape[0] % 8 == 0
        and w_down.shape[0] % 16 == 0
    )
    if direct:
        output, grad_tokens, grad_w_qkv, grad_w_out, grad_w_up, grad_w_down, whole = layer_step(
            tokens, cotangent, segments, w_qkv, w_out, w_up, w_down, vectors, nd, nf
        )
        results = adam_all(
            (grad_w_qkv, grad_w_out, grad_w_up, grad_w_down, whole),
            (w_qkv, w_out, w_up, w_down, vectors),
            (first_qkv, first_out, first_up, first_down, first_vec),
            (second_qkv, second_out, second_up, second_down, second_vec),
            (output, grad_tokens),
        )
        return tuple(results)
    else:
        segment = segments[0]
        allowed = doc_mask(segment)
        cosine_part, sine_part = rotary_tables(segment)
        whole = [
            lax.all_gather(x.astype(jnp.bfloat16), axes, axis=0, tiled=True)
            for x in (w_qkv, w_out, w_up, w_down, vectors)
        ]
        output, saved = forward_pass(tokens, allowed, cosine_part, sine_part, *whole)
        grad_tokens, *local = backward_pass(
            saved, cotangent, allowed, cosine_part, sine_part, *whole
        )
        factor = 1.0 / math.sqrt(device_count * tokens.shape[0])
        grad_w_qkv, grad_w_out, grad_w_up, grad_w_down, grad_vectors = (
            factor * lax.psum_scatter(x, axes, scatter_dimension=0, tiled=True) for x in local
        )
    new_w_qkv, new_first_qkv, new_second_qkv = adam_update(
        w_qkv, grad_w_qkv, first_qkv, second_qkv, rate_matrix, decay_matrix
    )
    new_w_out, new_first_out, new_second_out = adam_update(
        w_out, grad_w_out, first_out, second_out, rate_matrix, decay_matrix
    )
    new_w_up, new_first_up, new_second_up = adam_update(
        w_up, grad_w_up, first_up, second_up, rate_matrix, decay_matrix
    )
    new_w_down, new_first_down, new_second_down = adam_update(
        w_down, grad_w_down, first_down, second_down, rate_matrix, decay_matrix
    )
    new_vectors, new_first_vec, new_second_vec = adam_update(
        vectors, grad_vectors, first_vec, second_vec, rate_vector, 0.0
    )
    return (
        output,
        grad_tokens,
        grad_w_qkv,
        grad_w_out,
        grad_w_up,
        grad_w_down,
        grad_vectors,
        new_w_qkv,
        new_w_out,
        new_w_up,
        new_w_down,
        new_vectors,
        new_first_qkv,
        new_first_out,
        new_first_up,
        new_first_down,
        new_first_vec,
        new_second_qkv,
        new_second_out,
        new_second_up,
        new_second_down,
        new_second_vec,
    )


def solution(mesh):
    placed = (
        P(("dp", "fsdp"), None),
        P(("dp", "fsdp"), None),
        P(("dp", "fsdp"), None),
        P(("dp", "fsdp"), None),
        P(("dp", "fsdp"), None),
        P(("dp", "fsdp"), None),
        P(("dp", "fsdp"), None),
        P(("dp", "fsdp")),
        P(("dp", "fsdp"), None),
        P(("dp", "fsdp"), None),
        P(("dp", "fsdp"), None),
        P(("dp", "fsdp"), None),
        P(("dp", "fsdp")),
        P(("dp", "fsdp"), None),
        P(("dp", "fsdp"), None),
        P(("dp", "fsdp"), None),
        P(("dp", "fsdp"), None),
        P(("dp", "fsdp")),
    )
    return jax.shard_map(
        per_device,
        mesh=mesh,
        in_specs=placed,
        out_specs=(
            P(("dp", "fsdp"), None),
            P(("dp", "fsdp"), None),
            P(("dp", "fsdp"), None),
            P(("dp", "fsdp"), None),
            P(("dp", "fsdp"), None),
            P(("dp", "fsdp"), None),
            P(("dp", "fsdp")),
            P(("dp", "fsdp"), None),
            P(("dp", "fsdp"), None),
            P(("dp", "fsdp"), None),
            P(("dp", "fsdp"), None),
            P(("dp", "fsdp")),
            P(("dp", "fsdp"), None),
            P(("dp", "fsdp"), None),
            P(("dp", "fsdp"), None),
            P(("dp", "fsdp"), None),
            P(("dp", "fsdp")),
            P(("dp", "fsdp"), None),
            P(("dp", "fsdp"), None),
            P(("dp", "fsdp"), None),
            P(("dp", "fsdp"), None),
            P(("dp", "fsdp")),
        ),
        check_vma=False,
    )
```

```python
import functools
import math

import jax
import jax.numpy as jnp
import ml_dtypes
import numpy as np
from jax import lax
from jax.experimental import pallas as pl
from jax.experimental.pallas import tpu as pltpu
from jax.sharding import PartitionSpec as P

D = 768
HEADS = 12
HEAD_DIM = 64
ROT = 16
STEP = 3


eps_norm = 1e-05
beta_first = 0.9
beta_second = 0.95
adam_epsilon = 1e-08
rate_matrix = 0.008
rate_vector = 0.1
decay_matrix = 0.01
rotary_base = 10000.0
mask_fill = -1e30


def layer_norm(inputs, gain_row, offset):
    center = inputs - jnp.mean(inputs, axis=-1, keepdims=True)
    inv_sigma = lax.rsqrt(jnp.mean(center * center, axis=-1, keepdims=True) + eps_norm)
    normed = center * inv_sigma
    return (normed, inv_sigma, normed * gain_row + offset)


def layer_norm_back(grad_norm, normed, inv_sigma, gain_row):
    scaled = grad_norm * gain_row
    return inv_sigma * (
        scaled
        - jnp.mean(scaled, axis=-1, keepdims=True)
        - normed * jnp.mean(scaled * normed, axis=-1, keepdims=True)
    )


def gelu_value(inputs):
    return 0.5 * inputs * (1.0 + jax.scipy.special.erf(inputs * (1.0 / math.sqrt(2.0))))


def gelu_slope(inputs):
    cumulative = 0.5 * (1.0 + jax.scipy.special.erf(inputs * (1.0 / math.sqrt(2.0))))
    return cumulative + inputs * jnp.exp(-0.5 * inputs * inputs) * (1.0 / math.sqrt(2.0 * math.pi))


def rotary_tables(segment):
    rows_here = segment.shape[0]
    earlier = jnp.sum((segment[None, :] < segment[:, None]).astype(jnp.int32), axis=1)
    position = jnp.arange(rows_here, dtype=jnp.int32) - earlier
    half_rot = ROT // 2
    inverse = rotary_base ** (-2.0 * jnp.arange(half_rot, dtype=jnp.float32) / ROT)
    angles = position.astype(jnp.float32)[:, None] * inverse[None, :]
    return (jnp.cos(angles)[:, None, :], jnp.sin(angles)[:, None, :])


def rotate(tensor, cosine_part, sine_part):
    half_rot = ROT // 2
    front_part = tensor[..., :half_rot]
    middle = tensor[..., half_rot:ROT]
    remain = tensor[..., ROT:]
    return jnp.concatenate(
        [
            front_part * cosine_part - middle * sine_part,
            middle * cosine_part + front_part * sine_part,
            remain,
        ],
        axis=-1,
    )


def rotate_back(tensor, cosine_part, sine_part):
    half_rot = ROT // 2
    front_part = tensor[..., :half_rot]
    middle = tensor[..., half_rot:ROT]
    remain = tensor[..., ROT:]
    return jnp.concatenate(
        [
            front_part * cosine_part + middle * sine_part,
            middle * cosine_part - front_part * sine_part,
            remain,
        ],
        axis=-1,
    )


def doc_mask(segment):
    row_index = jnp.arange(segment.shape[0], dtype=jnp.int32)
    return (segment[:, None] == segment[None, :]) & (row_index[None, :] <= row_index[:, None])


def masked_scores(queries, key_rot, allowed):
    scores = jnp.einsum("qhd,khd->hqk", queries, key_rot, preferred_element_type=jnp.float32) * (
        1.0 / math.sqrt(HEAD_DIM)
    )
    return jnp.where(allowed[None, :, :], scores, mask_fill)


def forward_pass(
    tokens, allowed, cosine_part, sine_part, full_qkv, full_out, full_up, full_down, full_vec
):
    rows_here = tokens.shape[0]
    vec_table = full_vec.astype(jnp.float32).reshape(13, D)
    inputs = tokens.astype(jnp.float32)
    normed_one, sigma_one, hidden_one = layer_norm(inputs, vec_table[0], vec_table[1])
    normed_two, sigma_two, hidden_two = layer_norm(inputs, vec_table[2], vec_table[3])
    hidden_one = hidden_one.astype(jnp.bfloat16)
    hidden_two = hidden_two.astype(jnp.bfloat16)
    projected = jnp.dot(hidden_one, full_qkv, preferred_element_type=jnp.float32) + vec_table[
        4:7
    ].reshape(-1)
    queries = rotate(
        projected[:, :D].reshape(rows_here, HEADS, HEAD_DIM), cosine_part, sine_part
    ).astype(jnp.bfloat16)
    key_rot = rotate(
        projected[:, D : 2 * D].reshape(rows_here, HEADS, HEAD_DIM), cosine_part, sine_part
    ).astype(jnp.bfloat16)
    values = projected[:, 2 * D :].reshape(rows_here, HEADS, HEAD_DIM).astype(jnp.bfloat16)
    scores = masked_scores(queries, key_rot, allowed)
    top_score = jnp.max(scores, axis=-1, keepdims=True)
    log_total = top_score + jnp.log(jnp.sum(jnp.exp(scores - top_score), axis=-1, keepdims=True))
    soft_weights = jnp.exp(scores - log_total).astype(jnp.bfloat16)
    context = (
        jnp.einsum("hqk,khd->qhd", soft_weights, values, preferred_element_type=jnp.float32)
        .reshape(rows_here, D)
        .astype(jnp.bfloat16)
    )
    attended = jnp.dot(context, full_out, preferred_element_type=jnp.float32) + vec_table[7]
    up_proj = jnp.dot(hidden_two, full_up, preferred_element_type=jnp.float32) + vec_table[
        8:12
    ].reshape(-1)
    activated = gelu_value(up_proj).astype(jnp.bfloat16)
    feed_out = jnp.dot(activated, full_down, preferred_element_type=jnp.float32) + vec_table[12]
    output = (inputs + attended + feed_out).astype(jnp.bfloat16)
    saved = (
        normed_one,
        sigma_one,
        hidden_one,
        normed_two,
        sigma_two,
        hidden_two,
        queries,
        key_rot,
        values,
        log_total,
        context,
        up_proj,
        activated,
    )
    return (output, saved)


def backward_pass(
    saved,
    cotangent,
    allowed,
    cosine_part,
    sine_part,
    back_qkv,
    back_out,
    back_up,
    back_down,
    back_vec,
):
    (
        normed_one,
        sigma_one,
        hidden_one,
        normed_two,
        sigma_two,
        hidden_two,
        queries,
        key_rot,
        values,
        log_total,
        context,
        up_proj,
        activated,
    ) = saved
    rows_here = cotangent.shape[0]
    vec_table = back_vec.astype(jnp.float32).reshape(13, D)
    grad_out = cotangent.astype(jnp.float32)
    grad_w_down = jnp.dot(activated.T, cotangent, preferred_element_type=jnp.float32)
    grad_act = jnp.dot(cotangent, back_down.T, preferred_element_type=jnp.float32)
    grad_up = grad_act * gelu_slope(up_proj)
    grad_up_low = grad_up.astype(jnp.bfloat16)
    grad_w_up = jnp.dot(hidden_two.T, grad_up_low, preferred_element_type=jnp.float32)
    grad_hidden_two = jnp.dot(grad_up_low, back_up.T, preferred_element_type=jnp.float32)
    grad_w_out = jnp.dot(context.T, cotangent, preferred_element_type=jnp.float32)
    grad_context = (
        jnp.dot(cotangent, back_out.T, preferred_element_type=jnp.float32)
        .astype(jnp.bfloat16)
        .reshape(rows_here, HEADS, HEAD_DIM)
    )
    again_scores = masked_scores(queries, key_rot, allowed)
    probs_full = jnp.exp(again_scores - log_total)
    probs_low = probs_full.astype(jnp.bfloat16)
    grad_probs = jnp.einsum(
        "qhd,khd->hqk", grad_context, values, preferred_element_type=jnp.float32
    )
    row_inner = jnp.sum(probs_full * grad_probs, axis=-1, keepdims=True)
    grad_scores = (probs_full * (grad_probs - row_inner) * (1.0 / math.sqrt(HEAD_DIM))).astype(
        jnp.bfloat16
    )
    grad_queries = jnp.einsum(
        "hqk,khd->qhd", grad_scores, key_rot, preferred_element_type=jnp.float32
    )
    grad_keys = jnp.einsum("hqk,qhd->khd", grad_scores, queries, preferred_element_type=jnp.float32)
    grad_values = jnp.einsum(
        "hqk,qhd->khd", probs_low, grad_context, preferred_element_type=jnp.float32
    )
    grad_projected = jnp.concatenate(
        [
            rotate_back(grad_queries, cosine_part, sine_part).reshape(rows_here, D),
            rotate_back(grad_keys, cosine_part, sine_part).reshape(rows_here, D),
            grad_values.reshape(rows_here, D),
        ],
        axis=1,
    )
    grad_proj_low = grad_projected.astype(jnp.bfloat16)
    grad_w_qkv = jnp.dot(hidden_one.T, grad_proj_low, preferred_element_type=jnp.float32)
    grad_hidden_one = jnp.dot(grad_proj_low, back_qkv.T, preferred_element_type=jnp.float32)
    grad_table = jnp.concatenate(
        [
            jnp.sum(grad_hidden_one * normed_one, axis=0)[None],
            jnp.sum(grad_hidden_one, axis=0)[None],
            jnp.sum(grad_hidden_two * normed_two, axis=0)[None],
            jnp.sum(grad_hidden_two, axis=0)[None],
            jnp.sum(grad_projected, axis=0).reshape(3, D),
            jnp.sum(grad_out, axis=0)[None],
            jnp.sum(grad_up, axis=0).reshape(4, D),
            jnp.sum(grad_out, axis=0)[None],
        ],
        axis=0,
    )
    grad_tokens = (
        grad_out
        + layer_norm_back(grad_hidden_one, normed_one, sigma_one, vec_table[0])
        + layer_norm_back(grad_hidden_two, normed_two, sigma_two, vec_table[2])
    ).astype(jnp.bfloat16)
    grad_table = lax.optimization_barrier(grad_table)
    return (grad_tokens, grad_w_qkv, grad_w_out, grad_w_up, grad_w_down, grad_table.reshape(-1))


def adam_update(weight, gradient, moment_one, moment_two, rate_value, decay_value):
    new_one = beta_first * moment_one + (1.0 - beta_first) * gradient
    new_two = beta_second * moment_two + (1.0 - beta_second) * gradient * gradient
    corrected_one = new_one * (1.0 / (1.0 - beta_first**STEP))
    corrected_two = new_two * (1.0 / (1.0 - beta_second**STEP))
    new_weight = weight - rate_value * (
        corrected_one / (jnp.sqrt(corrected_two) + adam_epsilon) + decay_value * weight
    )
    return (new_weight, new_one, new_two)


MESH = pl.DeviceIdType.MESH
LANES = 128


def mm(left, right):
    return lax.dot_general(left, right, (((1,), (0,)), ((), ())), preferred_element_type=jnp.float32)


def mm_nt(left, right):
    return lax.dot_general(left, right, (((1,), (1,)), ((), ())), preferred_element_type=jnp.float32)


def mm_tn(left, right):
    return lax.dot_general(left, right, (((0,), (0,)), ((), ())), preferred_element_type=jnp.float32)


def rotary_constants(rows):
    half_rot = ROT // 2
    lane = np.arange(LANES) % HEAD_DIM
    inverse = np.float32(rotary_base) ** (-2.0 * np.arange(half_rot, dtype=np.float32) / ROT)
    angles = np.arange(rows, dtype=np.float32)[:, None] * inverse.astype(np.float32)[lane % half_rot]
    cosine = np.where(lane < ROT, np.cos(angles), 1.0).astype(np.float32)
    sine = np.where(lane < ROT, np.sin(angles), 0.0).astype(np.float32)
    both = np.concatenate([cosine, sine], axis=1)
    high = both.astype(ml_dtypes.bfloat16)
    low = (both - high.astype(np.float32)).astype(ml_dtypes.bfloat16)
    swap = np.zeros((LANES, LANES), np.float32)
    for j in range(LANES):
        if lane[j] < half_rot:
            swap[j + half_rot, j] = -1.0
        elif lane[j] < ROT:
            swap[j - half_rot, j] = 1.0
    return np.concatenate([high, low], axis=1), swap.astype(ml_dtypes.bfloat16)


def swapped(value, swap):
    high = value.astype(jnp.bfloat16)
    low = (value - high.astype(jnp.float32)).astype(jnp.bfloat16)
    return mm(high, swap) + mm(low, swap)


def normalize(value):
    center = value - jnp.mean(value, axis=-1, keepdims=True)
    inv_sigma = lax.rsqrt(jnp.mean(center * center, axis=-1, keepdims=True) + eps_norm)
    return center * inv_sigma, inv_sigma


SENDS, ARRIVALS = 160, 160


def layer_kernel(nd, nf, scale, *refs):
    (tok, cot, seg, wq_far, wo_far, wu_far, wd_far, vecs, trig, swap) = refs[:10]
    (out, gtok, gq, go, gu, gd, gv) = refs[10:17]
    (xs, ys, sg, vd, vz, vp, upS, qS, g_up, g_q, g_down, g_out, w_up, w_q, w_o) = refs[17:32]
    (norm, h1, h2, act, du, outp, ep, proj, ctx, dctx, dp_low, table) = refs[32:44]
    m_up, m_q, m_down, m_out = refs[44:48]
    p_up, p_q, p_down, p_out = refs[48:52]
    r_up, r_q, r_down, r_out = refs[52:56]
    l_up, l_q, l_down, l_out = refs[56:60]
    a_up, a_q, a_down, a_out = refs[60:64]
    (b_up, b_q, f_up, f_q, o_send, e_send, o_recv, e_recv, tz, tp) = refs[64:74]
    (tables, turned, values, weights), refs = refs[74:78], refs[:74] + refs[78:]
    wq, wo, wu, wd, vtab = refs[74:79]
    sent, came, near = refs[79:]
    nz = nf // 2
    rows, width = tok.shape
    low = jnp.bfloat16
    wide = jnp.float32
    d, f = lax.axis_index("dp"), lax.axis_index("fsdp")
    z, c = lax.div(f, 2), lax.rem(f, 2)
    loads = [
        pltpu.make_async_copy(far, close, near.at[i])
        for i, (far, close) in enumerate(
            ((wd_far, wd), (wo_far, wo), (wu_far, wu), (wq_far, wq))
        )
    ]
    for load in loads:
        load.start()
    part = wq.shape[1] // nd
    third = part // 3
    hid = wu.shape[1] // nd
    block = wq.shape[0]

    state = {"sent": 0, "came": 0}
    pend = []

    def grab(count):
        at = state["came"]
        state["came"] += count
        assert state["came"] <= ARRIVALS
        return at

    def send(source, target, arrival, peer, cond=None):
        slot = state["sent"]
        state["sent"] += 1
        assert slot < SENDS

        copy = pltpu.make_async_remote_copy(
            src_ref=source(),
            dst_ref=target(),
            send_sem=sent.at[slot],
            recv_sem=came.at[arrival],
            device_id=peer,
            device_id_type=MESH,
        )
        pend.append((cond, copy))
        if cond is None:
            copy.start()
        else:
            pl.when(cond)(lambda: copy.start())

    def landed(ref, arrival):
        pltpu.make_async_copy(ref, ref, came.at[arrival]).wait()

    def mate(k):
        return (lax.rem(d + k, nd), f)

    def origin(k):
        return lax.rem(d + nd - k, nd)

    pair = (d, z * 2 + 1 - c)
    right, left = (d, (z + 1) * 2 + c), (d, (z - 1) * 2 + c)
    level = lambda k: (d, lax.rem(z + k, nz) * 2 + c)

    def span(index, size):
        return pl.ds(pl.multiple_of(index * size, size), size)

    barrier = pltpu.get_barrier_semaphore()
    peers = [mate(k) for k in range(1, nd)] + [level(k) for k in range(1, nz)] + [pair]
    for peer in peers:
        pl.semaphore_signal(barrier, inc=1, device_id=peer, device_id_type=MESH)
    count = vecs.shape[0]
    first_at = (d * nf + f) * count
    row = lax.div(first_at, width)
    shift = first_at - row * width
    row_of = lax.broadcasted_iota(jnp.int32, (16, width), 0)
    lane_of = lax.broadcasted_iota(jnp.int32, (16, width), 1)
    wraps = lane_of < shift
    own_row = row_of == row + jnp.where(wraps, 1, 0)
    inside = lane_of - shift + jnp.where(wraps, width, 0) < count
    line = jnp.concatenate([vecs[...].reshape(1, count), jnp.zeros((1, width - count), wide)], axis=1)
    line = pltpu.roll(jnp.broadcast_to(line, (16, width)), shift, 1)
    vtab[...] = jnp.where(jnp.logical_and(own_row, inside), line, 0.0).astype(low)
    vd[d] = vtab[...]
    sg[d] = jnp.broadcast_to(seg[...], (8, rows))
    for load in loads[:2]:
        load.wait()
    g_down[f] = wd[...].astype(low)
    g_out[f] = wo[...].astype(low)
    pl.semaphore_wait(barrier, len(peers))

    gathered = [g_down, g_out, g_up, g_q]
    wire = [grab(nz) for _ in gathered]
    cross = [grab(nz) for _ in gathered]

    def own(p):
        buf = gathered[p]
        here = lambda: buf.at[f]
        send(here, here, wire[p] + z, right, z < nz - 1)
        send(here, here, wire[p] + z, left, z > 0)
        send(here, here, cross[p] + z, pair)

    def relay(p, hop):
        buf = gathered[p]
        for origin_z, cond, onward, more in (
            (z - hop, z >= hop, right, z < nz - 1),
            (z + hop, z + hop < nz, left, z > 0),
        ):
            piece = functools.partial(lambda o: buf.at[o * 2 + c], origin_z)
            pl.when(cond)(functools.partial(lambda pc, o: landed(pc(), wire[p] + o), piece, origin_z))
            send(piece, piece, wire[p] + origin_z, onward, jnp.logical_and(cond, more))
            send(piece, piece, cross[p] + origin_z, pair, cond)

    own(0)
    for load in loads[2:]:
        load.wait()
    mates = range(1, nd)
    up_in, q_in = grab(nd), grab(nd)
    x_in, y_in, s_in, v_in = grab(nd), grab(nd), grab(nd), grab(nd)
    for j in range(nd):
        upS[j] = wu[:, j * hid : (j + 1) * hid].astype(low)
    for k in mates:
        to = lax.rem(d + k, nd)
        send(lambda: upS.at[to], lambda: g_up.at[f, d], up_in + k, mate(k))
        send(lambda: vtab, lambda: vd.at[d], v_in + k, mate(k))
        send(lambda: sg.at[d], lambda: sg.at[d], s_in + k, mate(k))
    for j in range(nd):
        qS[j] = jnp.concatenate(
            [
                wq[:, t * width + j * third : t * width + (j + 1) * third]
                for t in range(3)
            ],
            axis=1,
        ).astype(low)
    for k in mates:
        to = lax.rem(d + k, nd)
        send(lambda: qS.at[to], lambda: g_q.at[f, d], q_in + k, mate(k))
    keep = [
        pltpu.make_async_copy(tok, xs.at[span(d, rows)], near.at[4]),
        pltpu.make_async_copy(cot, ys.at[span(d, rows)], near.at[5]),
    ]
    for copy in keep:
        copy.start()
    g_up[f, d] = upS[d]
    g_q[f, d] = qS[d]
    vz_in, vp_in = grab(nz), grab(1)
    for k in mates:
        landed(g_up.at[f, origin(k)], up_in + k)
    own(2)
    for k in mates:
        landed(g_q.at[f, origin(k)], q_in + k)
    for k in mates:
        send(lambda: tok, lambda: xs.at[span(d, rows)], x_in + k, mate(k))
    for k in mates:
        send(lambda: cot, lambda: ys.at[span(d, rows)], y_in + k, mate(k))
    for k in mates:
        landed(vd.at[origin(k)], v_in + k)
    vz[z] = sum(vd[j].astype(wide) for j in range(nd)).astype(low)
    for k in range(1, nz):
        send(lambda: vz.at[z], lambda: vz.at[z], vz_in + k, level(k))
    relay(0, 1)
    relay(2, 1)
    own(3)
    own(1)
    for k in range(1, nz):
        landed(vz.at[lax.rem(z + nz - k, nz)], vz_in + k)
    vp[c] = sum(vz[j].astype(wide) for j in range(nz)).astype(low)
    send(lambda: vp.at[c], lambda: vp.at[c], vp_in, pair)
    for hop in range(2, nz - 1):
        relay(0, hop)
        relay(2, hop)
    landed(vp.at[1 - c], vp_in)
    vec = vp[0].astype(wide) + vp[1].astype(wide)

    for copy in keep:
        copy.wait()
    for k in mates:
        landed(xs.at[span(origin(k), rows)], x_in + k)
    for b in range(nd):
        at = slice(b * rows, (b + 1) * rows)
        value, _ = normalize(xs[at, :].astype(wide))
        norm[at, :] = value
        h1[at, :] = (value * vec[0:1] + vec[1:2]).astype(low)
        h2[at, :] = (value * vec[2:3] + vec[3:4]).astype(low)

    def mine_of(pieces):
        return sum(jnp.where(d == j, pieces[j], 0.0) for j in range(nd))

    for p in (0, 2):
        relay(p, nz - 1)
    relay(3, 1)
    relay(1, 1)
    for k in mates:
        landed(ys.at[span(origin(k), rows)], y_in + k)
        landed(sg.at[origin(k)], s_in + k)
    for p in (0, 2):
        for o in range(nz):
            landed(gathered[p].at[2 * o + 1 - c], cross[p] + o)
    def unblock(source, target):
        for j in range(nd):
            for o in range(nz):
                value = jnp.concatenate(
                    [source[2 * o, j].astype(wide), source[2 * o + 1, j].astype(wide)], axis=0
                )
                start = (j * nf + 2 * o) * block
                target[start : start + 2 * block, :] = value.astype(low)

    unblock(g_up, w_up)
    w_down = g_down[...].reshape(hid, width)
    cu = mine_of([vec[8 + j : 9 + j] for j in range(nd)])
    cut = 256
    du_sums = []
    for n in range(hid // cut):
        cols = slice(n * cut, (n + 1) * cut)
        u = mm(h2[...], w_up[:, cols]) + cu[:, cols]
        da = mm_nt(ys[...], w_down[cols, :])
        phi = 0.5 * (1.0 + lax.erf(u * (1.0 / math.sqrt(2.0))))
        act[:, cols] = (u * phi).astype(low)
        value = da * (phi + u * jnp.exp(-0.5 * u * u) * (1.0 / math.sqrt(2.0 * math.pi)))
        du_sums.append(jnp.sum(value, axis=0, keepdims=True))
        du[:, cols] = value.astype(low)
    du_sum = jnp.concatenate(du_sums, axis=1)
    sums = [m_down, m_up, m_q, m_out]
    paired = [p_down, p_up, p_q, p_out]
    rights = [r_down, r_up, r_q, r_out]
    lefts = [l_down, l_up, l_q, l_out]
    totals = [a_down, a_up, a_q, a_out]
    pair_in = [grab(1) for _ in sums]
    right_in = [grab(nz) for _ in sums]
    left_in = [grab(nz) for _ in sums]

    def share(p):
        send(lambda: sums[p].at[1 - c], lambda: paired[p].at[...], pair_in[p], pair)

    def first(p):
        landed(paired[p], pair_in[p])
        for k in range(nz - 1, 0, -1):
            for target, bound, inbox, sem, peer in (
                (z + k, z == 0, rights[p], right_in[p], right),
                (z - k, z == nz - 1, lefts[p], left_in[p], left),
            ):

                def add(target=target):
                    sums[p][c, target] = (
                        sums[p][c, target].astype(wide) + paired[p][target].astype(wide)
                    ).astype(low)

                pl.when(bound)(add)
                send(
                    functools.partial(lambda t: sums[p].at[c, t], target),
                    functools.partial(lambda box, t: box.at[t], inbox, target),
                    sem + target,
                    peer,
                    bound,
                )

    def middle(p, k):
        for target, bound, inbox, sem, peer in (
            (z + k, jnp.logical_and(z > 0, z + k < nz), rights[p], right_in[p], right),
            (z - k, jnp.logical_and(z < nz - 1, z >= k), lefts[p], left_in[p], left),
        ):

            def add(target=target, inbox=inbox, sem=sem):
                landed(inbox.at[target], sem + target)
                sums[p][c, target] = (
                    sums[p][c, target].astype(wide)
                    + paired[p][target].astype(wide)
                    + inbox[target].astype(wide)
                ).astype(low)

            pl.when(bound)(add)
            send(
                functools.partial(lambda t: sums[p].at[c, t], target),
                functools.partial(lambda box, t: box.at[t], inbox, target),
                sem + target,
                peer,
                bound,
            )

    def last(p):
        totals[p][...] = sums[p][c, z].astype(wide) + paired[p][z].astype(wide)
        for bound, inbox, sem in ((z > 0, rights[p], right_in[p]), (z < nz - 1, lefts[p], left_in[p])):

            def add(inbox=inbox, sem=sem):
                landed(inbox.at[z], sem + z)
                totals[p][...] = totals[p][...] + inbox[z].astype(wide)

            pl.when(bound)(add)

    for hop in range(2, nz - 1):
        relay(3, hop)
        relay(1, hop)
    value = mm_tn(h2[...], du[...])
    for j in range(nd):
        for i in range(nf):
            start = (j * nf + i) * block
            m_up[i % 2, i // 2, j] = value[start : start + block].astype(low)
    share(1)
    value = mm_tn(act[...], ys[...])
    size = wd.shape[0]
    for i in range(nf):
        m_down[i % 2, i // 2] = value[i * size : (i + 1) * size].astype(low)
    share(0)
    first(1)
    first(0)
    outp[...] = mm(act[...], w_down)
    dh = mm_nt(du[...], w_up[...])
    ep[...] = dh * vec[2:3]
    table[...] = jnp.zeros_like(table)
    table[2:3, :] = jnp.sum(dh * norm[...], axis=0, keepdims=True)
    table[3:4, :] = jnp.sum(dh, axis=0, keepdims=True)
    dy_sum = jnp.sum(ys[span(d, rows), :].astype(wide), axis=0, keepdims=True)
    table[7:8, :] = dy_sum
    table[12:13, :] = dy_sum
    for j in range(nd):
        table[8 + j : 9 + j, :] = jnp.where(d == j, du_sum, 0.0)
    relay(3, nz - 1)
    relay(1, nz - 1)
    middle(1, nz - 2)

    for p in (1, 3):
        for o in range(nz):
            landed(gathered[p].at[2 * o + 1 - c], cross[p] + o)
    unblock(g_q, w_q)
    for o in range(nz):
        value = jnp.concatenate([g_out[2 * o].astype(wide), g_out[2 * o + 1].astype(wide)], axis=0)
        w_o[2 * o * block : 2 * (o + 1) * block, :] = value.astype(low)
    cq = jnp.concatenate(
        [
            mine_of([vec[4 + t : 5 + t, j * third : (j + 1) * third] for j in range(nd)])
            for t in range(3)
        ],
        axis=1,
    )
    proj[...] = mm(h1[...], w_q[...]) + cq
    dctx[...] = mm_nt(ys[...], w_o[...]).astype(low)
    row_at = lax.broadcasted_iota(jnp.int32, (rows, rows), 0)
    col_at = lax.broadcasted_iota(jnp.int32, (rows, rows), 1)
    causal = col_at <= row_at
    sharp = 1.0 / math.sqrt(HEAD_DIM)

    heads = third // HEAD_DIM

    def forward(blocks):
        masks, pairs = {}, [(b, h) for b in blocks for h in range(heads)]
        for b in blocks:
            name = jnp.broadcast_to(sg[b][0:1, :].astype(wide), (rows, rows))
            masks[b] = jnp.logical_and(name == name.T, causal)
        for b in blocks:
            pos = jnp.sum(jnp.where(masks[b], 1.0, 0.0), axis=1, keepdims=True) - 1.0
            hot = jnp.where(col_at.astype(wide) == pos, 1.0, 0.0).astype(low)
            both = mm(hot, trig[...])
            tables[b] = both[:, : 2 * LANES] + both[:, 2 * LANES :]
        for b in blocks:
            at = slice(b * rows, (b + 1) * rows)
            for t in range(2 * third // LANES):
                x = proj[at, t * LANES : (t + 1) * LANES]
                other = swapped(x, swap[...])
                turned[at, t * LANES : (t + 1) * LANES] = (
                    x * tables[b][:, :LANES] + other * tables[b][:, LANES:]
                ).astype(low)
            values[at, :] = proj[at, 2 * third :].astype(low)
        scores = {}
        for b, h in pairs:
            at = slice(b * rows, (b + 1) * rows)
            q = turned[at, h * HEAD_DIM : (h + 1) * HEAD_DIM]
            k = turned[at, third + h * HEAD_DIM : third + (h + 1) * HEAD_DIM]
            scores[b, h] = jnp.where(masks[b], mm_nt(q, k) * sharp, mask_fill)
        for b, h in pairs:
            scores[b, h] = jnp.exp(scores[b, h] - jnp.max(scores[b, h], axis=-1, keepdims=True))
        for b, h in pairs:
            weights[b * heads + h] = scores[b, h] / jnp.sum(scores[b, h], axis=-1, keepdims=True)
        for b in blocks:
            at = slice(b * rows, (b + 1) * rows)
            ctx[at, :] = jnp.concatenate(
                [
                    mm(
                        weights[b * heads + h].astype(low),
                        values[at, h * HEAD_DIM : (h + 1) * HEAD_DIM],
                    )
                    for h in range(heads)
                ],
                axis=1,
            ).astype(low)

    def backward(blocks):
        pairs = [(b, h) for b in blocks for h in range(heads)]
        grads_of, scored = {}, {}

        def head(ref, b, h, at=0):
            return ref[b * rows : (b + 1) * rows, at + h * HEAD_DIM : at + (h + 1) * HEAD_DIM]

        for b, h in pairs:
            grads_of[b, h] = mm_nt(head(dctx, b, h), head(values, b, h))
        for b, h in pairs:
            a = weights[b * heads + h]
            inner = jnp.sum(a * grads_of[b, h], axis=-1, keepdims=True)
            scored[b, h] = (a * (grads_of[b, h] - inner) * sharp).astype(low)
        dqs, dks, dvs = {}, {}, {}
        for b, h in pairs:
            dqs[b, h] = mm(scored[b, h], head(turned, b, h, third))
        for b, h in pairs:
            dks[b, h] = mm_tn(scored[b, h], head(turned, b, h))
        for b, h in pairs:
            dvs[b, h] = mm_tn(weights[b * heads + h].astype(low), head(dctx, b, h))
        total = jnp.zeros((1, part), wide)
        for b in blocks:
            each = range(heads)
            mixed = jnp.concatenate([dqs[b, h] for h in each] + [dks[b, h] for h in each], axis=1)
            grads = []
            for t in range(2 * third // LANES):
                x = mixed[:, t * LANES : (t + 1) * LANES]
                grads.append(
                    x * tables[b][:, :LANES] - swapped(x, swap[...]) * tables[b][:, LANES:]
                )
            grads = jnp.concatenate(grads + [dvs[b, h] for h in each], axis=1)
            dp_low[b * rows : (b + 1) * rows, :] = grads.astype(low)
            total = total + jnp.sum(grads, axis=0, keepdims=True)
        return total

    halves = [range(0, nd // 2), range(nd // 2, nd)]
    o_in, e_in, t_in = grab(nd), grab(nd), grab(nd)
    for blocks in halves:
        forward(blocks)
    outp[...] += mm(ctx[...], w_o[...])
    o_send[...] = outp[...].astype(low)
    for k in mates:
        to = lax.rem(d + k, nd)
        send(lambda: o_send.at[span(to, rows)], lambda: o_recv.at[k], o_in + k, mate(k))
    for k in range(nz - 3, 0, -1):
        middle(1, k)
    dp_sum = backward(halves[0]) + backward(halves[1])
    middle(0, nz - 2)
    dh = mm_nt(dp_low[...], w_q[...])
    ep[...] += dh * vec[0:1]
    e_send[...] = ep[...].astype(low)
    table[0:1, :] = jnp.sum(dh * norm[...], axis=0, keepdims=True)
    table[1:2, :] = jnp.sum(dh, axis=0, keepdims=True)
    for t in range(3):
        piece = dp_sum[:, t * third : (t + 1) * third]
        table[4 + t : 5 + t, :] = jnp.concatenate(
            [jnp.where(d == j, piece, 0.0) for j in range(nd)], axis=1
        )
    tz_in, tp_in = grab(nz), grab(1)
    tz[0] = table[...].astype(low)
    for k in mates:
        send(lambda: tz.at[0], lambda: tz.at[k], t_in + k, mate(k))
    for k in mates:
        to = lax.rem(d + k, nd)
        send(lambda: e_send.at[span(to, rows)], lambda: e_recv.at[k], e_in + k, mate(k))
    value = mm_tn(h1[...], dp_low[...])
    for j in range(nd):
        for i in range(nf):
            start = (j * nf + i) * block
            m_q[i % 2, i // 2, j] = value[start : start + block].astype(low)
    value = mm_tn(ctx[...], ys[...])
    for i in range(nf):
        m_out[i % 2, i // 2] = value[i * block : (i + 1) * block].astype(low)
    share(2)
    share(3)
    first(2)
    first(3)
    for k in range(nz - 3, 0, -1):
        middle(0, k)
    fu_in, fq_in = grab(nd), grab(nd)

    def give_back(p, whole, box, arrivals):
        last(p)
        whole[...] = totals[p][...].astype(low)
        for k in mates:
            to = lax.rem(d + k, nd)
            send(lambda: whole.at[to], lambda: box.at[d], arrivals + k, mate(k))
        box[d] = whole[d]

    give_back(1, b_up, f_up, fu_in)
    for k in mates:
        landed(tz.at[k], t_in + k)
    tz[nd] = (table[...] + sum(tz[k].astype(wide) for k in mates)).astype(low)
    for k in range(1, nz):
        send(lambda: tz.at[nd], lambda: tz.at[nd + k], tz_in + k, level(k))
    last(0)
    gd[...] = a_down[...] * scale
    for k in range(nz - 2, 0, -1):
        middle(2, k)
        middle(3, k)
    for k in range(1, nz):
        landed(tz.at[nd + k], tz_in + k)
    tp[0] = sum(tz[nd + k].astype(wide) for k in range(nz)).astype(low)
    send(lambda: tp.at[0], lambda: tp.at[1], tp_in, pair)
    give_back(2, b_q, f_q, fq_in)
    last(3)
    go[...] = a_out[...] * scale
    for k in mates:
        landed(o_recv.at[k], o_in + k)
        landed(e_recv.at[k], e_in + k)
    total = xs[span(d, rows), :].astype(wide) + vec[7:8] + vec[12:13] + outp[span(d, rows), :]
    out[...] = (total + sum(o_recv[k].astype(wide) for k in mates)).astype(low)
    value, inv_sigma = normalize(xs[span(d, rows), :].astype(wide))
    e = ep[span(d, rows), :] + sum(e_recv[k].astype(wide) for k in mates)
    gtok[...] = (
        ys[span(d, rows), :].astype(wide)
        + inv_sigma
        * (
            e
            - jnp.mean(e, axis=-1, keepdims=True)
            - value * jnp.mean(e * value, axis=-1, keepdims=True)
        )
    ).astype(low)
    landed(tp.at[1], tp_in)
    whole = (tp[0].astype(wide) + tp[1].astype(wide)) * scale
    line = jnp.sum(jnp.where(own_row, whole, 0.0), axis=0, keepdims=True)
    line = pltpu.roll(jnp.broadcast_to(line, (8, width)), lax.rem(width - shift, width), 1)
    gv[...] = line[0:1, :count].reshape(count)
    for k in mates:
        landed(f_up.at[origin(k)], fu_in + k)
        landed(f_q.at[origin(k)], fq_in + k)
    for j in range(nd):
        gu[:, j * hid : (j + 1) * hid] = f_up[j].astype(wide) * scale
    gq[...] = scale * jnp.concatenate(
        [f_q[j].astype(wide)[:, t * third : (t + 1) * third] for t in range(3) for j in range(nd)],
        axis=1,
    )
    for cond, copy in pend:
        if cond is None:
            copy.wait_send()
        else:
            pl.when(cond)(functools.partial(lambda x: x.wait_send(), copy))


def layer_step(tokens, cotangent, segments, w_qkv, w_out, w_up, w_down, vectors, nd, nf):
    rows, width = tokens.shape
    low, wide = jnp.bfloat16, jnp.float32
    nz, block, size = nf // 2, w_qkv.shape[0], w_down.shape[0]
    part, hid = w_qkv.shape[1] // nd, w_up.shape[1] // nd
    third = part // 3
    group = nd * rows
    count = vectors.shape[0]
    trig, swap = rotary_constants(rows)
    inputs = (
        tokens,
        cotangent,
        segments,
        w_qkv,
        w_out,
        w_up,
        w_down,
        vectors,
        jnp.asarray(trig),
        jnp.asarray(swap),
    )
    outs = [
        jax.ShapeDtypeStruct((rows, width), low),
        jax.ShapeDtypeStruct((rows, width), low),
        *[jax.ShapeDtypeStruct(x.shape, wide) for x in (w_qkv, w_out, w_up, w_down)],
        jax.ShapeDtypeStruct((count,), wide),
    ]
    vm = pltpu.VMEM
    four = [(nd, block, hid), (nd, block, part), (size, width), (block, width)]
    scratch = [
        vm((group, width), low),
        vm((group, width), low),
        vm((nd, 8, rows), jnp.int32),
        vm((nd, 16, width), low),
        vm((nz, 16, width), low),
        vm((2, 16, width), low),
        vm((nd, block, hid), low),
        vm((nd, block, part), low),
        *[vm((nf, *x), low) for x in four],
        vm((width, hid), low),
        vm((width, part), low),
        vm((third, width), low),
        vm((group, width), wide),
        vm((group, width), low),
        vm((group, width), low),
        vm((group, hid), low),
        vm((group, hid), low),
        vm((group, width), wide),
        vm((group, width), wide),
        vm((group, part), wide),
        vm((group, third), low),
        vm((group, third), low),
        vm((group, part), low),
        vm((16, width), wide),
        *[vm((2, nz, *x), low) for x in four],
        *[vm((nz, *x), low) for x in four],
        *[vm((nz, *x), low) for x in four],
        *[vm((nz, *x), low) for x in four],
        *[vm(x, wide) for x in four],
        vm((nd, block, hid), low),
        vm((nd, block, part), low),
        vm((nd, block, hid), low),
        vm((nd, block, part), low),
        vm((group, width), low),
        vm((group, width), low),
        vm((nd, rows, width), low),
        vm((nd, rows, width), low),
        vm((nd + nz, 16, width), low),
        vm((2, 16, width), low),
        vm((nd, rows, 2 * LANES), wide),
        vm((group, 2 * third), low),
        vm((group, third), low),
        vm((nd * third // HEAD_DIM, rows, rows), wide),
        *[vm(x.shape, wide) for x in (w_qkv, w_out, w_up, w_down)],
        vm((16, width), low),
        pltpu.SemaphoreType.DMA((SENDS,)),
        pltpu.SemaphoreType.DMA((ARRIVALS,)),
        pltpu.SemaphoreType.DMA((6,)),
    ]
    scale = 1.0 / math.sqrt(rows * nd * nf)
    spec = pl.BlockSpec(memory_space=pltpu.VMEM)
    far = pl.BlockSpec(memory_space=pl.ANY)
    return pl.pallas_call(
        functools.partial(layer_kernel, nd, nf, scale),
        out_shape=outs,
        in_specs=[far, far, spec, far, far, far, far, spec, spec, spec],
        out_specs=[spec] * len(outs),
        scratch_shapes=scratch,
        compiler_params=pltpu.CompilerParams(
            collective_id=0, has_side_effects=True, vmem_limit_bytes=60 << 20
        ),
    )(*inputs)


def adam_kernel(count, *refs):
    far = [refs[i * count : (i + 1) * count] for i in range(4)]
    passed, refs = refs[4 * count : 4 * count + 2], refs[4 * count + 2 :]
    pass_outs, refs = refs[:2], refs[2:]
    outs = [refs[i * count : (i + 1) * count] for i in range(4)]
    refs = refs[4 * count :]
    near = [refs[i * count : (i + 1) * count] for i in range(4)]
    held = [refs[(4 + i) * count : (5 + i) * count] for i in range(3)]
    passing = refs[7 * count : 7 * count + 2]
    load_sems, sems = refs[7 * count + 2 :]
    loads = [
        [
            pltpu.make_async_copy(far[j][i], near[j][i], load_sems.at[i * 4 + j])
            for j in range(4)
        ]
        for i in range(count)
    ]
    carried = [
        pltpu.make_async_copy(source, close, load_sems.at[4 * count + i])
        for i, (source, close) in enumerate(zip(passed, passing))
    ]
    for group in [carried] + loads:
        for copy in group:
            copy.start()
    copies = []

    def write(source, target):
        copies.append(pltpu.make_async_copy(source, target, sems.at[len(copies)]))
        copies[-1].start()

    for copy, close, target in zip(carried, passing, pass_outs):
        copy.wait()
        write(close, target)
    for i in range(count):
        for copy in loads[i]:
            copy.wait()
        write(near[0][i], outs[0][i])
        vector = i == count - 1
        results = adam_update(
            near[1][i][...],
            near[0][i][...],
            near[2][i][...],
            near[3][i][...],
            rate_vector if vector else rate_matrix,
            0.0 if vector else decay_matrix,
        )
        for j in range(3):
            held[j][i][...] = results[j]
            write(held[j][i], outs[j + 1][i])
    for copy in copies:
        copy.wait()


def adam_all(grads, weights, firsts, seconds, passed):
    count = len(grads)
    shapes = [jax.ShapeDtypeStruct(x.shape, x.dtype) for x in weights]
    given = [jax.ShapeDtypeStruct(x.shape, x.dtype) for x in passed]
    total = 4 * count + len(passed)
    return pl.pallas_call(
        functools.partial(adam_kernel, count),
        out_shape=given + shapes * 4,
        in_specs=[pl.BlockSpec(memory_space=pl.ANY)] * total,
        out_specs=[pl.BlockSpec(memory_space=pl.ANY)] * total,
        scratch_shapes=[pltpu.VMEM(x.shape, x.dtype) for x in shapes * 7 + given]
        + [pltpu.SemaphoreType.DMA((total,)), pltpu.SemaphoreType.DMA((total,))],
        compiler_params=pltpu.CompilerParams(vmem_limit_bytes=60 << 20),
    )(*grads, *weights, *firsts, *seconds, *passed)


def per_device(
    tokens,
    cotangent,
    segments,
    w_qkv,
    w_out,
    w_up,
    w_down,
    vectors,
    first_qkv,
    first_out,
    first_up,
    first_down,
    first_vec,
    second_qkv,
    second_out,
    second_up,
    second_down,
    second_vec,
):
    device_count = lax.axis_size(("dp", "fsdp"))
    axes = ("dp", "fsdp")
    nd, nf = lax.axis_size("dp"), lax.axis_size("fsdp")
    direct = (
        nd > 1
        and nf % 2 == 0
        and nf > 2
        and HEADS % nd == 0
        and tokens.shape[0] == LANES
        and w_up.shape[1] == nd * D
        and (2 * D // nd) % LANES == 0
        and w_qkv.shape[0] % 8 == 0
        and w_down.shape[0] % 16 == 0
    )
    if direct:
        output, grad_tokens, grad_w_qkv, grad_w_out, grad_w_up, grad_w_down, whole = layer_step(
            tokens, cotangent, segments, w_qkv, w_out, w_up, w_down, vectors, nd, nf
        )
        results = adam_all(
            (grad_w_qkv, grad_w_out, grad_w_up, grad_w_down, whole),
            (w_qkv, w_out, w_up, w_down, vectors),
            (first_qkv, first_out, first_up, first_down, first_vec),
            (second_qkv, second_out, second_up, second_down, second_vec),
            (output, grad_tokens),
        )
        return tuple(results)
    else:
        segment = segments[0]
        allowed = doc_mask(segment)
        cosine_part, sine_part = rotary_tables(segment)
        whole = [
            lax.all_gather(x.astype(jnp.bfloat16), axes, axis=0, tiled=True)
            for x in (w_qkv, w_out, w_up, w_down, vectors)
        ]
        output, saved = forward_pass(tokens, allowed, cosine_part, sine_part, *whole)
        grad_tokens, *local = backward_pass(
            saved, cotangent, allowed, cosine_part, sine_part, *whole
        )
        factor = 1.0 / math.sqrt(device_count * tokens.shape[0])
        grad_w_qkv, grad_w_out, grad_w_up, grad_w_down, grad_vectors = (
            factor * lax.psum_scatter(x, axes, scatter_dimension=0, tiled=True) for x in local
        )
    new_w_qkv, new_first_qkv, new_second_qkv = adam_update(
        w_qkv, grad_w_qkv, first_qkv, second_qkv, rate_matrix, decay_matrix
    )
    new_w_out, new_first_out, new_second_out = adam_update(
        w_out, grad_w_out, first_out, second_out, rate_matrix, decay_matrix
    )
    new_w_up, new_first_up, new_second_up = adam_update(
        w_up, grad_w_up, first_up, second_up, rate_matrix, decay_matrix
    )
    new_w_down, new_first_down, new_second_down = adam_update(
        w_down, grad_w_down, first_down, second_down, rate_matrix, decay_matrix
    )
    new_vectors, new_first_vec, new_second_vec = adam_update(
        vectors, grad_vectors, first_vec, second_vec, rate_vector, 0.0
    )
    return (
        output,
        grad_tokens,
        grad_w_qkv,
        grad_w_out,
        grad_w_up,
        grad_w_down,
        grad_vectors,
        new_w_qkv,
        new_w_out,
        new_w_up,
        new_w_down,
        new_vectors,
        new_first_qkv,
        new_first_out,
        new_first_up,
        new_first_down,
        new_first_vec,
        new_second_qkv,
        new_second_out,
        new_second_up,
        new_second_down,
        new_second_vec,
    )


def solution(mesh):
    placed = (
        P(("dp", "fsdp"), None),
        P(("dp", "fsdp"), None),
        P(("dp", "fsdp"), None),
        P(("dp", "fsdp"), None),
        P(("dp", "fsdp"), None),
        P(("dp", "fsdp"), None),
        P(("dp", "fsdp"), None),
        P(("dp", "fsdp")),
        P(("dp", "fsdp"), None),
        P(("dp", "fsdp"), None),
        P(("dp", "fsdp"), None),
        P(("dp", "fsdp"), None),
        P(("dp", "fsdp")),
        P(("dp", "fsdp"), None),
        P(("dp", "fsdp"), None),
        P(("dp", "fsdp"), None),
        P(("dp", "fsdp"), None),
        P(("dp", "fsdp")),
    )
    return jax.shard_map(
        per_device,
        mesh=mesh,
        in_specs=placed,
        out_specs=(
            P(("dp", "fsdp"), None),
            P(("dp", "fsdp"), None),
            P(("dp", "fsdp"), None),
            P(("dp", "fsdp"), None),
            P(("dp", "fsdp"), None),
            P(("dp", "fsdp"), None),
            P(("dp", "fsdp")),
            P(("dp", "fsdp"), None),
            P(("dp", "fsdp"), None),
            P(("dp", "fsdp"), None),
            P(("dp", "fsdp"), None),
            P(("dp", "fsdp")),
            P(("dp", "fsdp"), None),
            P(("dp", "fsdp"), None),
            P(("dp", "fsdp"), None),
            P(("dp", "fsdp"), None),
            P(("dp", "fsdp")),
            P(("dp", "fsdp"), None),
            P(("dp", "fsdp"), None),
            P(("dp", "fsdp"), None),
            P(("dp", "fsdp"), None),
            P(("dp", "fsdp")),
        ),
        check_vma=False,
    )
```

```python
import functools
import math

import jax
import jax.numpy as jnp
import ml_dtypes
import numpy as np
from jax import lax
from jax.experimental import pallas as pl
from jax.experimental.pallas import tpu as pltpu
from jax.sharding import PartitionSpec as P

D = 768
HEADS = 12
HEAD_DIM = 64
ROT = 16
STEP = 3


eps_norm = 1e-05
beta_first = 0.9
beta_second = 0.95
adam_epsilon = 1e-08
rate_matrix = 0.008
rate_vector = 0.1
decay_matrix = 0.01
rotary_base = 10000.0
mask_fill = -1e30


def layer_norm(inputs, gain_row, offset):
    center = inputs - jnp.mean(inputs, axis=-1, keepdims=True)
    inv_sigma = lax.rsqrt(jnp.mean(center * center, axis=-1, keepdims=True) + eps_norm)
    normed = center * inv_sigma
    return (normed, inv_sigma, normed * gain_row + offset)


def layer_norm_back(grad_norm, normed, inv_sigma, gain_row):
    scaled = grad_norm * gain_row
    return inv_sigma * (
        scaled
        - jnp.mean(scaled, axis=-1, keepdims=True)
        - normed * jnp.mean(scaled * normed, axis=-1, keepdims=True)
    )


def gelu_value(inputs):
    return 0.5 * inputs * (1.0 + jax.scipy.special.erf(inputs * (1.0 / math.sqrt(2.0))))


def gelu_slope(inputs):
    cumulative = 0.5 * (1.0 + jax.scipy.special.erf(inputs * (1.0 / math.sqrt(2.0))))
    return cumulative + inputs * jnp.exp(-0.5 * inputs * inputs) * (1.0 / math.sqrt(2.0 * math.pi))


def rotary_tables(segment):
    rows_here = segment.shape[0]
    earlier = jnp.sum((segment[None, :] < segment[:, None]).astype(jnp.int32), axis=1)
    position = jnp.arange(rows_here, dtype=jnp.int32) - earlier
    half_rot = ROT // 2
    inverse = rotary_base ** (-2.0 * jnp.arange(half_rot, dtype=jnp.float32) / ROT)
    angles = position.astype(jnp.float32)[:, None] * inverse[None, :]
    return (jnp.cos(angles)[:, None, :], jnp.sin(angles)[:, None, :])


def rotate(tensor, cosine_part, sine_part):
    half_rot = ROT // 2
    front_part = tensor[..., :half_rot]
    middle = tensor[..., half_rot:ROT]
    remain = tensor[..., ROT:]
    return jnp.concatenate(
        [
            front_part * cosine_part - middle * sine_part,
            middle * cosine_part + front_part * sine_part,
            remain,
        ],
        axis=-1,
    )


def rotate_back(tensor, cosine_part, sine_part):
    half_rot = ROT // 2
    front_part = tensor[..., :half_rot]
    middle = tensor[..., half_rot:ROT]
    remain = tensor[..., ROT:]
    return jnp.concatenate(
        [
            front_part * cosine_part + middle * sine_part,
            middle * cosine_part - front_part * sine_part,
            remain,
        ],
        axis=-1,
    )


def doc_mask(segment):
    row_index = jnp.arange(segment.shape[0], dtype=jnp.int32)
    return (segment[:, None] == segment[None, :]) & (row_index[None, :] <= row_index[:, None])


def masked_scores(queries, key_rot, allowed):
    scores = jnp.einsum("qhd,khd->hqk", queries, key_rot, preferred_element_type=jnp.float32) * (
        1.0 / math.sqrt(HEAD_DIM)
    )
    return jnp.where(allowed[None, :, :], scores, mask_fill)


def forward_pass(
    tokens, allowed, cosine_part, sine_part, full_qkv, full_out, full_up, full_down, full_vec
):
    rows_here = tokens.shape[0]
    vec_table = full_vec.astype(jnp.float32).reshape(13, D)
    inputs = tokens.astype(jnp.float32)
    normed_one, sigma_one, hidden_one = layer_norm(inputs, vec_table[0], vec_table[1])
    normed_two, sigma_two, hidden_two = layer_norm(inputs, vec_table[2], vec_table[3])
    hidden_one = hidden_one.astype(jnp.bfloat16)
    hidden_two = hidden_two.astype(jnp.bfloat16)
    projected = jnp.dot(hidden_one, full_qkv, preferred_element_type=jnp.float32) + vec_table[
        4:7
    ].reshape(-1)
    queries = rotate(
        projected[:, :D].reshape(rows_here, HEADS, HEAD_DIM), cosine_part, sine_part
    ).astype(jnp.bfloat16)
    key_rot = rotate(
        projected[:, D : 2 * D].reshape(rows_here, HEADS, HEAD_DIM), cosine_part, sine_part
    ).astype(jnp.bfloat16)
    values = projected[:, 2 * D :].reshape(rows_here, HEADS, HEAD_DIM).astype(jnp.bfloat16)
    scores = masked_scores(queries, key_rot, allowed)
    top_score = jnp.max(scores, axis=-1, keepdims=True)
    log_total = top_score + jnp.log(jnp.sum(jnp.exp(scores - top_score), axis=-1, keepdims=True))
    soft_weights = jnp.exp(scores - log_total).astype(jnp.bfloat16)
    context = (
        jnp.einsum("hqk,khd->qhd", soft_weights, values, preferred_element_type=jnp.float32)
        .reshape(rows_here, D)
        .astype(jnp.bfloat16)
    )
    attended = jnp.dot(context, full_out, preferred_element_type=jnp.float32) + vec_table[7]
    up_proj = jnp.dot(hidden_two, full_up, preferred_element_type=jnp.float32) + vec_table[
        8:12
    ].reshape(-1)
    activated = gelu_value(up_proj).astype(jnp.bfloat16)
    feed_out = jnp.dot(activated, full_down, preferred_element_type=jnp.float32) + vec_table[12]
    output = (inputs + attended + feed_out).astype(jnp.bfloat16)
    saved = (
        normed_one,
        sigma_one,
        hidden_one,
        normed_two,
        sigma_two,
        hidden_two,
        queries,
        key_rot,
        values,
        log_total,
        context,
        up_proj,
        activated,
    )
    return (output, saved)


def backward_pass(
    saved,
    cotangent,
    allowed,
    cosine_part,
    sine_part,
    back_qkv,
    back_out,
    back_up,
    back_down,
    back_vec,
):
    (
        normed_one,
        sigma_one,
        hidden_one,
        normed_two,
        sigma_two,
        hidden_two,
        queries,
        key_rot,
        values,
        log_total,
        context,
        up_proj,
        activated,
    ) = saved
    rows_here = cotangent.shape[0]
    vec_table = back_vec.astype(jnp.float32).reshape(13, D)
    grad_out = cotangent.astype(jnp.float32)
    grad_w_down = jnp.dot(activated.T, cotangent, preferred_element_type=jnp.float32)
    grad_act = jnp.dot(cotangent, back_down.T, preferred_element_type=jnp.float32)
    grad_up = grad_act * gelu_slope(up_proj)
    grad_up_low = grad_up.astype(jnp.bfloat16)
    grad_w_up = jnp.dot(hidden_two.T, grad_up_low, preferred_element_type=jnp.float32)
    grad_hidden_two = jnp.dot(grad_up_low, back_up.T, preferred_element_type=jnp.float32)
    grad_w_out = jnp.dot(context.T, cotangent, preferred_element_type=jnp.float32)
    grad_context = (
        jnp.dot(cotangent, back_out.T, preferred_element_type=jnp.float32)
        .astype(jnp.bfloat16)
        .reshape(rows_here, HEADS, HEAD_DIM)
    )
    again_scores = masked_scores(queries, key_rot, allowed)
    probs_full = jnp.exp(again_scores - log_total)
    probs_low = probs_full.astype(jnp.bfloat16)
    grad_probs = jnp.einsum(
        "qhd,khd->hqk", grad_context, values, preferred_element_type=jnp.float32
    )
    row_inner = jnp.sum(probs_full * grad_probs, axis=-1, keepdims=True)
    grad_scores = (probs_full * (grad_probs - row_inner) * (1.0 / math.sqrt(HEAD_DIM))).astype(
        jnp.bfloat16
    )
    grad_queries = jnp.einsum(
        "hqk,khd->qhd", grad_scores, key_rot, preferred_element_type=jnp.float32
    )
    grad_keys = jnp.einsum("hqk,qhd->khd", grad_scores, queries, preferred_element_type=jnp.float32)
    grad_values = jnp.einsum(
        "hqk,qhd->khd", probs_low, grad_context, preferred_element_type=jnp.float32
    )
    grad_projected = jnp.concatenate(
        [
            rotate_back(grad_queries, cosine_part, sine_part).reshape(rows_here, D),
            rotate_back(grad_keys, cosine_part, sine_part).reshape(rows_here, D),
            grad_values.reshape(rows_here, D),
        ],
        axis=1,
    )
    grad_proj_low = grad_projected.astype(jnp.bfloat16)
    grad_w_qkv = jnp.dot(hidden_one.T, grad_proj_low, preferred_element_type=jnp.float32)
    grad_hidden_one = jnp.dot(grad_proj_low, back_qkv.T, preferred_element_type=jnp.float32)
    grad_table = jnp.concatenate(
        [
            jnp.sum(grad_hidden_one * normed_one, axis=0)[None],
            jnp.sum(grad_hidden_one, axis=0)[None],
            jnp.sum(grad_hidden_two * normed_two, axis=0)[None],
            jnp.sum(grad_hidden_two, axis=0)[None],
            jnp.sum(grad_projected, axis=0).reshape(3, D),
            jnp.sum(grad_out, axis=0)[None],
            jnp.sum(grad_up, axis=0).reshape(4, D),
            jnp.sum(grad_out, axis=0)[None],
        ],
        axis=0,
    )
    grad_tokens = (
        grad_out
        + layer_norm_back(grad_hidden_one, normed_one, sigma_one, vec_table[0])
        + layer_norm_back(grad_hidden_two, normed_two, sigma_two, vec_table[2])
    ).astype(jnp.bfloat16)
    grad_table = lax.optimization_barrier(grad_table)
    return (grad_tokens, grad_w_qkv, grad_w_out, grad_w_up, grad_w_down, grad_table.reshape(-1))


def adam_update(weight, gradient, moment_one, moment_two, rate_value, decay_value):
    new_one = beta_first * moment_one + (1.0 - beta_first) * gradient
    new_two = beta_second * moment_two + (1.0 - beta_second) * gradient * gradient
    corrected_one = new_one * (1.0 / (1.0 - beta_first**STEP))
    corrected_two = new_two * (1.0 / (1.0 - beta_second**STEP))
    new_weight = weight - rate_value * (
        corrected_one / (jnp.sqrt(corrected_two) + adam_epsilon) + decay_value * weight
    )
    return (new_weight, new_one, new_two)


MESH = pl.DeviceIdType.MESH
LANES = 128


def mm(left, right):
    return lax.dot_general(left, right, (((1,), (0,)), ((), ())), preferred_element_type=jnp.float32)


def mm_nt(left, right):
    return lax.dot_general(left, right, (((1,), (1,)), ((), ())), preferred_element_type=jnp.float32)


def mm_tn(left, right):
    return lax.dot_general(left, right, (((0,), (0,)), ((), ())), preferred_element_type=jnp.float32)


def rotary_constants(rows):
    half_rot = ROT // 2
    lane = np.arange(LANES) % HEAD_DIM
    inverse = np.float32(rotary_base) ** (-2.0 * np.arange(half_rot, dtype=np.float32) / ROT)
    angles = np.arange(rows, dtype=np.float32)[:, None] * inverse.astype(np.float32)[lane % half_rot]
    cosine = np.where(lane < ROT, np.cos(angles), 1.0).astype(np.float32)
    sine = np.where(lane < ROT, np.sin(angles), 0.0).astype(np.float32)
    both = np.concatenate([cosine, sine], axis=1)
    high = both.astype(ml_dtypes.bfloat16)
    low = (both - high.astype(np.float32)).astype(ml_dtypes.bfloat16)
    swap = np.zeros((LANES, LANES), np.float32)
    for j in range(LANES):
        if lane[j] < half_rot:
            swap[j + half_rot, j] = -1.0
        elif lane[j] < ROT:
            swap[j - half_rot, j] = 1.0
    return np.concatenate([high, low], axis=1), swap.astype(ml_dtypes.bfloat16)


def swapped(value, swap):
    high = value.astype(jnp.bfloat16)
    low = (value - high.astype(jnp.float32)).astype(jnp.bfloat16)
    return mm(high, swap) + mm(low, swap)


def normalize(value):
    center = value - jnp.mean(value, axis=-1, keepdims=True)
    inv_sigma = lax.rsqrt(jnp.mean(center * center, axis=-1, keepdims=True) + eps_norm)
    return center * inv_sigma, inv_sigma


SENDS, ARRIVALS = 160, 160


def layer_kernel(nd, nf, scale, *refs):
    (tok, cot, seg, wq_far, wo_far, wu_far, wd_far, vecs, trig, swap) = refs[:10]
    (out, gtok, gq, go, gu, gd, gv) = refs[10:17]
    (xs, ys, sg, vd, vz, vp, upS, qS, g_up, g_q, g_down, g_out, w_up, w_q, w_o) = refs[17:32]
    (norm, h1, h2, act, du, outp, ep, proj, ctx, dctx, dp_low, table) = refs[32:44]
    m_up, m_q, m_down, m_out = refs[44:48]
    p_up, p_q, p_down, p_out = refs[48:52]
    r_up, r_q, r_down, r_out = refs[52:56]
    l_up, l_q, l_down, l_out = refs[56:60]
    a_up, a_q, a_down, a_out = refs[60:64]
    (b_up, b_q, f_up, f_q, o_send, e_send, o_recv, e_recv, tz, tp) = refs[64:74]
    (tables, turned, values, weights), refs = refs[74:78], refs[:74] + refs[78:]
    wq, wo, wu, wd, vtab = refs[74:79]
    sent, came, near = refs[79:]
    nz = nf // 2
    rows, width = tok.shape
    low = jnp.bfloat16
    wide = jnp.float32
    d, f = lax.axis_index("dp"), lax.axis_index("fsdp")
    z, c = lax.div(f, 2), lax.rem(f, 2)
    loads = [
        pltpu.make_async_copy(far, close, near.at[i])
        for i, (far, close) in enumerate(
            ((wd_far, wd), (wo_far, wo), (wu_far, wu), (wq_far, wq))
        )
    ]
    for load in loads:
        load.start()
    part = wq.shape[1] // nd
    third = part // 3
    hid = wu.shape[1] // nd
    block = wq.shape[0]

    state = {"sent": 0, "came": 0}
    pend = []

    def grab(count):
        at = state["came"]
        state["came"] += count
        assert state["came"] <= ARRIVALS
        return at

    def send(source, target, arrival, peer, cond=None):
        slot = state["sent"]
        state["sent"] += 1
        assert slot < SENDS

        copy = pltpu.make_async_remote_copy(
            src_ref=source(),
            dst_ref=target(),
            send_sem=sent.at[slot],
            recv_sem=came.at[arrival],
            device_id=peer,
            device_id_type=MESH,
        )
        pend.append((cond, copy))
        if cond is None:
            copy.start()
        else:
            pl.when(cond)(lambda: copy.start())

    def landed(ref, arrival):
        pltpu.make_async_copy(ref, ref, came.at[arrival]).wait()

    def mate(k):
        return (lax.rem(d + k, nd), f)

    def origin(k):
        return lax.rem(d + nd - k, nd)

    pair = (d, z * 2 + 1 - c)
    right, left = (d, (z + 1) * 2 + c), (d, (z - 1) * 2 + c)
    level = lambda k: (d, lax.rem(z + k, nz) * 2 + c)

    def span(index, size):
        return pl.ds(pl.multiple_of(index * size, size), size)

    barrier = pltpu.get_barrier_semaphore()
    peers = [mate(k) for k in range(1, nd)] + [level(k) for k in range(1, nz)] + [pair]
    for peer in peers:
        pl.semaphore_signal(barrier, inc=1, device_id=peer, device_id_type=MESH)
    count = vecs.shape[0]
    first_at = (d * nf + f) * count
    row = lax.div(first_at, width)
    shift = first_at - row * width
    row_of = lax.broadcasted_iota(jnp.int32, (16, width), 0)
    lane_of = lax.broadcasted_iota(jnp.int32, (16, width), 1)
    wraps = lane_of < shift
    own_row = row_of == row + jnp.where(wraps, 1, 0)
    inside = lane_of - shift + jnp.where(wraps, width, 0) < count
    line = jnp.concatenate([vecs[...].reshape(1, count), jnp.zeros((1, width - count), wide)], axis=1)
    line = pltpu.roll(jnp.broadcast_to(line, (16, width)), shift, 1)
    vtab[...] = jnp.where(jnp.logical_and(own_row, inside), line, 0.0).astype(low)
    vd[d] = vtab[...]
    sg[d] = jnp.broadcast_to(seg[...], (8, rows))
    for load in loads[:2]:
        load.wait()
    g_down[f] = wd[...].astype(low)
    g_out[f] = wo[...].astype(low)
    pl.semaphore_wait(barrier, len(peers))

    gathered = [g_down, g_out, g_up, g_q]
    wire = [grab(nz) for _ in gathered]
    cross = [grab(nz) for _ in gathered]

    def own(p):
        buf = gathered[p]
        here = lambda: buf.at[f]
        send(here, here, wire[p] + z, right, z < nz - 1)
        send(here, here, wire[p] + z, left, z > 0)
        send(here, here, cross[p] + z, pair)

    def relay(p, hop):
        buf = gathered[p]
        for origin_z, cond, onward, more in (
            (z - hop, z >= hop, right, z < nz - 1),
            (z + hop, z + hop < nz, left, z > 0),
        ):
            piece = functools.partial(lambda o: buf.at[o * 2 + c], origin_z)
            pl.when(cond)(functools.partial(lambda pc, o: landed(pc(), wire[p] + o), piece, origin_z))
            send(piece, piece, wire[p] + origin_z, onward, jnp.logical_and(cond, more))
            send(piece, piece, cross[p] + origin_z, pair, cond)

    own(0)
    own(1)
    for load in loads[2:]:
        load.wait()
    mates = range(1, nd)
    up_in, q_in = grab(nd), grab(nd)
    x_in, y_in, s_in, v_in = grab(nd), grab(nd), grab(nd), grab(nd)
    for j in range(nd):
        upS[j] = wu[:, j * hid : (j + 1) * hid].astype(low)
    for k in mates:
        to = lax.rem(d + k, nd)
        send(lambda: upS.at[to], lambda: g_up.at[f, d], up_in + k, mate(k))
        send(lambda: vtab, lambda: vd.at[d], v_in + k, mate(k))
        send(lambda: sg.at[d], lambda: sg.at[d], s_in + k, mate(k))
    for j in range(nd):
        qS[j] = jnp.concatenate(
            [
                wq[:, t * width + j * third : t * width + (j + 1) * third]
                for t in range(3)
            ],
            axis=1,
        ).astype(low)
    for k in mates:
        to = lax.rem(d + k, nd)
        send(lambda: qS.at[to], lambda: g_q.at[f, d], q_in + k, mate(k))
    keep = [
        pltpu.make_async_copy(tok, xs.at[span(d, rows)], near.at[4]),
        pltpu.make_async_copy(cot, ys.at[span(d, rows)], near.at[5]),
    ]
    for copy in keep:
        copy.start()
    g_up[f, d] = upS[d]
    g_q[f, d] = qS[d]
    vz_in, vp_in = grab(nz), grab(1)
    for k in mates:
        landed(g_up.at[f, origin(k)], up_in + k)
    own(2)
    for k in mates:
        landed(g_q.at[f, origin(k)], q_in + k)
    for k in mates:
        send(lambda: tok, lambda: xs.at[span(d, rows)], x_in + k, mate(k))
    for k in mates:
        send(lambda: cot, lambda: ys.at[span(d, rows)], y_in + k, mate(k))
    for k in mates:
        landed(vd.at[origin(k)], v_in + k)
    vz[z] = sum(vd[j].astype(wide) for j in range(nd)).astype(low)
    for k in range(1, nz):
        send(lambda: vz.at[z], lambda: vz.at[z], vz_in + k, level(k))
    relay(0, 1)
    relay(2, 1)
    own(3)
    for k in range(1, nz):
        landed(vz.at[lax.rem(z + nz - k, nz)], vz_in + k)
    vp[c] = sum(vz[j].astype(wide) for j in range(nz)).astype(low)
    send(lambda: vp.at[c], lambda: vp.at[c], vp_in, pair)
    for hop in range(2, nz - 1):
        relay(0, hop)
        relay(2, hop)
    landed(vp.at[1 - c], vp_in)
    vec = vp[0].astype(wide) + vp[1].astype(wide)

    for copy in keep:
        copy.wait()
    for k in mates:
        landed(xs.at[span(origin(k), rows)], x_in + k)
    for b in range(nd):
        at = slice(b * rows, (b + 1) * rows)
        value, _ = normalize(xs[at, :].astype(wide))
        norm[at, :] = value
        h1[at, :] = (value * vec[0:1] + vec[1:2]).astype(low)
        h2[at, :] = (value * vec[2:3] + vec[3:4]).astype(low)

    def mine_of(pieces):
        return sum(jnp.where(d == j, pieces[j], 0.0) for j in range(nd))

    relay(3, 1)
    relay(1, 1)
    for p in (0, 2):
        relay(p, nz - 1)
    for k in mates:
        landed(ys.at[span(origin(k), rows)], y_in + k)
        landed(sg.at[origin(k)], s_in + k)
    for p in (0, 2):
        for o in range(nz):
            landed(gathered[p].at[2 * o + 1 - c], cross[p] + o)
    def unblock(source, target):
        for j in range(nd):
            for o in range(nz):
                value = jnp.concatenate(
                    [source[2 * o, j].astype(wide), source[2 * o + 1, j].astype(wide)], axis=0
                )
                start = (j * nf + 2 * o) * block
                target[start : start + 2 * block, :] = value.astype(low)

    unblock(g_up, w_up)
    w_down = g_down[...].reshape(hid, width)
    cu = mine_of([vec[8 + j : 9 + j] for j in range(nd)])
    cut = 256
    du_sums = []
    for n in range(hid // cut):
        cols = slice(n * cut, (n + 1) * cut)
        u = mm(h2[...], w_up[:, cols]) + cu[:, cols]
        da = mm_nt(ys[...], w_down[cols, :])
        phi = 0.5 * (1.0 + lax.erf(u * (1.0 / math.sqrt(2.0))))
        act[:, cols] = (u * phi).astype(low)
        value = da * (phi + u * jnp.exp(-0.5 * u * u) * (1.0 / math.sqrt(2.0 * math.pi)))
        du_sums.append(jnp.sum(value, axis=0, keepdims=True))
        du[:, cols] = value.astype(low)
    du_sum = jnp.concatenate(du_sums, axis=1)
    sums = [m_down, m_up, m_q, m_out]
    paired = [p_down, p_up, p_q, p_out]
    rights = [r_down, r_up, r_q, r_out]
    lefts = [l_down, l_up, l_q, l_out]
    totals = [a_down, a_up, a_q, a_out]
    pair_in = [grab(1) for _ in sums]
    right_in = [grab(nz) for _ in sums]
    left_in = [grab(nz) for _ in sums]

    def share(p):
        send(lambda: sums[p].at[1 - c], lambda: paired[p].at[...], pair_in[p], pair)

    def first(p):
        landed(paired[p], pair_in[p])
        for k in range(nz - 1, 0, -1):
            for target, bound, inbox, sem, peer in (
                (z + k, z == 0, rights[p], right_in[p], right),
                (z - k, z == nz - 1, lefts[p], left_in[p], left),
            ):

                def add(target=target):
                    sums[p][c, target] = (
                        sums[p][c, target].astype(wide) + paired[p][target].astype(wide)
                    ).astype(low)

                pl.when(bound)(add)
                send(
                    functools.partial(lambda t: sums[p].at[c, t], target),
                    functools.partial(lambda box, t: box.at[t], inbox, target),
                    sem + target,
                    peer,
                    bound,
                )

    def middle(p, k):
        for target, bound, inbox, sem, peer in (
            (z + k, jnp.logical_and(z > 0, z + k < nz), rights[p], right_in[p], right),
            (z - k, jnp.logical_and(z < nz - 1, z >= k), lefts[p], left_in[p], left),
        ):

            def add(target=target, inbox=inbox, sem=sem):
                landed(inbox.at[target], sem + target)
                sums[p][c, target] = (
                    sums[p][c, target].astype(wide)
                    + paired[p][target].astype(wide)
                    + inbox[target].astype(wide)
                ).astype(low)

            pl.when(bound)(add)
            send(
                functools.partial(lambda t: sums[p].at[c, t], target),
                functools.partial(lambda box, t: box.at[t], inbox, target),
                sem + target,
                peer,
                bound,
            )

    def last(p):
        totals[p][...] = sums[p][c, z].astype(wide) + paired[p][z].astype(wide)
        for bound, inbox, sem in ((z > 0, rights[p], right_in[p]), (z < nz - 1, lefts[p], left_in[p])):

            def add(inbox=inbox, sem=sem):
                landed(inbox.at[z], sem + z)
                totals[p][...] = totals[p][...] + inbox[z].astype(wide)

            pl.when(bound)(add)

    value = mm_tn(h2[...], du[...])
    for j in range(nd):
        for i in range(nf):
            start = (j * nf + i) * block
            m_up[i % 2, i // 2, j] = value[start : start + block].astype(low)
    share(1)
    value = mm_tn(act[...], ys[...])
    size = wd.shape[0]
    for i in range(nf):
        m_down[i % 2, i // 2] = value[i * size : (i + 1) * size].astype(low)
    share(0)
    first(1)
    for hop in range(2, nz - 1):
        relay(3, hop)
        relay(1, hop)
    first(0)
    outp[...] = mm(act[...], w_down)
    dh = mm_nt(du[...], w_up[...])
    ep[...] = dh * vec[2:3]
    table[...] = jnp.zeros_like(table)
    table[2:3, :] = jnp.sum(dh * norm[...], axis=0, keepdims=True)
    table[3:4, :] = jnp.sum(dh, axis=0, keepdims=True)
    dy_sum = jnp.sum(ys[span(d, rows), :].astype(wide), axis=0, keepdims=True)
    table[7:8, :] = dy_sum
    table[12:13, :] = dy_sum
    for j in range(nd):
        table[8 + j : 9 + j, :] = jnp.where(d == j, du_sum, 0.0)
    relay(3, nz - 1)
    relay(1, nz - 1)
    middle(1, nz - 2)

    for p in (1, 3):
        for o in range(nz):
            landed(gathered[p].at[2 * o + 1 - c], cross[p] + o)
    unblock(g_q, w_q)
    for o in range(nz):
        value = jnp.concatenate([g_out[2 * o].astype(wide), g_out[2 * o + 1].astype(wide)], axis=0)
        w_o[2 * o * block : 2 * (o + 1) * block, :] = value.astype(low)
    cq = jnp.concatenate(
        [
            mine_of([vec[4 + t : 5 + t, j * third : (j + 1) * third] for j in range(nd)])
            for t in range(3)
        ],
        axis=1,
    )
    proj[...] = mm(h1[...], w_q[...]) + cq
    dctx[...] = mm_nt(ys[...], w_o[...]).astype(low)
    row_at = lax.broadcasted_iota(jnp.int32, (rows, rows), 0)
    col_at = lax.broadcasted_iota(jnp.int32, (rows, rows), 1)
    causal = col_at <= row_at
    sharp = 1.0 / math.sqrt(HEAD_DIM)

    heads = third // HEAD_DIM

    def forward(blocks):
        masks, pairs = {}, [(b, h) for b in blocks for h in range(heads)]
        for b in blocks:
            name = jnp.broadcast_to(sg[b][0:1, :].astype(wide), (rows, rows))
            masks[b] = jnp.logical_and(name == name.T, causal)
        for b in blocks:
            pos = jnp.sum(jnp.where(masks[b], 1.0, 0.0), axis=1, keepdims=True) - 1.0
            hot = jnp.where(col_at.astype(wide) == pos, 1.0, 0.0).astype(low)
            both = mm(hot, trig[...])
            tables[b] = both[:, : 2 * LANES] + both[:, 2 * LANES :]
        for b in blocks:
            at = slice(b * rows, (b + 1) * rows)
            for t in range(2 * third // LANES):
                x = proj[at, t * LANES : (t + 1) * LANES]
                other = swapped(x, swap[...])
                turned[at, t * LANES : (t + 1) * LANES] = (
                    x * tables[b][:, :LANES] + other * tables[b][:, LANES:]
                ).astype(low)
            values[at, :] = proj[at, 2 * third :].astype(low)
        scores = {}
        for b, h in pairs:
            at = slice(b * rows, (b + 1) * rows)
            q = turned[at, h * HEAD_DIM : (h + 1) * HEAD_DIM]
            k = turned[at, third + h * HEAD_DIM : third + (h + 1) * HEAD_DIM]
            scores[b, h] = jnp.where(masks[b], mm_nt(q, k) * sharp, mask_fill)
        for b, h in pairs:
            scores[b, h] = jnp.exp(scores[b, h] - jnp.max(scores[b, h], axis=-1, keepdims=True))
        for b, h in pairs:
            weights[b * heads + h] = scores[b, h] / jnp.sum(scores[b, h], axis=-1, keepdims=True)
        for b in blocks:
            at = slice(b * rows, (b + 1) * rows)
            ctx[at, :] = jnp.concatenate(
                [
                    mm(
                        weights[b * heads + h].astype(low),
                        values[at, h * HEAD_DIM : (h + 1) * HEAD_DIM],
                    )
                    for h in range(heads)
                ],
                axis=1,
            ).astype(low)

    def backward(blocks):
        pairs = [(b, h) for b in blocks for h in range(heads)]
        grads_of, scored = {}, {}

        def head(ref, b, h, at=0):
            return ref[b * rows : (b + 1) * rows, at + h * HEAD_DIM : at + (h + 1) * HEAD_DIM]

        for b, h in pairs:
            grads_of[b, h] = mm_nt(head(dctx, b, h), head(values, b, h))
        for b, h in pairs:
            a = weights[b * heads + h]
            inner = jnp.sum(a * grads_of[b, h], axis=-1, keepdims=True)
            scored[b, h] = (a * (grads_of[b, h] - inner) * sharp).astype(low)
        dqs, dks, dvs = {}, {}, {}
        for b, h in pairs:
            dqs[b, h] = mm(scored[b, h], head(turned, b, h, third))
        for b, h in pairs:
            dks[b, h] = mm_tn(scored[b, h], head(turned, b, h))
        for b, h in pairs:
            dvs[b, h] = mm_tn(weights[b * heads + h].astype(low), head(dctx, b, h))
        total = jnp.zeros((1, part), wide)
        for b in blocks:
            each = range(heads)
            mixed = jnp.concatenate([dqs[b, h] for h in each] + [dks[b, h] for h in each], axis=1)
            grads = []
            for t in range(2 * third // LANES):
                x = mixed[:, t * LANES : (t + 1) * LANES]
                grads.append(
                    x * tables[b][:, :LANES] - swapped(x, swap[...]) * tables[b][:, LANES:]
                )
            grads = jnp.concatenate(grads + [dvs[b, h] for h in each], axis=1)
            dp_low[b * rows : (b + 1) * rows, :] = grads.astype(low)
            total = total + jnp.sum(grads, axis=0, keepdims=True)
        return total

    halves = [range(0, nd // 2), range(nd // 2, nd)]
    o_in, e_in, t_in = grab(nd), grab(nd), grab(nd)
    for blocks in halves:
        forward(blocks)
    outp[...] += mm(ctx[...], w_o[...])
    o_send[...] = outp[...].astype(low)
    for k in mates:
        to = lax.rem(d + k, nd)
        send(lambda: o_send.at[span(to, rows)], lambda: o_recv.at[k], o_in + k, mate(k))
    for k in range(nz - 3, 0, -1):
        middle(1, k)
    dp_sum = backward(halves[0]) + backward(halves[1])
    middle(0, nz - 2)
    dh = mm_nt(dp_low[...], w_q[...])
    ep[...] += dh * vec[0:1]
    e_send[...] = ep[...].astype(low)
    table[0:1, :] = jnp.sum(dh * norm[...], axis=0, keepdims=True)
    table[1:2, :] = jnp.sum(dh, axis=0, keepdims=True)
    for t in range(3):
        piece = dp_sum[:, t * third : (t + 1) * third]
        table[4 + t : 5 + t, :] = jnp.concatenate(
            [jnp.where(d == j, piece, 0.0) for j in range(nd)], axis=1
        )
    tz_in, tp_in = grab(nz), grab(1)
    tz[0] = table[...].astype(low)
    for k in mates:
        send(lambda: tz.at[0], lambda: tz.at[k], t_in + k, mate(k))
    for k in mates:
        to = lax.rem(d + k, nd)
        send(lambda: e_send.at[span(to, rows)], lambda: e_recv.at[k], e_in + k, mate(k))
    value = mm_tn(h1[...], dp_low[...])
    for j in range(nd):
        for i in range(nf):
            start = (j * nf + i) * block
            m_q[i % 2, i // 2, j] = value[start : start + block].astype(low)
    share(2)
    value = mm_tn(ctx[...], ys[...])
    for i in range(nf):
        m_out[i % 2, i // 2] = value[i * block : (i + 1) * block].astype(low)
    share(3)
    first(2)
    first(3)
    for k in range(nz - 3, 0, -1):
        middle(0, k)
    fu_in, fq_in = grab(nd), grab(nd)

    def give_back(p, whole, box, arrivals):
        last(p)
        whole[...] = totals[p][...].astype(low)
        for k in mates:
            to = lax.rem(d + k, nd)
            send(lambda: whole.at[to], lambda: box.at[d], arrivals + k, mate(k))
        box[d] = whole[d]

    give_back(1, b_up, f_up, fu_in)
    for k in mates:
        landed(tz.at[k], t_in + k)
    tz[nd] = (table[...] + sum(tz[k].astype(wide) for k in mates)).astype(low)
    for k in range(1, nz):
        send(lambda: tz.at[nd], lambda: tz.at[nd + k], tz_in + k, level(k))
    last(0)
    gd[...] = a_down[...] * scale
    for k in range(nz - 2, 0, -1):
        middle(2, k)
    give_back(2, b_q, f_q, fq_in)
    for k in range(nz - 2, 0, -1):
        middle(3, k)
    for k in range(1, nz):
        landed(tz.at[nd + k], tz_in + k)
    tp[0] = sum(tz[nd + k].astype(wide) for k in range(nz)).astype(low)
    send(lambda: tp.at[0], lambda: tp.at[1], tp_in, pair)
    for k in mates:
        landed(o_recv.at[k], o_in + k)
        landed(e_recv.at[k], e_in + k)
    total = xs[span(d, rows), :].astype(wide) + vec[7:8] + vec[12:13] + outp[span(d, rows), :]
    out[...] = (total + sum(o_recv[k].astype(wide) for k in mates)).astype(low)
    value, inv_sigma = normalize(xs[span(d, rows), :].astype(wide))
    e = ep[span(d, rows), :] + sum(e_recv[k].astype(wide) for k in mates)
    gtok[...] = (
        ys[span(d, rows), :].astype(wide)
        + inv_sigma
        * (
            e
            - jnp.mean(e, axis=-1, keepdims=True)
            - value * jnp.mean(e * value, axis=-1, keepdims=True)
        )
    ).astype(low)
    landed(tp.at[1], tp_in)
    whole = (tp[0].astype(wide) + tp[1].astype(wide)) * scale
    line = jnp.sum(jnp.where(own_row, whole, 0.0), axis=0, keepdims=True)
    line = pltpu.roll(jnp.broadcast_to(line, (8, width)), lax.rem(width - shift, width), 1)
    gv[...] = line[0:1, :count].reshape(count)
    for k in mates:
        landed(f_up.at[origin(k)], fu_in + k)
    for j in range(nd):
        gu[:, j * hid : (j + 1) * hid] = f_up[j].astype(wide) * scale
    last(3)
    go[...] = a_out[...] * scale
    for k in mates:
        landed(f_q.at[origin(k)], fq_in + k)
    gq[...] = scale * jnp.concatenate(
        [f_q[j].astype(wide)[:, t * third : (t + 1) * third] for t in range(3) for j in range(nd)],
        axis=1,
    )
    for cond, copy in pend:
        if cond is None:
            copy.wait_send()
        else:
            pl.when(cond)(functools.partial(lambda x: x.wait_send(), copy))


def layer_step(tokens, cotangent, segments, w_qkv, w_out, w_up, w_down, vectors, nd, nf):
    rows, width = tokens.shape
    low, wide = jnp.bfloat16, jnp.float32
    nz, block, size = nf // 2, w_qkv.shape[0], w_down.shape[0]
    part, hid = w_qkv.shape[1] // nd, w_up.shape[1] // nd
    third = part // 3
    group = nd * rows
    count = vectors.shape[0]
    trig, swap = rotary_constants(rows)
    inputs = (
        tokens,
        cotangent,
        segments,
        w_qkv,
        w_out,
        w_up,
        w_down,
        vectors,
        jnp.asarray(trig),
        jnp.asarray(swap),
    )
    outs = [
        jax.ShapeDtypeStruct((rows, width), low),
        jax.ShapeDtypeStruct((rows, width), low),
        *[jax.ShapeDtypeStruct(x.shape, wide) for x in (w_qkv, w_out, w_up, w_down)],
        jax.ShapeDtypeStruct((count,), wide),
    ]
    vm = pltpu.VMEM
    four = [(nd, block, hid), (nd, block, part), (size, width), (block, width)]
    scratch = [
        vm((group, width), low),
        vm((group, width), low),
        vm((nd, 8, rows), jnp.int32),
        vm((nd, 16, width), low),
        vm((nz, 16, width), low),
        vm((2, 16, width), low),
        vm((nd, block, hid), low),
        vm((nd, block, part), low),
        *[vm((nf, *x), low) for x in four],
        vm((width, hid), low),
        vm((width, part), low),
        vm((third, width), low),
        vm((group, width), wide),
        vm((group, width), low),
        vm((group, width), low),
        vm((group, hid), low),
        vm((group, hid), low),
        vm((group, width), wide),
        vm((group, width), wide),
        vm((group, part), wide),
        vm((group, third), low),
        vm((group, third), low),
        vm((group, part), low),
        vm((16, width), wide),
        *[vm((2, nz, *x), low) for x in four],
        *[vm((nz, *x), low) for x in four],
        *[vm((nz, *x), low) for x in four],
        *[vm((nz, *x), low) for x in four],
        *[vm(x, wide) for x in four],
        vm((nd, block, hid), low),
        vm((nd, block, part), low),
        vm((nd, block, hid), low),
        vm((nd, block, part), low),
        vm((group, width), low),
        vm((group, width), low),
        vm((nd, rows, width), low),
        vm((nd, rows, width), low),
        vm((nd + nz, 16, width), low),
        vm((2, 16, width), low),
        vm((nd, rows, 2 * LANES), wide),
        vm((group, 2 * third), low),
        vm((group, third), low),
        vm((nd * third // HEAD_DIM, rows, rows), wide),
        *[vm(x.shape, wide) for x in (w_qkv, w_out, w_up, w_down)],
        vm((16, width), low),
        pltpu.SemaphoreType.DMA((SENDS,)),
        pltpu.SemaphoreType.DMA((ARRIVALS,)),
        pltpu.SemaphoreType.DMA((6,)),
    ]
    scale = 1.0 / math.sqrt(rows * nd * nf)
    spec = pl.BlockSpec(memory_space=pltpu.VMEM)
    far = pl.BlockSpec(memory_space=pl.ANY)
    return pl.pallas_call(
        functools.partial(layer_kernel, nd, nf, scale),
        out_shape=outs,
        in_specs=[far, far, spec, far, far, far, far, spec, spec, spec],
        out_specs=[spec] * len(outs),
        scratch_shapes=scratch,
        compiler_params=pltpu.CompilerParams(
            collective_id=0, has_side_effects=True, vmem_limit_bytes=60 << 20
        ),
    )(*inputs)


def adam_kernel(count, *refs):
    far = [refs[i * count : (i + 1) * count] for i in range(4)]
    passed, refs = refs[4 * count : 4 * count + 2], refs[4 * count + 2 :]
    pass_outs, refs = refs[:2], refs[2:]
    outs = [refs[i * count : (i + 1) * count] for i in range(4)]
    refs = refs[4 * count :]
    near = [refs[i * count : (i + 1) * count] for i in range(4)]
    held = [refs[(4 + i) * count : (5 + i) * count] for i in range(3)]
    passing = refs[7 * count : 7 * count + 2]
    load_sems, sems = refs[7 * count + 2 :]
    loads = [
        [
            pltpu.make_async_copy(far[j][i], near[j][i], load_sems.at[i * 4 + j])
            for j in range(4)
        ]
        for i in range(count)
    ]
    carried = [
        pltpu.make_async_copy(source, close, load_sems.at[4 * count + i])
        for i, (source, close) in enumerate(zip(passed, passing))
    ]
    for group in [carried] + loads:
        for copy in group:
            copy.start()
    copies = []

    def write(source, target):
        copies.append(pltpu.make_async_copy(source, target, sems.at[len(copies)]))
        copies[-1].start()

    for copy, close, target in zip(carried, passing, pass_outs):
        copy.wait()
        write(close, target)
    for i in range(count):
        for copy in loads[i]:
            copy.wait()
        write(near[0][i], outs[0][i])
        vector = i == count - 1
        results = adam_update(
            near[1][i][...],
            near[0][i][...],
            near[2][i][...],
            near[3][i][...],
            rate_vector if vector else rate_matrix,
            0.0 if vector else decay_matrix,
        )
        for j in range(3):
            held[j][i][...] = results[j]
            write(held[j][i], outs[j + 1][i])
    for copy in copies:
        copy.wait()


def adam_all(grads, weights, firsts, seconds, passed):
    count = len(grads)
    shapes = [jax.ShapeDtypeStruct(x.shape, x.dtype) for x in weights]
    given = [jax.ShapeDtypeStruct(x.shape, x.dtype) for x in passed]
    total = 4 * count + len(passed)
    return pl.pallas_call(
        functools.partial(adam_kernel, count),
        out_shape=given + shapes * 4,
        in_specs=[pl.BlockSpec(memory_space=pl.ANY)] * total,
        out_specs=[pl.BlockSpec(memory_space=pl.ANY)] * total,
        scratch_shapes=[pltpu.VMEM(x.shape, x.dtype) for x in shapes * 7 + given]
        + [pltpu.SemaphoreType.DMA((total,)), pltpu.SemaphoreType.DMA((total,))],
        compiler_params=pltpu.CompilerParams(vmem_limit_bytes=60 << 20),
    )(*grads, *weights, *firsts, *seconds, *passed)


def per_device(
    tokens,
    cotangent,
    segments,
    w_qkv,
    w_out,
    w_up,
    w_down,
    vectors,
    first_qkv,
    first_out,
    first_up,
    first_down,
    first_vec,
    second_qkv,
    second_out,
    second_up,
    second_down,
    second_vec,
):
    device_count = lax.axis_size(("dp", "fsdp"))
    axes = ("dp", "fsdp")
    nd, nf = lax.axis_size("dp"), lax.axis_size("fsdp")
    direct = (
        nd > 1
        and nf % 2 == 0
        and nf > 2
        and HEADS % nd == 0
        and tokens.shape[0] == LANES
        and w_up.shape[1] == nd * D
        and (2 * D // nd) % LANES == 0
        and w_qkv.shape[0] % 8 == 0
        and w_down.shape[0] % 16 == 0
    )
    if direct:
        output, grad_tokens, grad_w_qkv, grad_w_out, grad_w_up, grad_w_down, whole = layer_step(
            tokens, cotangent, segments, w_qkv, w_out, w_up, w_down, vectors, nd, nf
        )
        results = adam_all(
            (grad_w_qkv, grad_w_out, grad_w_up, grad_w_down, whole),
            (w_qkv, w_out, w_up, w_down, vectors),
            (first_qkv, first_out, first_up, first_down, first_vec),
            (second_qkv, second_out, second_up, second_down, second_vec),
            (output, grad_tokens),
        )
        return tuple(results)
    else:
        segment = segments[0]
        allowed = doc_mask(segment)
        cosine_part, sine_part = rotary_tables(segment)
        whole = [
            lax.all_gather(x.astype(jnp.bfloat16), axes, axis=0, tiled=True)
            for x in (w_qkv, w_out, w_up, w_down, vectors)
        ]
        output, saved = forward_pass(tokens, allowed, cosine_part, sine_part, *whole)
        grad_tokens, *local = backward_pass(
            saved, cotangent, allowed, cosine_part, sine_part, *whole
        )
        factor = 1.0 / math.sqrt(device_count * tokens.shape[0])
        grad_w_qkv, grad_w_out, grad_w_up, grad_w_down, grad_vectors = (
            factor * lax.psum_scatter(x, axes, scatter_dimension=0, tiled=True) for x in local
        )
    new_w_qkv, new_first_qkv, new_second_qkv = adam_update(
        w_qkv, grad_w_qkv, first_qkv, second_qkv, rate_matrix, decay_matrix
    )
    new_w_out, new_first_out, new_second_out = adam_update(
        w_out, grad_w_out, first_out, second_out, rate_matrix, decay_matrix
    )
    new_w_up, new_first_up, new_second_up = adam_update(
        w_up, grad_w_up, first_up, second_up, rate_matrix, decay_matrix
    )
    new_w_down, new_first_down, new_second_down = adam_update(
        w_down, grad_w_down, first_down, second_down, rate_matrix, decay_matrix
    )
    new_vectors, new_first_vec, new_second_vec = adam_update(
        vectors, grad_vectors, first_vec, second_vec, rate_vector, 0.0
    )
    return (
        output,
        grad_tokens,
        grad_w_qkv,
        grad_w_out,
        grad_w_up,
        grad_w_down,
        grad_vectors,
        new_w_qkv,
        new_w_out,
        new_w_up,
        new_w_down,
        new_vectors,
        new_first_qkv,
        new_first_out,
        new_first_up,
        new_first_down,
        new_first_vec,
        new_second_qkv,
        new_second_out,
        new_second_up,
        new_second_down,
        new_second_vec,
    )


def solution(mesh):
    placed = (
        P(("dp", "fsdp"), None),
        P(("dp", "fsdp"), None),
        P(("dp", "fsdp"), None),
        P(("dp", "fsdp"), None),
        P(("dp", "fsdp"), None),
        P(("dp", "fsdp"), None),
        P(("dp", "fsdp"), None),
        P(("dp", "fsdp")),
        P(("dp", "fsdp"), None),
        P(("dp", "fsdp"), None),
        P(("dp", "fsdp"), None),
        P(("dp", "fsdp"), None),
        P(("dp", "fsdp")),
        P(("dp", "fsdp"), None),
        P(("dp", "fsdp"), None),
        P(("dp", "fsdp"), None),
        P(("dp", "fsdp"), None),
        P(("dp", "fsdp")),
    )
    return jax.shard_map(
        per_device,
        mesh=mesh,
        in_specs=placed,
        out_specs=(
            P(("dp", "fsdp"), None),
            P(("dp", "fsdp"), None),
            P(("dp", "fsdp"), None),
            P(("dp", "fsdp"), None),
            P(("dp", "fsdp"), None),
            P(("dp", "fsdp"), None),
            P(("dp", "fsdp")),
            P(("dp", "fsdp"), None),
            P(("dp", "fsdp"), None),
            P(("dp", "fsdp"), None),
            P(("dp", "fsdp"), None),
            P(("dp", "fsdp")),
            P(("dp", "fsdp"), None),
            P(("dp", "fsdp"), None),
            P(("dp", "fsdp"), None),
            P(("dp", "fsdp"), None),
            P(("dp", "fsdp")),
            P(("dp", "fsdp"), None),
            P(("dp", "fsdp"), None),
            P(("dp", "fsdp"), None),
            P(("dp", "fsdp"), None),
            P(("dp", "fsdp")),
        ),
        check_vma=False,
    )
```
